32 devices in a mesh: groups: 2 (over y), row: 8 (over z, x), col: 2 (over core).
Axes of the slice: x: 2, y: 2, z: 4, core: 2. Of those that a mesh axis runs over, the one named last changes fastest.
Arguments:
- object_slices: float32 [4, 2, 2048, 512], P(None, None, ('groups', 'row'), 'col'), parts along dimension 2, may hold values from -4 to 4
- probe: float32 [16, 2, 128, 128], P('groups'), parts along dimension 0, may hold values from -3 to 3
- taps: float32 [2, 63], replicated, may hold values from -0.5 to 0.5
- measured: float32 [64, 128, 128], P(('groups', 'row', 'col')), parts along dimension 0, may hold values from 0.5 to 16
- positions: int32 [64, 2], P(('groups', 'row', 'col')), parts along dimension 0, may hold values from -64 to 959, as said below
Outputs:
- object_grad: float32 [4, 2, 2048, 512], P(None, None, ('groups', 'row'), 'col'), parts along dimension 2
- new_probe: float32 [16, 2, 16384], P('groups', None, ('row', 'col')), parts along dimension 0
The draws below stay inside these ranges and needn't reach their ends.
There are 2 independent parts, one for each index of `groups`. The reference program is written for one: setup_inputs(seed, part) draws one part's arguments, and reference() takes and returns one part's arrays. A program takes and returns all parts, laid end to end along the dimension named above; an argument that names none is the same for every part. Nothing has to cross between parts.
Inputs may be any that keep to these rules, and one draw needn't show every extreme that they name: `positions`: record r belongs to device d = r // 2 in row-major order over the (row, col) device grid, with tile indices (i, q); its row lies in [i * 128 - 128/2, (i + 1) * 128 - 128/2) and its column in [q * 256 - 128/2, (q + 1) * 256 - 128/2).
All inputs are finite; a program needn't handle non-finite values.
Results may differ from the reference program's by a relative error of at most 0.0003.
Values sent between devices are 32-bit elements; how exact they have to be, the bound alone decides.
No kernel may reach another device: no remote copies, remote signals or barrier semaphores. Data moves between devices by JAX's collectives and lax.ppermute only.
A program may use at most 64 MiB of HBM per device.

```python
import math
import jax
import jax.numpy as jnp
from jax import lax

SLICES = 4
MODES = 8
WINDOW = 128
TAPS = 63
TILE_R = 128
TILE_C = 256
REC_DEV = 2
OBJ_R = 1024
OBJ_C = 512
RECORDS = 32


def draw_positions(key, part):
    tiles_across = OBJ_C // TILE_C
    record_idx = jnp.arange(RECORDS, dtype=jnp.int32)
    device_idx = record_idx // REC_DEV
    tile_row = device_idx // tiles_across
    tile_col = device_idx % tiles_across
    key_rows, key_cols = jax.random.split(jax.random.fold_in(key, 11))
    row_off = jax.random.randint(key_rows, (RECORDS,), 0, TILE_R, dtype=jnp.int32)
    col_off = jax.random.randint(key_cols, (RECORDS,), 0, TILE_C, dtype=jnp.int32)
    row_off = row_off.at[0].set(0)
    row_off = row_off.at[RECORDS - 1].set(TILE_R - 1)
    col_off = col_off.at[RECORDS - 1].set(TILE_C - 1)
    rows = row_off + tile_row * TILE_R - WINDOW // 2
    cols = col_off + tile_col * TILE_C - WINDOW // 2
    return jnp.stack([rows, cols], axis=1)


def shard_levels(key, dims, shards, smallest, high):
    level, own = 1.0, jax.random.fold_in(key, 6)
    for dim, parts in shards:
        draws = jnp.exp(jax.random.uniform(jax.random.fold_in(own, dim), (parts,), jnp.float32, smallest / len(shards), high / len(shards)))
        level = level * jnp.repeat(draws, dims[dim] // parts).reshape([-1 if axis == dim else 1 for axis in range(len(dims))])
    return level


def bell_draw(stream_key, shape, scale, bound, cuts=(), held_as=jnp.bfloat16):
    level = shard_levels(stream_key, shape, cuts, -0.22, 0.18) if cuts else 1.0
    array = jax.random.normal(stream_key, shape, jnp.float32) * scale * level
    return jnp.minimum(jnp.maximum(array, -bound), bound).astype(held_as)


def setup_inputs(seed: int = 0, part: int = 0) -> dict:
    seeds = jax.random.split(jax.random.key(seed), 6)
    part_splits = jax.random.split(jax.random.fold_in(seeds[5], part), 6)
    return {
        "object_slices": bell_draw(part_splits[0], (SLICES, 2, OBJ_R, OBJ_C), 0.7071, 4.0, ((2, 8), (3, 2)), jnp.float32),
        "probe": bell_draw(part_splits[1], (MODES, 2, WINDOW, WINDOW), 0.5, 3.0, (), jnp.float32),
        "taps": bell_draw(seeds[2], (2, TAPS), 0.09, 0.5, (), jnp.float32),
        "measured": jnp.clip(jnp.exp(math.log(16.0) - 3.465736 * jax.random.uniform(part_splits[3], (RECORDS, WINDOW, WINDOW), jnp.float32) ** shard_levels(part_splits[3], (RECORDS, WINDOW, WINDOW), ((0, 16),), -0.2, 0.2)), 0.5, 16.0),
        "positions": draw_positions(jax.random.fold_in(jax.random.fold_in(seeds[5], part), 71), part),
    }


highest_mode = lax.Precision.HIGHEST

def einsum_exact(form, first, second):
    return jnp.einsum(form, first, second, precision=highest_mode)

def make_tables(taps, width):
    reach = taps.shape[1] // 2
    pixel_idx = lax.iota(jnp.int32, width)
    offset = pixel_idx[None, :] - pixel_idx[:, None] + reach
    tap_idx = lax.iota(jnp.int32, taps.shape[1])
    one_hot = (offset[:, :, None] == tap_idx[None, None, :]).astype(jnp.float32)
    band_re = einsum_exact('abt,t->ab', one_hot, taps[0])
    band_im = einsum_exact('abt,t->ab', one_hot, taps[1])
    phase_idx = pixel_idx[:, None] * pixel_idx[None, :] % width
    angle = 2.0 * math.pi / width * phase_idx.astype(jnp.float32)
    norm_factor = 1.0 / math.sqrt(width)
    return (band_re, band_im, jnp.cos(angle) * norm_factor, -jnp.sin(angle) * norm_factor)

def both_sides(mat_re, mat_im, wave_re, wave_im):
    left_re = einsum_exact('ab,kbc->kac', mat_re, wave_re) - einsum_exact('ab,kbc->kac', mat_im, wave_im)
    left_im = einsum_exact('ab,kbc->kac', mat_re, wave_im) + einsum_exact('ab,kbc->kac', mat_im, wave_re)
    out_re = einsum_exact('kac,dc->kad', left_re, mat_re) - einsum_exact('kac,dc->kad', left_im, mat_im)
    out_im = einsum_exact('kac,dc->kad', left_re, mat_im) + einsum_exact('kac,dc->kad', left_im, mat_re)
    return (out_re, out_im)

def record_loss(probe, patch, measured_one, tables):
    band_re, band_im, dft_re, dft_im = tables
    wave_re = probe[:, 0]
    wave_im = probe[:, 1]
    layers = patch.shape[0]
    for layer_idx in range(layers):
        obj_re = patch[layer_idx, 0]
        obj_im = patch[layer_idx, 1]
        wave_re, wave_im = (wave_re * obj_re - wave_im * obj_im, wave_re * obj_im + wave_im * obj_re)
        if layer_idx + 1 < layers:
            wave_re, wave_im = both_sides(band_re, band_im, wave_re, wave_im)
    far_re, far_im = both_sides(dft_re, dft_im, wave_re, wave_im)
    intensity = lax.optimization_barrier(jnp.sum(far_re * far_re + far_im * far_im, axis=0))
    weight = 1.0 / (8.0 * probe.shape[0])
    return 0.5 * weight * jnp.sum((intensity - measured_one) ** 2)

def accumulate(grid, probe, measured, places, tables, patch_width):
    sizes = (grid.shape[0], 2, patch_width, patch_width)

    def one_record(carry, item):
        grad_grid, grad_probe = carry
        place, measured_one = item
        zero_idx = jnp.zeros((), jnp.int32)
        starts = (zero_idx, zero_idx, place[0].astype(jnp.int32), place[1].astype(jnp.int32))
        patch = lax.dynamic_slice(grid, starts, sizes)
        grad_wave, grad_patch = jax.grad(record_loss, argnums=(0, 1))(probe, patch, measured_one, tables)
        current = lax.dynamic_slice(grad_grid, starts, sizes)
        grad_grid = lax.dynamic_update_slice(grad_grid, current + grad_patch, starts)
        return ((grad_grid, grad_probe + grad_wave), None)
    init = (jnp.zeros(grid.shape, jnp.float32), jnp.zeros(probe.shape, jnp.float32))
    (grad_grid, grad_probe), unused = lax.scan(one_record, init, (places, measured))
    return (grad_grid, grad_probe)

def gram_of(first, second):
    stacked = jnp.concatenate([first, second], axis=0)
    col_re = stacked[:, 0]
    col_im = stacked[:, 1]
    gram_re = einsum_exact('ax,bx->ab', col_re, col_re) + einsum_exact('ax,bx->ab', col_im, col_im)
    gram_im = einsum_exact('ax,bx->ab', col_re, col_im) - einsum_exact('ax,bx->ab', col_im, col_re)
    return (gram_re, gram_im)

def complex_cholesky(herm_re, herm_im):
    count = herm_re.shape[0]
    order_idx = lax.iota(jnp.int32, count)
    cols_re = []
    cols_im = []
    for col_idx in range(count):
        numer_re = herm_re[:, col_idx]
        numer_im = herm_im[:, col_idx]
        for prev_idx in range(col_idx):
            vec_re = cols_re[prev_idx]
            vec_im = cols_im[prev_idx]
            pivot_re = vec_re[col_idx]
            pivot_im = vec_im[col_idx]
            numer_re = numer_re - (vec_re * pivot_re + vec_im * pivot_im)
            numer_im = numer_im - (vec_im * pivot_re - vec_re * pivot_im)
        diag_val = jnp.sqrt(numer_re[col_idx])
        below = order_idx > col_idx
        at_diag = order_idx == col_idx
        cols_re.append(jnp.where(below, numer_re / diag_val, 0.0) + jnp.where(at_diag, diag_val, 0.0))
        cols_im.append(jnp.where(below, numer_im / diag_val, 0.0))
    return (jnp.stack(cols_re, axis=1), jnp.stack(cols_im, axis=1))

def lower_inverse(low_re, low_im):
    count = low_re.shape[0]
    unit = jnp.eye(count, dtype=low_re.dtype)
    rows_re = []
    rows_im = []
    for row_idx in range(count):
        acc_re = unit[row_idx]
        acc_im = jnp.zeros_like(unit[row_idx])
        for prev_idx in range(row_idx):
            coef_re = low_re[row_idx, prev_idx]
            coef_im = low_im[row_idx, prev_idx]
            acc_re = acc_re - (coef_re * rows_re[prev_idx] - coef_im * rows_im[prev_idx])
            acc_im = acc_im - (coef_re * rows_im[prev_idx] + coef_im * rows_re[prev_idx])
        rows_re.append(acc_re / low_re[row_idx, row_idx])
        rows_im.append(acc_im / low_re[row_idx, row_idx])
    return (jnp.stack(rows_re, axis=0), jnp.stack(rows_im, axis=0))

def orthonormalize(probe_cols, grad_cols, gram_re, gram_im, scale_out):
    modes = probe_cols.shape[0]
    trace_pp = jnp.trace(gram_re[:modes, :modes])
    trace_gg = jnp.trace(gram_re[modes:, modes:])
    factor = 0.5 * jnp.sqrt(trace_pp / (trace_gg + 1e-06))
    new_re = gram_re[:modes, :modes] - factor * (gram_re[:modes, modes:] + gram_re[modes:, :modes]) + factor * factor * gram_re[modes:, modes:]
    new_im = gram_im[:modes, :modes] - factor * (gram_im[:modes, modes:] + gram_im[modes:, :modes]) + factor * factor * gram_im[modes:, modes:]
    low_re, low_im = complex_cholesky(new_re, new_im)
    inv_re, inv_im = lower_inverse(low_re, low_im)
    right_re = inv_re.T
    right_im = -inv_im.T
    moved = probe_cols - factor * grad_cols
    moved_re = moved[:, 0]
    moved_im = moved[:, 1]
    out_re = einsum_exact('kx,kj->jx', moved_re, right_re) - einsum_exact('kx,kj->jx', moved_im, right_im)
    out_im = einsum_exact('kx,kj->jx', moved_re, right_im) + einsum_exact('kx,kj->jx', moved_im, right_re)
    return jnp.stack([out_re, out_im], axis=1) * scale_out

def reference(object_slices, probe, taps, measured, positions):
    width = probe.shape[-1]
    half = width // 2
    tables = make_tables(taps, width)
    grid = jnp.pad(object_slices, ((0, 0), (0, 0), (half, half), (half, half)))
    places = positions + half
    grad_grid, grad_probe = accumulate(grid, probe, measured, places, tables, width)
    object_grad = grad_grid[:, :, half:-half, half:-half]
    modes = probe.shape[0]
    probe_cols = probe.reshape(modes, 2, width * width)
    grad_cols = grad_probe.reshape(modes, 2, width * width)
    gram_re, gram_im = gram_of(probe_cols, grad_cols)
    new_probe = orthonormalize(probe_cols, grad_cols, gram_re, gram_im, float(width))
    return (object_grad, new_probe)
```

```python
import math

import jax
import jax.numpy as jnp
import numpy as np
from jax import lax
from jax.experimental import pallas as pl
from jax.experimental.pallas import tpu as pltpu
from jax.sharding import PartitionSpec as P

F32 = jnp.float32
BF16 = jnp.bfloat16
LANES = 128
SUBLANES = 8


def shifted(value, axis, step):
    count = lax.axis_size(axis)
    pairs = [(i, i + step) for i in range(count) if 0 <= i + step < count]
    return lax.ppermute(value, axis, pairs)


def swapped(value, axis, bit):
    count = lax.axis_size(axis)
    return lax.ppermute(value, axis, [(i, i ^ bit) for i in range(count)])


def hi_lo(value):
    high = lax.reduce_precision(value, 8, 7)
    return high.astype(BF16), (value - high).astype(BF16)


def block_tables(taps, width):
    reach = taps.shape[1] // 2
    padded = jnp.pad(taps, ((0, 0), (width, width)))
    idx = lax.iota(jnp.int32, width)
    offset = idx[None, :] - idx[:, None] + reach
    tap_idx = lax.iota(jnp.int32, taps.shape[1])
    hot = (offset[None, :, :] == tap_idx[:, None, None]).astype(F32)
    band_re = jnp.sum(hot * taps[0][:, None, None], axis=0)
    band_im = jnp.sum(hot * taps[1][:, None, None], axis=0)
    phase = np.arange(width)[:, None] * np.arange(width)[None, :] % width
    angle = 2.0 * math.pi / width * phase
    norm = 1.0 / math.sqrt(width)
    dft_re = jnp.asarray(np.cos(angle) * norm, F32)
    dft_im = jnp.asarray(-np.sin(angle) * norm, F32)

    def block(re, im):
        return jnp.concatenate(
            [jnp.concatenate([re, -im], axis=1), jnp.concatenate([im, re], axis=1)], axis=0
        )

    band, dft = block(band_re, band_im), block(dft_re, dft_im)
    parts = []
    for matrix in (band, band.T, dft, dft.T):
        parts.extend(hi_lo(matrix))
    return jnp.stack(parts)


def split(value):
    high = value.astype(BF16)
    return high, (value - high.astype(F32)).astype(BF16)


def mxu(a, b):
    return lax.dot_general(a, b, (((1,), (0,)), ((), ())), preferred_element_type=F32)


def left_product(tab, which, x):
    high, low = split(x)
    w_high, w_low = tab[2 * which], tab[2 * which + 1]
    return mxu(w_high, high) + (mxu(w_high, low) + mxu(w_low, high))


def right_product(tab, which, x):
    high, low = split(x)
    w_high, w_low = tab[2 * which], tab[2 * which + 1]
    return mxu(high, w_high) + (mxu(low, w_high) + mxu(high, w_low))


def to_rows(y):
    n = LANES
    return jnp.concatenate(
        [
            jnp.concatenate([y[:n, :n], y[n:, :n]], axis=1),
            jnp.concatenate([y[:n, n:], y[n:, n:]], axis=1),
        ],
        axis=0,
    )


def two_sided(tab, forward, x):
    base, adjoint = forward
    return right_product(tab, adjoint, to_rows(left_product(tab, base, x)))


BAND, BAND_ADJ, DFT, DFT_ADJ = range(4)


def field_kernel(
    places, side, own, above, below, beside, probe, tab, measured,
    gown, gside, gprobe, ext, gext, patch, waves, far, intensity, gpatch,
):
    rec = pl.program_id(0)
    slices = own.shape[0]
    modes = probe.shape[0]
    n = LANES
    tile_cols = own.shape[3]
    half = above.shape[2]
    tile_rows = own.shape[2]
    weight = 1.0 / (8.0 * modes)

    @pl.when(rec == 0)
    def _():
        gext[...] = jnp.zeros(gext.shape, F32)
        gprobe[...] = jnp.zeros(gprobe.shape, F32)
        ext[:, :, :half, n : n + tile_cols] = above[...]
        ext[:, :, half : half + tile_rows, n : n + tile_cols] = own[...]
        ext[:, :, half + tile_rows :, n : n + tile_cols] = below[...]
        nothing = jnp.zeros(beside.shape, F32)

        @pl.when(side[0] == 0)
        def _():
            ext[:, :, :, :n] = nothing
            ext[:, :, :, n + tile_cols :] = beside[...]

        @pl.when(side[0] != 0)
        def _():
            ext[:, :, :, :n] = beside[...]
            ext[:, :, :, n + tile_cols :] = nothing

    row = places[rec, 0]
    col = places[rec, 1]
    lane_tile = pl.multiple_of(col // n * n, n)
    shift = col % n
    row_tile = pl.multiple_of(row // SUBLANES * SUBLANES, SUBLANES)
    drop = row % SUBLANES
    for s in range(slices):
        for c in range(2):
            window = ext[s, c, pl.ds(row_tile, n + SUBLANES), pl.ds(lane_tile, 2 * n)]
            window = pltpu.roll(window, (2 * n - shift) % (2 * n), 1)[:, :n]
            patch[s, c] = pltpu.roll(window, (n + SUBLANES - drop) % (n + SUBLANES), 0)[:n]

    def wave_in(s, mode):
        if s == 0:
            return probe[mode, 0], probe[mode, 1]
        block = waves[s - 1, mode * n : (mode + 1) * n, :]
        return block[:, :n], block[:, n:]

    intensity[...] = jnp.zeros(intensity.shape, F32)
    for s in range(slices):
        last = s + 1 == slices
        obj_re, obj_im = patch[s, 0], patch[s, 1]
        for pair in range(modes // 2):
            res, ims = [], []
            for mode in (2 * pair, 2 * pair + 1):
                re, im = wave_in(s, mode)
                res.append(re * obj_re - im * obj_im)
                ims.append(re * obj_im + im * obj_re)
            x = jnp.concatenate(
                [jnp.concatenate(res, axis=1), jnp.concatenate(ims, axis=1)], axis=0
            )
            z = two_sided(tab, (DFT, DFT_ADJ) if last else (BAND, BAND_ADJ), x)
            if last:
                far[pair * 2 * n : (pair + 1) * 2 * n, :] = z
                squares = z * z
                both = squares[:n] + squares[n:]
                intensity[...] += both[:, :n] + both[:, n:]
            else:
                waves[s, pair * 2 * n : (pair + 1) * 2 * n, :] = z

    factor = 2.0 * weight * (intensity[...] - measured[0])
    for pair in range(modes // 2):
        block = far[pair * 2 * n : (pair + 1) * 2 * n, :]
        scale = jnp.concatenate([jnp.concatenate([factor, factor], axis=1)] * 2, axis=0)
        far[pair * 2 * n : (pair + 1) * 2 * n, :] = two_sided(
            tab, (DFT_ADJ, DFT), to_rows(block * scale)
        )
    for s in reversed(range(slices)):
        obj_re, obj_im = patch[s, 0], patch[s, 1]
        for pair in range(modes // 2):
            res, ims = [], []
            sum_re = sum_im = None
            for mode in (2 * pair, 2 * pair + 1):
                block = far[mode * n : (mode + 1) * n, :]
                g_re, g_im = block[:, :n], block[:, n:]
                re, im = wave_in(s, mode)
                add_re = g_re * re + g_im * im
                add_im = g_im * re - g_re * im
                sum_re = add_re if sum_re is None else sum_re + add_re
                sum_im = add_im if sum_im is None else sum_im + add_im
                res.append(g_re * obj_re + g_im * obj_im)
                ims.append(g_im * obj_re - g_re * obj_im)
            if pair == 0:
                gpatch[0] = sum_re
                gpatch[1] = sum_im
            else:
                gpatch[0] += sum_re
                gpatch[1] += sum_im
            if s > 0:
                x = jnp.concatenate(
                    [jnp.concatenate(res, axis=1), jnp.concatenate(ims, axis=1)], axis=0
                )
                far[pair * 2 * n : (pair + 1) * 2 * n, :] = two_sided(tab, (BAND_ADJ, BAND), x)
            else:
                for k, mode in enumerate((2 * pair, 2 * pair + 1)):
                    gprobe[mode, 0] += res[k]
                    gprobe[mode, 1] += ims[k]
        for c in range(2):
            tall = jnp.concatenate([gpatch[c], jnp.zeros((SUBLANES, n), F32)], axis=0)
            tall = pltpu.roll(tall, drop, 0)
            wide = jnp.concatenate([tall, jnp.zeros(tall.shape, F32)], axis=1)
            wide = pltpu.roll(wide, shift, 1)
            gext[s, c, pl.ds(row_tile, n + SUBLANES), pl.ds(lane_tile, 2 * n)] += wide

    @pl.when(rec == pl.num_programs(0) - 1)
    def _():
        gown[...] = gext[:, :, :, n : n + tile_cols]

        @pl.when(side[0] == 0)
        def _():
            gside[...] = gext[:, :, :, n + tile_cols :]

        @pl.when(side[0] != 0)
        def _():
            gside[...] = gext[:, :, :, :n]


def fields(places, side, own, above, below, beside, probe, tab, measured):
    slices, _, tile_rows, tile_cols = own.shape
    modes, _, n, _ = probe.shape
    rows = tile_rows + 2 * above.shape[2]
    records = measured.shape[0]

    def whole(shape):
        return pl.BlockSpec(shape, lambda r, *_: (0,) * len(shape))

    inputs = (own, above, below, beside, probe, tab)
    outs = [(slices, 2, rows, tile_cols), (slices, 2, rows, n), (modes, 2, n, n)]
    return pl.pallas_call(
        field_kernel,
        out_shape=[jax.ShapeDtypeStruct(s, F32) for s in outs],
        grid_spec=pltpu.PrefetchScalarGridSpec(
            num_scalar_prefetch=2,
            grid=(records,),
            in_specs=[whole(x.shape) for x in inputs]
            + [pl.BlockSpec((1, n, n), lambda r, *_: (r, 0, 0))],
            out_specs=[whole(s) for s in outs],
            scratch_shapes=[
                pltpu.VMEM((slices, 2, rows, tile_cols + 2 * n), F32),
                pltpu.VMEM((slices, 2, rows, tile_cols + 2 * n), F32),
                pltpu.VMEM((slices, 2, n, n), F32),
                pltpu.VMEM((slices - 1, modes * n, 2 * n), F32),
                pltpu.VMEM((modes * n, 2 * n), F32),
                pltpu.VMEM((n, n), F32),
                pltpu.VMEM((2, n, n), F32),
            ],
        ),
        compiler_params=pltpu.CompilerParams(vmem_limit_bytes=56 << 20),
        name="fields",
    )(places, side, *inputs, measured)


def gram_kernel(probe, grad, out):
    rows = jnp.concatenate([probe[...], grad[...]], axis=0)
    out[...] = lax.dot_general(
        rows, rows, (((1,), (1,)), ((), ())), precision=lax.Precision.HIGHEST,
        preferred_element_type=F32,
    )


def gram(probe, grad):
    rows = probe.shape[0] + grad.shape[0]
    return pl.pallas_call(
        gram_kernel, out_shape=jax.ShapeDtypeStruct((rows, rows), F32), name="gram"
    )(probe, grad)


def ortho_kernel(gram_ref, probe, grad, out, *, modes, scale):
    m = modes
    s = gram_ref[...]

    def part(a, b):
        return s[a * m : (a + 1) * m, b * m : (b + 1) * m]

    def complex_part(a, b):
        re = part(2 * a, 2 * b) + part(2 * a + 1, 2 * b + 1)
        im = part(2 * a, 2 * b + 1) - part(2 * a + 1, 2 * b)
        return re, im

    pp, pg, gp, gg = (complex_part(a, b) for a, b in ((0, 0), (0, 1), (1, 0), (1, 1)))
    eye = (
        lax.broadcasted_iota(jnp.int32, (m, m), 0) == lax.broadcasted_iota(jnp.int32, (m, m), 1)
    ).astype(F32)

    def trace(x):
        return jnp.sum(jnp.sum(x * eye, axis=1, keepdims=True), axis=0, keepdims=True)

    factor = 0.5 * jnp.sqrt(trace(pp[0]) / (trace(gg[0]) + 1e-06))
    new_re = pp[0] - factor * (pg[0] + gp[0]) + factor * factor * gg[0]
    new_im = pp[1] - factor * (pg[1] + gp[1]) + factor * factor * gg[1]
    a_re = jnp.concatenate([new_re, eye], axis=1)
    a_im = jnp.concatenate([new_im, jnp.zeros((m, m), F32)], axis=1)
    row_idx = lax.broadcasted_iota(jnp.int32, (m, 1), 0)
    for j in range(m):
        inv = 1.0 / jnp.sqrt(a_re[j : j + 1, j : j + 1])
        r_re = a_re[j : j + 1, :] * inv
        r_im = a_im[j : j + 1, :] * inv
        c_re = jnp.where(row_idx > j, a_re[:, j : j + 1] * inv, 0.0)
        c_im = jnp.where(row_idx > j, a_im[:, j : j + 1] * inv, 0.0)
        at = row_idx == j
        a_re, a_im = (
            jnp.where(at, r_re, a_re - (c_re * r_re - c_im * r_im)),
            jnp.where(at, r_im, a_im - (c_re * r_im + c_im * r_re)),
        )
    inv_re = a_re[:, m:] * scale
    inv_im = a_im[:, m:] * scale
    moved = probe[...] - factor * grad[...]
    mix = jnp.concatenate(
        [
            jnp.concatenate([inv_re, inv_im], axis=1),
            jnp.concatenate([-inv_im, inv_re], axis=1),
        ],
        axis=0,
    )
    out[...] = lax.dot_general(
        mix, moved, (((1,), (0,)), ((), ())), precision=lax.Precision.HIGHEST,
        preferred_element_type=F32,
    )


def ortho(gram_all, probe, grad, modes, scale):
    def body(*refs):
        ortho_kernel(*refs, modes=modes, scale=scale)

    return pl.pallas_call(
        body, out_shape=jax.ShapeDtypeStruct(probe.shape, F32), name="ortho"
    )(gram_all, probe, grad)


def per_device(object_slices, probe, taps, measured, positions):
    width = probe.shape[-1]
    half = width // 2
    slices, _, tile_rows, tile_cols = object_slices.shape
    modes = probe.shape[0]
    row_devices = lax.axis_size("row")
    col_devices = lax.axis_size("col")
    row_idx = lax.axis_index("row")
    col_idx = lax.axis_index("col")

    above = shifted(object_slices[:, :, tile_rows - half :], "row", 1)
    below = shifted(object_slices[:, :, :half], "row", -1)
    near = (1 - col_idx) * (tile_cols - LANES)
    strip = jnp.concatenate([
        lax.dynamic_slice_in_dim(x, near, LANES, 3) for x in (above, object_slices, below)
    ], axis=2)
    beside = swapped(strip, "col", 1)

    tab = block_tables(taps, width)
    anchor = jnp.stack([row_idx * tile_rows - half, col_idx * tile_cols - LANES])
    places = (positions - anchor[None, :]).astype(jnp.int32)
    side = col_idx.astype(jnp.int32).reshape(1)
    gown, gside, gprobe = fields(
        places, side, object_slices, above, below, beside, probe, tab, measured
    )

    devices = row_devices * col_devices
    share = width // devices
    index = row_idx * col_devices + col_idx
    total = gprobe.reshape(modes * 2, width, width)
    lows = [("col", 1, 1)]
    bit = 1
    while bit < row_devices:
        lows.append(("row", bit, bit * col_devices))
        bit *= 2
    span = width
    lows = [lows[0], lows[1]] + lows[:1:-1]
    shape = (modes * 2,) + (2,) * len(lows) + (share, width)
    total = total.reshape(shape)
    dims = list(range(len(lows) - 1, -1, -1))
    for axis, bit, global_bit in lows:
        which = dims.index(global_bit.bit_length() - 1)
        mine = (index // global_bit) % 2
        keep = lax.dynamic_index_in_dim(total, mine, which + 1, keepdims=False)
        send = lax.dynamic_index_in_dim(total, 1 - mine, which + 1, keepdims=False)
        total = keep + swapped(send, axis, bit)
        dims.pop(which)

    def by_part(x):
        return x.reshape(modes, 2, share * width).transpose(1, 0, 2).reshape(2 * modes, -1)

    own_probe = lax.dynamic_slice_in_dim(probe, index * share, share, 2)
    p_rows = by_part(own_probe)
    g_rows = by_part(total)
    gram_all = gram(p_rows, g_rows)
    for axis, bit, _ in lows:
        gram_all = gram_all + swapped(gram_all, axis, bit)
    new_rows = ortho(gram_all, p_rows, g_rows, modes, float(width))
    new_probe = new_rows.reshape(2, modes, share * width).transpose(1, 0, 2)

    got = swapped(gside, "col", 1)
    folded = lax.dynamic_update_slice_in_dim(
        gown, lax.dynamic_slice_in_dim(gown, near, LANES, 3) + got, near, 3
    )
    from_above = shifted(folded[:, :, half + tile_rows :], "row", 1)
    from_below = shifted(folded[:, :, :half], "row", -1)
    middle = folded[:, :, half : half + tile_rows]
    object_grad = middle + jnp.concatenate([from_above, from_below], axis=2)
    return (object_grad, new_probe)


def solution(mesh):
    placed = (
        P(None, None, ("groups", "row"), "col"),
        P("groups", None, None, None),
        P(),
        P(("groups", "row", "col"), None, None),
        P(("groups", "row", "col"), None),
    )
    return jax.shard_map(
        per_device,
        mesh=mesh,
        in_specs=placed,
        out_specs=(P(None, None, ("groups", "row"), "col"), P("groups", None, ("row", "col"))),
        check_vma=False,
    )
```

```python
import math

import jax
import jax.numpy as jnp
import numpy as np
from jax import lax
from jax.experimental import pallas as pl
from jax.experimental.pallas import tpu as pltpu
from jax.sharding import PartitionSpec as P

F32 = jnp.float32
BF16 = jnp.bfloat16
LANES = 128
SUBLANES = 8


def shifted(value, axis, step):
    count = lax.axis_size(axis)
    pairs = [(i, i + step) for i in range(count) if 0 <= i + step < count]
    return lax.ppermute(value, axis, pairs)


def swapped(value, axis, bit):
    count = lax.axis_size(axis)
    return lax.ppermute(value, axis, [(i, i ^ bit) for i in range(count)])


def hi_lo(value):
    high = lax.reduce_precision(value, 8, 7)
    return high.astype(BF16), (value - high).astype(BF16)


def block_tables(taps, width):
    reach = taps.shape[1] // 2
    padded = jnp.pad(taps, ((0, 0), (width, width)))
    idx = lax.iota(jnp.int32, width)
    offset = idx[None, :] - idx[:, None] + reach
    tap_idx = lax.iota(jnp.int32, taps.shape[1])
    hot = (offset[None, :, :] == tap_idx[:, None, None]).astype(F32)
    band_re = jnp.sum(hot * taps[0][:, None, None], axis=0)
    band_im = jnp.sum(hot * taps[1][:, None, None], axis=0)
    phase = np.arange(width)[:, None] * np.arange(width)[None, :] % width
    angle = 2.0 * math.pi / width * phase
    norm = 1.0 / math.sqrt(width)
    dft_re = jnp.asarray(np.cos(angle) * norm, F32)
    dft_im = jnp.asarray(-np.sin(angle) * norm, F32)

    def block(re, im):
        return jnp.concatenate(
            [jnp.concatenate([re, -im], axis=1), jnp.concatenate([im, re], axis=1)], axis=0
        )

    band, dft = block(band_re, band_im), block(dft_re, dft_im)
    parts = []
    for matrix in (band, band.T, dft, dft.T):
        parts.extend(hi_lo(matrix))
    return jnp.stack(parts)


def split(value):
    high = value.astype(BF16)
    return high, (value - high.astype(F32)).astype(BF16)


def mxu(a, b):
    return lax.dot_general(a, b, (((1,), (0,)), ((), ())), preferred_element_type=F32)


def left_product(tab, which, x):
    high, low = split(x)
    w_high, w_low = tab[2 * which], tab[2 * which + 1]
    return mxu(w_high, high) + (mxu(w_high, low) + mxu(w_low, high))


def right_product(tab, which, x):
    high, low = split(x)
    w_high, w_low = tab[2 * which], tab[2 * which + 1]
    return mxu(high, w_high) + (mxu(low, w_high) + mxu(high, w_low))


def to_rows(y):
    n = LANES
    return jnp.concatenate(
        [
            jnp.concatenate([y[:n, :n], y[n:, :n]], axis=1),
            jnp.concatenate([y[:n, n:], y[n:, n:]], axis=1),
        ],
        axis=0,
    )


def two_sided(tab, forward, x):
    base, adjoint = forward
    return right_product(tab, adjoint, to_rows(left_product(tab, base, x)))


BAND, BAND_ADJ, DFT, DFT_ADJ = range(4)


def cut_windows(rec, places, side, own, above, below, beside, ext, patch):
    slices, _, tile_rows, tile_cols = own.shape
    half = above.shape[2]
    n = LANES

    @pl.when(rec == 0)
    def _():
        ext[:, :, :half, n : n + tile_cols] = above[...]
        ext[:, :, half : half + tile_rows, n : n + tile_cols] = own[...]
        ext[:, :, half + tile_rows :, n : n + tile_cols] = below[...]
        nothing = jnp.zeros(beside.shape, F32)

        @pl.when(side[0] == 0)
        def _():
            ext[:, :, :, :n] = nothing
            ext[:, :, :, n + tile_cols :] = beside[...]

        @pl.when(side[0] != 0)
        def _():
            ext[:, :, :, :n] = beside[...]
            ext[:, :, :, n + tile_cols :] = nothing

    row_tile, drop, lane_tile, shift = window_place(places, rec)
    for s in range(slices):
        for c in range(2):
            window = ext[s, c, pl.ds(row_tile, n + SUBLANES), pl.ds(lane_tile, 2 * n)]
            window = pltpu.roll(window, (2 * n - shift) % (2 * n), 1)[:, :n]
            patch[s, c] = pltpu.roll(window, (n + SUBLANES - drop) % (n + SUBLANES), 0)[:n]


def window_place(places, rec):
    row, col = places[rec, 0], places[rec, 1]
    lane_tile = pl.multiple_of(col // LANES * LANES, LANES)
    row_tile = pl.multiple_of(row // SUBLANES * SUBLANES, SUBLANES)
    return row_tile, row % SUBLANES, lane_tile, col % LANES


def through_slice(wave, patch, pair):
    obj_re, obj_im = patch[0], patch[1]
    res, ims = [], []
    for mode in (2 * pair, 2 * pair + 1):
        re, im = wave(mode)
        res.append(re * obj_re - im * obj_im)
        ims.append(re * obj_im + im * obj_re)
    return jnp.concatenate([jnp.concatenate(res, axis=1), jnp.concatenate(ims, axis=1)], axis=0)


def probe_waves(probe):
    return lambda mode: (probe[mode, 0], probe[mode, 1])


def row_waves(waves):
    n = LANES

    def wave(mode):
        block = waves[mode * n : (mode + 1) * n, :]
        return block[:, :n], block[:, n:]

    return wave


def forward_kernel(
    places, side, own, above, below, beside, probe, tab, waves, patches, ext
):
    rec = pl.program_id(0)
    n = LANES
    patch = patches.at[0]
    cut_windows(rec, places, side, own, above, below, beside, ext, patch)
    for s in range(own.shape[0]):
        wave = probe_waves(probe) if s == 0 else row_waves(waves.at[0, s - 1])
        for pair in range(probe.shape[0] // 2):
            x = through_slice(wave, patch.at[s], pair)
            z = two_sided(tab, (BAND, BAND_ADJ), x)
            waves[0, s, pair * 2 * n : (pair + 1) * 2 * n, :] = z


def backward_kernel(
    places, side, own, above, below, beside, probe, tab, measured, waves, patches,
    gown, gside, gprobe, ext, gext, last_patch, far, intensity, gpatch,
):
    rec = pl.program_id(0)
    modes = probe.shape[0]
    n = LANES
    tile_cols = own.shape[3]
    weight = 1.0 / (8.0 * modes)
    slices = waves.shape[1] + 1

    @pl.when(rec == 0)
    def _():
        gext[...] = jnp.zeros(gext.shape, F32)
        gprobe[...] = jnp.zeros(gprobe.shape, F32)

    cut_windows(rec, places, side, own, above, below, beside, ext, last_patch)
    row_tile, drop, lane_tile, shift = window_place(places, rec)

    def wave_into(s):
        return probe_waves(probe) if s == 0 else row_waves(waves.at[0, s - 1])

    def patch_of(s):
        return last_patch.at[0] if s + 1 == slices else patches.at[0, s]

    intensity[...] = jnp.zeros(intensity.shape, F32)
    for pair in range(modes // 2):
        x = through_slice(wave_into(slices - 1), patch_of(slices - 1), pair)
        z = two_sided(tab, (DFT, DFT_ADJ), x)
        far[pair * 2 * n : (pair + 1) * 2 * n, :] = z
        squares = z * z
        both = squares[:n] + squares[n:]
        intensity[...] += both[:, :n] + both[:, n:]

    factor = 2.0 * weight * (intensity[...] - measured[0])
    for pair in range(modes // 2):
        block = far[pair * 2 * n : (pair + 1) * 2 * n, :]
        scale = jnp.concatenate([jnp.concatenate([factor, factor], axis=1)] * 2, axis=0)
        far[pair * 2 * n : (pair + 1) * 2 * n, :] = two_sided(
            tab, (DFT_ADJ, DFT), to_rows(block * scale)
        )
    for s in reversed(range(slices)):
        patch = patch_of(s)
        obj_re, obj_im = patch[0], patch[1]
        wave = wave_into(s)
        for pair in range(modes // 2):
            res, ims = [], []
            sum_re = sum_im = None
            for mode in (2 * pair, 2 * pair + 1):
                g_re, g_im = row_waves(far)(mode)
                re, im = wave(mode)
                add_re = g_re * re + g_im * im
                add_im = g_im * re - g_re * im
                sum_re = add_re if sum_re is None else sum_re + add_re
                sum_im = add_im if sum_im is None else sum_im + add_im
                res.append(g_re * obj_re + g_im * obj_im)
                ims.append(g_im * obj_re - g_re * obj_im)
            if pair == 0:
                gpatch[0] = sum_re
                gpatch[1] = sum_im
            else:
                gpatch[0] += sum_re
                gpatch[1] += sum_im
            if s > 0:
                x = jnp.concatenate(
                    [jnp.concatenate(res, axis=1), jnp.concatenate(ims, axis=1)], axis=0
                )
                far[pair * 2 * n : (pair + 1) * 2 * n, :] = two_sided(tab, (BAND_ADJ, BAND), x)
            else:
                for k, mode in enumerate((2 * pair, 2 * pair + 1)):
                    for c, part in enumerate((res[k], ims[k])):
                        gprobe[:, c * modes + mode] += part.reshape(
                            n // SUBLANES, SUBLANES, n
                        )
        for c in range(2):
            tall = jnp.concatenate([gpatch[c], jnp.zeros((SUBLANES, n), F32)], axis=0)
            tall = pltpu.roll(tall, drop, 0)
            wide = jnp.concatenate([tall, jnp.zeros(tall.shape, F32)], axis=1)
            wide = pltpu.roll(wide, shift, 1)
            gext[s, c, pl.ds(row_tile, n + SUBLANES), pl.ds(lane_tile, 2 * n)] += wide

    @pl.when(rec == pl.num_programs(0) - 1)
    def _():
        gown[...] = gext[:, :, :, n : n + tile_cols]

        @pl.when(side[0] == 0)
        def _():
            gside[...] = gext[:, :, :, n + tile_cols :]

        @pl.when(side[0] != 0)
        def _():
            gside[...] = gext[:, :, :, :n]


def whole(shape):
    return pl.BlockSpec(shape, lambda r, *_: (0,) * len(shape))


def one_record(shape):
    return pl.BlockSpec((1,) + shape[1:], lambda r, *_: (r,) + (0,) * (len(shape) - 1))


def forward(places, side, objects, halo, probe, tab):
    above, below, beside = halo
    slices = above.shape[0]
    tile_rows, tile_cols = objects.shape[2:]
    modes, _, n, _ = probe.shape
    rows = tile_rows + 2 * above.shape[2]
    records = places.shape[0]
    outs = [(records, slices, modes * n, 2 * n), (records, slices, 2, n, n)]
    return pl.pallas_call(
        forward_kernel,
        out_shape=[jax.ShapeDtypeStruct(s, F32) for s in outs],
        grid_spec=pltpu.PrefetchScalarGridSpec(
            num_scalar_prefetch=2,
            grid=(records,),
            in_specs=[whole((slices,) + objects.shape[1:])]
            + [whole(x.shape) for x in (above, below, beside, probe, tab)],
            out_specs=[one_record(s) for s in outs],
            scratch_shapes=[pltpu.VMEM((slices, 2, rows, tile_cols + 2 * n), F32)],
        ),
        compiler_params=pltpu.CompilerParams(vmem_limit_bytes=56 << 20),
        name="forward",
    )(places, side, objects, above, below, beside, probe, tab)


def backward(places, side, objects, halo, probe, tab, measured, waves, patches):
    above, below, beside = halo
    slices, _, tile_rows, tile_cols = objects.shape
    modes, _, n, _ = probe.shape
    rows = tile_rows + 2 * above.shape[2]
    records = measured.shape[0]
    last = (1,) + objects.shape[1:]
    outs = [(slices, 2, rows, tile_cols), (slices, 2, rows, n)]
    outs.append((n // SUBLANES, 2 * modes, SUBLANES, n))
    return pl.pallas_call(
        backward_kernel,
        out_shape=[jax.ShapeDtypeStruct(s, F32) for s in outs],
        grid_spec=pltpu.PrefetchScalarGridSpec(
            num_scalar_prefetch=2,
            grid=(records,),
            in_specs=[pl.BlockSpec(last, lambda r, *_: (slices - 1, 0, 0, 0))]
            + [whole(x.shape) for x in (above, below, beside, probe, tab)]
            + [one_record(x.shape) for x in (measured, waves, patches)],
            out_specs=[whole(s) for s in outs],
            scratch_shapes=[
                pltpu.VMEM((1, 2, rows, tile_cols + 2 * n), F32),
                pltpu.VMEM((slices, 2, rows, tile_cols + 2 * n), F32),
                pltpu.VMEM((1, 2, n, n), F32),
                pltpu.VMEM((modes * n, 2 * n), F32),
                pltpu.VMEM((n, n), F32),
                pltpu.VMEM((2, n, n), F32),
            ],
        ),
        compiler_params=pltpu.CompilerParams(vmem_limit_bytes=56 << 20),
        name="backward",
    )(places, side, objects, above, below, beside, probe, tab, measured, waves, patches)


def gram_kernel(which, probe, first, second, out, own):
    total = None
    for b in range(probe.shape[0]):
        for i in range(probe.shape[2]):
            grad = first[b, :, i, :] + second[b, :, i, :]
            rows = jnp.concatenate([probe[b, :, i, :], grad], axis=0)
            one = lax.dot_general(
                rows, rows, (((1,), (1,)), ((), ())), precision=lax.Precision.HIGHEST,
                preferred_element_type=F32,
            )
            total = one if total is None else total + one
    out[...] = total
    own[...] = first[which[0]] + second[which[0]]


def gram(which, probe, first, second):
    rows = 2 * probe.shape[1]
    specs = [pl.BlockSpec(memory_space=pltpu.VMEM)] * 3
    return pl.pallas_call(
        gram_kernel,
        in_specs=[pl.BlockSpec(memory_space=pltpu.SMEM)] + specs,
        out_specs=[specs[0]] * 2,
        out_shape=[
            jax.ShapeDtypeStruct((rows, rows), F32),
            jax.ShapeDtypeStruct(probe.shape[1:], F32),
        ],
        name="gram",
    )(which, probe, first, second)


def ortho_kernel(*refs, modes, scale):
    *grams, probe, grad, out = refs
    m = modes
    s = grams[0][...]
    for other in grams[1:]:
        s = s + other[...]

    def part(a, b):
        return s[a * m : (a + 1) * m, b * m : (b + 1) * m]

    def complex_part(a, b):
        re = part(2 * a, 2 * b) + part(2 * a + 1, 2 * b + 1)
        im = part(2 * a, 2 * b + 1) - part(2 * a + 1, 2 * b)
        return re, im

    pp, pg, gp, gg = (complex_part(a, b) for a, b in ((0, 0), (0, 1), (1, 0), (1, 1)))
    eye = (
        lax.broadcasted_iota(jnp.int32, (m, m), 0) == lax.broadcasted_iota(jnp.int32, (m, m), 1)
    ).astype(F32)

    def trace(x):
        return jnp.sum(jnp.sum(x * eye, axis=1, keepdims=True), axis=0, keepdims=True)

    factor = 0.5 * jnp.sqrt(trace(pp[0]) / (trace(gg[0]) + 1e-06))
    new_re = pp[0] - factor * (pg[0] + gp[0]) + factor * factor * gg[0]
    new_im = pp[1] - factor * (pg[1] + gp[1]) + factor * factor * gg[1]
    a_re = jnp.concatenate([new_re, eye], axis=1)
    a_im = jnp.concatenate([new_im, jnp.zeros((m, m), F32)], axis=1)
    row_idx = lax.broadcasted_iota(jnp.int32, (m, 1), 0)
    for j in range(m):
        inv = 1.0 / jnp.sqrt(a_re[j : j + 1, j : j + 1])
        r_re = a_re[j : j + 1, :] * inv
        r_im = a_im[j : j + 1, :] * inv
        c_re = jnp.where(row_idx > j, a_re[:, j : j + 1] * inv, 0.0)
        c_im = jnp.where(row_idx > j, a_im[:, j : j + 1] * inv, 0.0)
        at = row_idx == j
        a_re, a_im = (
            jnp.where(at, r_re, a_re - (c_re * r_re - c_im * r_im)),
            jnp.where(at, r_im, a_im - (c_re * r_im + c_im * r_re)),
        )
    inv_re = a_re[:, m:] * scale
    inv_im = a_im[:, m:] * scale
    mix = jnp.concatenate(
        [
            jnp.concatenate([inv_re, inv_im], axis=1),
            jnp.concatenate([-inv_im, inv_re], axis=1),
        ],
        axis=0,
    )
    n = probe.shape[2]
    for i in range(probe.shape[1]):
        moved = probe[:, i, :] - factor * grad[:, i, :]
        new = lax.dot_general(
            mix, moved, (((1,), (0,)), ((), ())), precision=lax.Precision.HIGHEST,
            preferred_element_type=F32,
        )
        out[:, 0, i * n : (i + 1) * n] = new[:m]
        out[:, 1, i * n : (i + 1) * n] = new[m:]


def ortho(grams, probe, grad, modes, scale):
    def body(*refs):
        ortho_kernel(*refs, modes=modes, scale=scale)

    pixels = probe.shape[1] * probe.shape[2]
    return pl.pallas_call(
        body, out_shape=jax.ShapeDtypeStruct((modes, 2, pixels), F32), name="ortho"
    )(*grams, probe, grad)


def take(array, which, dim):
    return lax.dynamic_index_in_dim(array, which, dim, keepdims=False)


def updates(probe, grad, bottom, top, middle):
    modes, _, width, _ = probe.shape
    row_devices = lax.axis_size("row")
    col_devices = lax.axis_size("col")
    devices = row_devices * col_devices
    share = width // devices
    index = lax.axis_index("row") * col_devices + lax.axis_index("col")
    if share != SUBLANES:
        grad = grad.transpose(0, 2, 1, 3).reshape(devices, share, 2 * modes, width)
        grad = grad.transpose(0, 2, 1, 3)

    bits = devices.bit_length() - 1
    grad = grad.reshape((2,) * bits + (2 * modes, share, width))
    row_bits = [1 << b for b in range(bits - 1)]
    order = [("col", 1, 0)] + [("row", bit, bit.bit_length()) for bit in row_bits[1:]]
    left = list(range(bits))[::-1]
    parts = [grad]
    for axis, bit, place in order:
        dim = left.index(place)
        mine = (index >> place) % 2
        send = sum(take(p, 1 - mine, dim) for p in parts)
        keep = sum(take(p, mine, dim) for p in parts)
        received = swapped(send, axis, bit)
        left.pop(dim)
        if len(left) == bits - 2:
            received, bottom, top = lax.optimization_barrier((received, bottom, top))
        parts = [keep, received]
    from_above = shifted(bottom, "row", 1)
    from_below = shifted(top, "row", -1)
    first = sum(parts)
    second = swapped(first, "row", 1)
    mine = (index >> 1) % 2
    base = index - 2 * mine
    blocks = jnp.stack([
        lax.dynamic_slice_in_dim(probe, (base + 2 * k) * share, share, 2) for k in range(2)
    ])
    blocks = blocks.transpose(0, 2, 1, 3, 4).reshape(2, 2 * modes, share, width)
    total, own_grad = gram(mine.astype(jnp.int32).reshape(1), blocks, first, second)
    own_probe = take(blocks, mine, 0)
    left = row_bits[1:]
    while left:
        if len(left) > 1:
            a, b, *left = left
            total = (total + swapped(total, "row", a)) + (
                swapped(total, "row", b) + swapped(total, "row", a ^ b)
            )
        else:
            total = total + swapped(total, "row", left.pop())
    object_grad = middle + jnp.concatenate([from_above, from_below], axis=2)
    total, object_grad = lax.optimization_barrier((total, object_grad))
    grams = [total, swapped(total, "col", 1)]
    return ortho(grams, own_probe, own_grad, modes, float(width)), object_grad


def row_halo(objects, half):
    rows = objects.shape[2]
    above = shifted(objects[:, :, rows - half :], "row", 1)
    below = shifted(objects[:, :, :half], "row", -1)
    return above, below


def with_strip(objects, above, below, near):
    strip = jnp.concatenate([
        lax.dynamic_slice_in_dim(x, near, LANES, 3) for x in (above, objects, below)
    ], axis=2)
    return above, below, swapped(strip, "col", 1)


def per_device(object_slices, probe, taps, measured, positions):
    width = probe.shape[-1]
    half = width // 2
    slices, _, tile_rows, tile_cols = object_slices.shape
    row_idx = lax.axis_index("row")
    col_idx = lax.axis_index("col")
    near = (1 - col_idx) * (tile_cols - LANES)

    lead, last = object_slices[: slices - 1], object_slices[slices - 1 :]
    lead_rows = row_halo(lead, half)
    last_rows = row_halo(last, half)
    tab = block_tables(taps, width)
    anchor = jnp.stack([row_idx * tile_rows - half, col_idx * tile_cols - LANES])
    places = (positions - anchor[None, :]).astype(jnp.int32)
    side = col_idx.astype(jnp.int32).reshape(1)
    lead_rows, tab = lax.optimization_barrier((lead_rows, tab))
    waves, patches = forward(
        places, side, object_slices, with_strip(lead, *lead_rows, near), probe, tab
    )
    last_rows, waves = lax.optimization_barrier((last_rows, waves))
    gown, gside, gprobe = backward(
        places, side, object_slices, with_strip(last, *last_rows, near), probe, tab,
        measured, waves, patches,
    )

    got = swapped(gside, "col", 1)
    folded = lax.dynamic_update_slice_in_dim(
        gown, lax.dynamic_slice_in_dim(gown, near, LANES, 3) + got, near, 3
    )
    bottom, top = folded[:, :, half + tile_rows :], folded[:, :, :half]
    middle = folded[:, :, half : half + tile_rows]
    new_probe, object_grad = updates(probe, gprobe, bottom, top, middle)
    return (object_grad, new_probe)


def solution(mesh):
    placed = (
        P(None, None, ("groups", "row"), "col"),
        P("groups", None, None, None),
        P(),
        P(("groups", "row", "col"), None, None),
        P(("groups", "row", "col"), None),
    )
    return jax.shard_map(
        per_device,
        mesh=mesh,
        in_specs=placed,
        out_specs=(P(None, None, ("groups", "row"), "col"), P("groups", None, ("row", "col"))),
        check_vma=False,
    )
```

```python
import math

import jax
import jax.numpy as jnp
import numpy as np
from jax import lax
from jax.experimental import pallas as pl
from jax.experimental.pallas import tpu as pltpu
from jax.sharding import PartitionSpec as P

F32 = jnp.float32
BF16 = jnp.bfloat16
LANES = 128
SUBLANES = 8


def shifted(value, axis, step):
    count = lax.axis_size(axis)
    pairs = [(i, i + step) for i in range(count) if 0 <= i + step < count]
    return lax.ppermute(value, axis, pairs)


def swapped(value, axis, bit):
    count = lax.axis_size(axis)
    return lax.ppermute(value, axis, [(i, i ^ bit) for i in range(count)])


def hi_lo(value):
    high = lax.reduce_precision(value, 8, 7)
    return high.astype(BF16), (value - high).astype(BF16)


def block_tables(taps, width):
    reach = taps.shape[1] // 2
    padded = jnp.pad(taps, ((0, 0), (width, width)))
    idx = lax.iota(jnp.int32, width)
    offset = idx[None, :] - idx[:, None] + reach
    tap_idx = lax.iota(jnp.int32, taps.shape[1])
    hot = (offset[None, :, :] == tap_idx[:, None, None]).astype(F32)
    band_re = jnp.sum(hot * taps[0][:, None, None], axis=0)
    band_im = jnp.sum(hot * taps[1][:, None, None], axis=0)
    phase = np.arange(width)[:, None] * np.arange(width)[None, :] % width
    angle = 2.0 * math.pi / width * phase
    norm = 1.0 / math.sqrt(width)
    dft_re = jnp.asarray(np.cos(angle) * norm, F32)
    dft_im = jnp.asarray(-np.sin(angle) * norm, F32)

    def block(re, im):
        return jnp.concatenate(
            [jnp.concatenate([re, -im], axis=1), jnp.concatenate([im, re], axis=1)], axis=0
        )

    band, dft = block(band_re, band_im), block(dft_re, dft_im)
    parts = []
    for matrix in (band, band.T, dft, dft.T):
        parts.extend(hi_lo(matrix))
    return jnp.stack(parts)


def split(value):
    high = value.astype(BF16)
    return high, (value - high.astype(F32)).astype(BF16)


def mxu(a, b):
    return lax.dot_general(a, b, (((1,), (0,)), ((), ())), preferred_element_type=F32)


def left_product(tab, which, x):
    high, low = split(x)
    w_high, w_low = tab[2 * which], tab[2 * which + 1]
    return mxu(w_high, high) + (mxu(w_high, low) + mxu(w_low, high))


def right_product(tab, which, x):
    high, low = split(x)
    w_high, w_low = tab[2 * which], tab[2 * which + 1]
    return mxu(high, w_high) + (mxu(low, w_high) + mxu(high, w_low))


def to_rows(y):
    n = LANES
    return jnp.concatenate(
        [
            jnp.concatenate([y[:n, :n], y[n:, :n]], axis=1),
            jnp.concatenate([y[:n, n:], y[n:, n:]], axis=1),
        ],
        axis=0,
    )


def two_sided(tab, forward, x):
    base, adjoint = forward
    return right_product(tab, adjoint, to_rows(left_product(tab, base, x)))


BAND, BAND_ADJ, DFT, DFT_ADJ = range(4)


def field_kernel(
    places, side, own, above, below, beside, probe, tab, measured,
    gown, gside, gprobe, ext, gext, patch, waves, far, intensity, gpatch,
):
    rec = pl.program_id(0)
    slices = own.shape[0]
    modes = probe.shape[0]
    n = LANES
    tile_cols = own.shape[3]
    half = above.shape[2]
    tile_rows = own.shape[2]
    weight = 1.0 / (8.0 * modes)

    @pl.when(rec == 0)
    def _():
        gext[...] = jnp.zeros(gext.shape, F32)
        gprobe[...] = jnp.zeros(gprobe.shape, F32)
        ext[:, :, :half, n : n + tile_cols] = above[...]
        ext[:, :, half : half + tile_rows, n : n + tile_cols] = own[...]
        ext[:, :, half + tile_rows :, n : n + tile_cols] = below[...]
        nothing = jnp.zeros(beside.shape, F32)

        @pl.when(side[0] == 0)
        def _():
            ext[:, :, :, :n] = nothing
            ext[:, :, :, n + tile_cols :] = beside[...]

        @pl.when(side[0] != 0)
        def _():
            ext[:, :, :, :n] = beside[...]
            ext[:, :, :, n + tile_cols :] = nothing

    row = places[rec, 0]
    col = places[rec, 1]
    lane_tile = pl.multiple_of(col // n * n, n)
    shift = col % n
    row_tile = pl.multiple_of(row // SUBLANES * SUBLANES, SUBLANES)
    drop = row % SUBLANES
    for s in range(slices):
        for c in range(2):
            window = ext[s, c, pl.ds(row_tile, n + SUBLANES), pl.ds(lane_tile, 2 * n)]
            window = pltpu.roll(window, (2 * n - shift) % (2 * n), 1)[:, :n]
            patch[s, c] = pltpu.roll(window, (n + SUBLANES - drop) % (n + SUBLANES), 0)[:n]

    def wave_in(s, mode):
        if s == 0:
            return probe[mode, 0], probe[mode, 1]
        block = waves[s - 1, mode * n : (mode + 1) * n, :]
        return block[:, :n], block[:, n:]

    intensity[...] = jnp.zeros(intensity.shape, F32)
    for s in range(slices):
        last = s + 1 == slices
        obj_re, obj_im = patch[s, 0], patch[s, 1]
        for pair in range(modes // 2):
            res, ims = [], []
            for mode in (2 * pair, 2 * pair + 1):
                re, im = wave_in(s, mode)
                res.append(re * obj_re - im * obj_im)
                ims.append(re * obj_im + im * obj_re)
            x = jnp.concatenate(
                [jnp.concatenate(res, axis=1), jnp.concatenate(ims, axis=1)], axis=0
            )
            z = two_sided(tab, (DFT, DFT_ADJ) if last else (BAND, BAND_ADJ), x)
            if last:
                far[pair * 2 * n : (pair + 1) * 2 * n, :] = z
                squares = z * z
                both = squares[:n] + squares[n:]
                intensity[...] += both[:, :n] + both[:, n:]
            else:
                waves[s, pair * 2 * n : (pair + 1) * 2 * n, :] = z

    factor = 2.0 * weight * (intensity[...] - measured[0])
    for pair in range(modes // 2):
        block = far[pair * 2 * n : (pair + 1) * 2 * n, :]
        scale = jnp.concatenate([jnp.concatenate([factor, factor], axis=1)] * 2, axis=0)
        far[pair * 2 * n : (pair + 1) * 2 * n, :] = two_sided(
            tab, (DFT_ADJ, DFT), to_rows(block * scale)
        )
    for s in reversed(range(slices)):
        obj_re, obj_im = patch[s, 0], patch[s, 1]
        for pair in range(modes // 2):
            res, ims = [], []
            sum_re = sum_im = None
            for mode in (2 * pair, 2 * pair + 1):
                block = far[mode * n : (mode + 1) * n, :]
                g_re, g_im = block[:, :n], block[:, n:]
                re, im = wave_in(s, mode)
                add_re = g_re * re + g_im * im
                add_im = g_im * re - g_re * im
                sum_re = add_re if sum_re is None else sum_re + add_re
                sum_im = add_im if sum_im is None else sum_im + add_im
                res.append(g_re * obj_re + g_im * obj_im)
                ims.append(g_im * obj_re - g_re * obj_im)
            if pair == 0:
                gpatch[0] = sum_re
                gpatch[1] = sum_im
            else:
                gpatch[0] += sum_re
                gpatch[1] += sum_im
            if s > 0:
                x = jnp.concatenate(
                    [jnp.concatenate(res, axis=1), jnp.concatenate(ims, axis=1)], axis=0
                )
                far[pair * 2 * n : (pair + 1) * 2 * n, :] = two_sided(tab, (BAND_ADJ, BAND), x)
            else:
                for k, mode in enumerate((2 * pair, 2 * pair + 1)):
                    for c, part in enumerate((res[k], ims[k])):
                        gprobe[:, c * modes + mode] += part.reshape(
                            n // SUBLANES, SUBLANES, n
                        )
        for c in range(2):
            tall = jnp.concatenate([gpatch[c], jnp.zeros((SUBLANES, n), F32)], axis=0)
            tall = pltpu.roll(tall, drop, 0)
            wide = jnp.concatenate([tall, jnp.zeros(tall.shape, F32)], axis=1)
            wide = pltpu.roll(wide, shift, 1)
            gext[s, c, pl.ds(row_tile, n + SUBLANES), pl.ds(lane_tile, 2 * n)] += wide

    @pl.when(rec == pl.num_programs(0) - 1)
    def _():
        gown[...] = gext[:, :, :, n : n + tile_cols]

        @pl.when(side[0] == 0)
        def _():
            gside[...] = gext[:, :, :, n + tile_cols :]

        @pl.when(side[0] != 0)
        def _():
            gside[...] = gext[:, :, :, :n]


def fields(places, side, own, above, below, beside, probe, tab, measured):
    slices, _, tile_rows, tile_cols = own.shape
    modes, _, n, _ = probe.shape
    rows = tile_rows + 2 * above.shape[2]
    records = measured.shape[0]

    def whole(shape):
        return pl.BlockSpec(shape, lambda r, *_: (0,) * len(shape))

    inputs = (own, above, below, beside, probe, tab)
    outs = [(slices, 2, rows, tile_cols), (slices, 2, rows, n)]
    outs.append((n // SUBLANES, 2 * modes, SUBLANES, n))
    return pl.pallas_call(
        field_kernel,
        out_shape=[jax.ShapeDtypeStruct(s, F32) for s in outs],
        grid_spec=pltpu.PrefetchScalarGridSpec(
            num_scalar_prefetch=2,
            grid=(records,),
            in_specs=[whole(x.shape) for x in inputs]
            + [pl.BlockSpec((1, n, n), lambda r, *_: (r, 0, 0))],
            out_specs=[whole(s) for s in outs],
            scratch_shapes=[
                pltpu.VMEM((slices, 2, rows, tile_cols + 2 * n), F32),
                pltpu.VMEM((slices, 2, rows, tile_cols + 2 * n), F32),
                pltpu.VMEM((slices, 2, n, n), F32),
                pltpu.VMEM((slices - 1, modes * n, 2 * n), F32),
                pltpu.VMEM((modes * n, 2 * n), F32),
                pltpu.VMEM((n, n), F32),
                pltpu.VMEM((2, n, n), F32),
            ],
        ),
        compiler_params=pltpu.CompilerParams(vmem_limit_bytes=56 << 20),
        name="fields",
    )(places, side, *inputs, measured)


def gram_kernel(which, probe, first, second, out, own):
    total = None
    for b in range(probe.shape[0]):
        for i in range(probe.shape[2]):
            grad = first[b, :, i, :] + second[b, :, i, :]
            rows = jnp.concatenate([probe[b, :, i, :], grad], axis=0)
            one = lax.dot_general(
                rows, rows, (((1,), (1,)), ((), ())), precision=lax.Precision.HIGHEST,
                preferred_element_type=F32,
            )
            total = one if total is None else total + one
    out[...] = total
    own[...] = first[which[0]] + second[which[0]]


def gram(which, probe, first, second):
    rows = 2 * probe.shape[1]
    specs = [pl.BlockSpec(memory_space=pltpu.VMEM)] * 3
    return pl.pallas_call(
        gram_kernel,
        in_specs=[pl.BlockSpec(memory_space=pltpu.SMEM)] + specs,
        out_specs=[specs[0]] * 2,
        out_shape=[
            jax.ShapeDtypeStruct((rows, rows), F32),
            jax.ShapeDtypeStruct(probe.shape[1:], F32),
        ],
        name="gram",
    )(which, probe, first, second)


def ortho_kernel(*refs, modes, scale):
    *grams, probe, grad, out = refs
    m = modes
    s = grams[0][...]
    for other in grams[1:]:
        s = s + other[...]

    def part(a, b):
        return s[a * m : (a + 1) * m, b * m : (b + 1) * m]

    def complex_part(a, b):
        re = part(2 * a, 2 * b) + part(2 * a + 1, 2 * b + 1)
        im = part(2 * a, 2 * b + 1) - part(2 * a + 1, 2 * b)
        return re, im

    pp, pg, gp, gg = (complex_part(a, b) for a, b in ((0, 0), (0, 1), (1, 0), (1, 1)))
    eye = (
        lax.broadcasted_iota(jnp.int32, (m, m), 0) == lax.broadcasted_iota(jnp.int32, (m, m), 1)
    ).astype(F32)

    def trace(x):
        return jnp.sum(jnp.sum(x * eye, axis=1, keepdims=True), axis=0, keepdims=True)

    factor = 0.5 * jnp.sqrt(trace(pp[0]) / (trace(gg[0]) + 1e-06))
    new_re = pp[0] - factor * (pg[0] + gp[0]) + factor * factor * gg[0]
    new_im = pp[1] - factor * (pg[1] + gp[1]) + factor * factor * gg[1]
    a_re = jnp.concatenate([new_re, eye], axis=1)
    a_im = jnp.concatenate([new_im, jnp.zeros((m, m), F32)], axis=1)
    row_idx = lax.broadcasted_iota(jnp.int32, (m, 1), 0)
    for j in range(m):
        inv = 1.0 / jnp.sqrt(a_re[j : j + 1, j : j + 1])
        r_re = a_re[j : j + 1, :] * inv
        r_im = a_im[j : j + 1, :] * inv
        c_re = jnp.where(row_idx > j, a_re[:, j : j + 1] * inv, 0.0)
        c_im = jnp.where(row_idx > j, a_im[:, j : j + 1] * inv, 0.0)
        at = row_idx == j
        a_re, a_im = (
            jnp.where(at, r_re, a_re - (c_re * r_re - c_im * r_im)),
            jnp.where(at, r_im, a_im - (c_re * r_im + c_im * r_re)),
        )
    inv_re = a_re[:, m:] * scale
    inv_im = a_im[:, m:] * scale
    mix = jnp.concatenate(
        [
            jnp.concatenate([inv_re, inv_im], axis=1),
            jnp.concatenate([-inv_im, inv_re], axis=1),
        ],
        axis=0,
    )
    n = probe.shape[2]
    for i in range(probe.shape[1]):
        moved = probe[:, i, :] - factor * grad[:, i, :]
        new = lax.dot_general(
            mix, moved, (((1,), (0,)), ((), ())), precision=lax.Precision.HIGHEST,
            preferred_element_type=F32,
        )
        out[:, 0, i * n : (i + 1) * n] = new[:m]
        out[:, 1, i * n : (i + 1) * n] = new[m:]


def ortho(grams, probe, grad, modes, scale):
    def body(*refs):
        ortho_kernel(*refs, modes=modes, scale=scale)

    pixels = probe.shape[1] * probe.shape[2]
    return pl.pallas_call(
        body, out_shape=jax.ShapeDtypeStruct((modes, 2, pixels), F32), name="ortho"
    )(*grams, probe, grad)


def take(array, which, dim):
    return lax.dynamic_index_in_dim(array, which, dim, keepdims=False)


def updates(probe, grad, bottom, top, middle):
    modes, _, width, _ = probe.shape
    row_devices = lax.axis_size("row")
    col_devices = lax.axis_size("col")
    devices = row_devices * col_devices
    share = width // devices
    index = lax.axis_index("row") * col_devices + lax.axis_index("col")
    if share != SUBLANES:
        grad = grad.transpose(0, 2, 1, 3).reshape(devices, share, 2 * modes, width)
        grad = grad.transpose(0, 2, 1, 3)

    bits = devices.bit_length() - 1
    grad = grad.reshape((2,) * bits + (2 * modes, share, width))
    row_bits = [1 << b for b in range(bits - 1)]
    order = [("col", 1, 0)] + [("row", bit, bit.bit_length()) for bit in row_bits[:-1]]
    left = list(range(bits))[::-1]
    parts = [grad]
    for axis, bit, place in order:
        dim = left.index(place)
        mine = (index >> place) % 2
        send = sum(take(p, 1 - mine, dim) for p in parts)
        keep = sum(take(p, mine, dim) for p in parts)
        received = swapped(send, axis, bit)
        left.pop(dim)
        if len(left) == bits - 2:
            received, bottom, top = lax.optimization_barrier((received, bottom, top))
        parts = [keep, received]
    from_above = shifted(bottom, "row", 1)
    from_below = shifted(top, "row", -1)
    first = sum(parts)
    second = swapped(first, "row", row_bits[-1])
    place = left[0]
    mine = (index >> place) % 2
    base = index - (mine << place)
    blocks = jnp.stack([
        lax.dynamic_slice_in_dim(probe, (base + (k << place)) * share, share, 2) for k in range(2)
    ])
    blocks = blocks.transpose(0, 2, 1, 3, 4).reshape(2, 2 * modes, share, width)
    total, own_grad = gram(mine.astype(jnp.int32).reshape(1), blocks, first, second)
    own_probe = take(blocks, mine, 0)
    total = total + swapped(total, "col", 1)
    for bit in row_bits[-2:0:-1]:
        total = total + swapped(total, "row", bit)
    grams = [total, swapped(total, "row", 1)]
    new_probe = ortho(grams, own_probe, own_grad, modes, float(width))
    object_grad = middle() + jnp.concatenate([from_above, from_below], axis=2)
    return new_probe, object_grad


def per_device(object_slices, probe, taps, measured, positions):
    width = probe.shape[-1]
    half = width // 2
    slices, _, tile_rows, tile_cols = object_slices.shape
    row_idx = lax.axis_index("row")
    col_idx = lax.axis_index("col")

    above = shifted(object_slices[:, :, tile_rows - half :], "row", 1)
    below = shifted(object_slices[:, :, :half], "row", -1)
    tab = block_tables(taps, width)
    above, below, tab = lax.optimization_barrier((above, below, tab))
    near = (1 - col_idx) * (tile_cols - LANES)
    strip = jnp.concatenate([
        lax.dynamic_slice_in_dim(x, near, LANES, 3) for x in (above, object_slices, below)
    ], axis=2)
    beside = swapped(strip, "col", 1)

    anchor = jnp.stack([row_idx * tile_rows - half, col_idx * tile_cols - LANES])
    places = (positions - anchor[None, :]).astype(jnp.int32)
    side = col_idx.astype(jnp.int32).reshape(1)
    gown, gside, gprobe = fields(
        places, side, object_slices, above, below, beside, probe, tab, measured
    )

    got = swapped(gside, "col", 1)

    def folded(first, last):
        part = got[:, :, first:last]
        low = jnp.where(col_idx == 0, 0.0, part)
        high = jnp.where(col_idx == 0, part, 0.0)
        inner = jnp.zeros(part.shape[:3] + (tile_cols - 2 * LANES,), F32)
        return gown[:, :, first:last] + jnp.concatenate([low, inner, high], axis=3)

    bottom, top = folded(half + tile_rows, tile_rows + 2 * half), folded(0, half)
    new_probe, object_grad = updates(
        probe, gprobe, bottom, top, lambda: folded(half, half + tile_rows)
    )
    return (object_grad, new_probe)


def solution(mesh):
    placed = (
        P(None, None, ("groups", "row"), "col"),
        P("groups", None, None, None),
        P(),
        P(("groups", "row", "col"), None, None),
        P(("groups", "row", "col"), None),
    )
    return jax.shard_map(
        per_device,
        mesh=mesh,
        in_specs=placed,
        out_specs=(P(None, None, ("groups", "row"), "col"), P("groups", None, ("row", "col"))),
        check_vma=False,
    )
```

```python
import math

import jax
import jax.numpy as jnp
import numpy as np
from jax import lax
from jax.experimental import pallas as pl
from jax.experimental.pallas import tpu as pltpu
from jax.sharding import PartitionSpec as P

F32 = jnp.float32
BF16 = jnp.bfloat16
LANES = 128
SUBLANES = 8


def shifted(value, axis, step):
    count = lax.axis_size(axis)
    pairs = [(i, i + step) for i in range(count) if 0 <= i + step < count]
    return lax.ppermute(value, axis, pairs)


def swapped(value, axis, bit):
    count = lax.axis_size(axis)
    return lax.ppermute(value, axis, [(i, i ^ bit) for i in range(count)])


def hi_lo(value):
    high = lax.reduce_precision(value, 8, 7)
    return high.astype(BF16), (value - high).astype(BF16)


def block_tables(taps, width):
    reach = taps.shape[1] // 2
    padded = jnp.pad(taps, ((0, 0), (width, width)))
    idx = lax.iota(jnp.int32, width)
    offset = idx[None, :] - idx[:, None] + reach
    tap_idx = lax.iota(jnp.int32, taps.shape[1])
    hot = (offset[None, :, :] == tap_idx[:, None, None]).astype(F32)
    band_re = jnp.sum(hot * taps[0][:, None, None], axis=0)
    band_im = jnp.sum(hot * taps[1][:, None, None], axis=0)
    phase = np.arange(width)[:, None] * np.arange(width)[None, :] % width
    angle = 2.0 * math.pi / width * phase
    norm = 1.0 / math.sqrt(width)
    dft_re = jnp.asarray(np.cos(angle) * norm, F32)
    dft_im = jnp.asarray(-np.sin(angle) * norm, F32)

    def block(re, im):
        return jnp.concatenate(
            [jnp.concatenate([re, -im], axis=1), jnp.concatenate([im, re], axis=1)], axis=0
        )

    band, dft = block(band_re, band_im), block(dft_re, dft_im)
    parts = []
    for matrix in (band, band.T, dft, dft.T):
        parts.extend(hi_lo(matrix))
    return jnp.stack(parts)


def split(value):
    high = value.astype(BF16)
    return high, (value - high.astype(F32)).astype(BF16)


def mxu(a, b):
    return lax.dot_general(a, b, (((1,), (0,)), ((), ())), preferred_element_type=F32)


def left_product(tab, which, x):
    high, low = split(x)
    w_high, w_low = tab[2 * which], tab[2 * which + 1]
    return mxu(w_high, high) + (mxu(w_high, low) + mxu(w_low, high))


def right_product(tab, which, x):
    high, low = split(x)
    w_high, w_low = tab[2 * which], tab[2 * which + 1]
    return mxu(high, w_high) + (mxu(low, w_high) + mxu(high, w_low))


def to_rows(y):
    n = LANES
    return jnp.concatenate(
        [
            jnp.concatenate([y[:n, :n], y[n:, :n]], axis=1),
            jnp.concatenate([y[:n, n:], y[n:, n:]], axis=1),
        ],
        axis=0,
    )


def two_sided(tab, forward, x):
    base, adjoint = forward
    return right_product(tab, adjoint, to_rows(left_product(tab, base, x)))


BAND, BAND_ADJ, DFT, DFT_ADJ = range(4)


def field_kernel(
    places, side, own, above, below, beside, probe, tab, measured,
    gown, gside, gkeep, gsend, ext, gext, gprobe, patch, waves, far, intensity, gpatch,
):
    rec = pl.program_id(0)
    slices = own.shape[0]
    modes = probe.shape[0]
    n = LANES
    tile_cols = own.shape[3]
    half = above.shape[2]
    tile_rows = own.shape[2]
    weight = 1.0 / (8.0 * modes)

    @pl.when(rec == 0)
    def _():
        gext[...] = jnp.zeros(gext.shape, F32)
        gprobe[...] = jnp.zeros(gprobe.shape, F32)
        ext[:, :, :half, n : n + tile_cols] = above[...]
        ext[:, :, half : half + tile_rows, n : n + tile_cols] = own[...]
        ext[:, :, half + tile_rows :, n : n + tile_cols] = below[...]
        nothing = jnp.zeros(beside.shape, F32)

        @pl.when(side[0] == 0)
        def _():
            ext[:, :, :, :n] = nothing
            ext[:, :, :, n + tile_cols :] = beside[...]

        @pl.when(side[0] != 0)
        def _():
            ext[:, :, :, :n] = beside[...]
            ext[:, :, :, n + tile_cols :] = nothing

    row = places[rec, 0]
    col = places[rec, 1]
    lane_tile = pl.multiple_of(col // n * n, n)
    shift = col % n
    row_tile = pl.multiple_of(row // SUBLANES * SUBLANES, SUBLANES)
    drop = row % SUBLANES
    for s in range(slices):
        for c in range(2):
            window = ext[s, c, pl.ds(row_tile, n + SUBLANES), pl.ds(lane_tile, 2 * n)]
            window = pltpu.roll(window, (2 * n - shift) % (2 * n), 1)[:, :n]
            patch[s, c] = pltpu.roll(window, (n + SUBLANES - drop) % (n + SUBLANES), 0)[:n]

    def wave_in(s, mode):
        if s == 0:
            return probe[mode, 0], probe[mode, 1]
        block = waves[s - 1, mode * n : (mode + 1) * n, :]
        return block[:, :n], block[:, n:]

    intensity[...] = jnp.zeros(intensity.shape, F32)
    for s in range(slices):
        last = s + 1 == slices
        obj_re, obj_im = patch[s, 0], patch[s, 1]
        for pair in range(modes // 2):
            res, ims = [], []
            for mode in (2 * pair, 2 * pair + 1):
                re, im = wave_in(s, mode)
                res.append(re * obj_re - im * obj_im)
                ims.append(re * obj_im + im * obj_re)
            x = jnp.concatenate(
                [jnp.concatenate(res, axis=1), jnp.concatenate(ims, axis=1)], axis=0
            )
            z = two_sided(tab, (DFT, DFT_ADJ) if last else (BAND, BAND_ADJ), x)
            if last:
                far[pair * 2 * n : (pair + 1) * 2 * n, :] = z
                squares = z * z
                both = squares[:n] + squares[n:]
                intensity[...] += both[:, :n] + both[:, n:]
            else:
                waves[s, pair * 2 * n : (pair + 1) * 2 * n, :] = z

    factor = 2.0 * weight * (intensity[...] - measured[0])
    for pair in range(modes // 2):
        block = far[pair * 2 * n : (pair + 1) * 2 * n, :]
        scale = jnp.concatenate([jnp.concatenate([factor, factor], axis=1)] * 2, axis=0)
        far[pair * 2 * n : (pair + 1) * 2 * n, :] = two_sided(
            tab, (DFT_ADJ, DFT), to_rows(block * scale)
        )
    for s in reversed(range(slices)):
        obj_re, obj_im = patch[s, 0], patch[s, 1]
        for pair in range(modes // 2):
            res, ims = [], []
            sum_re = sum_im = None
            for mode in (2 * pair, 2 * pair + 1):
                block = far[mode * n : (mode + 1) * n, :]
                g_re, g_im = block[:, :n], block[:, n:]
                re, im = wave_in(s, mode)
                add_re = g_re * re + g_im * im
                add_im = g_im * re - g_re * im
                sum_re = add_re if sum_re is None else sum_re + add_re
                sum_im = add_im if sum_im is None else sum_im + add_im
                res.append(g_re * obj_re + g_im * obj_im)
                ims.append(g_im * obj_re - g_re * obj_im)
            if pair == 0:
                gpatch[0] = sum_re
                gpatch[1] = sum_im
            else:
                gpatch[0] += sum_re
                gpatch[1] += sum_im
            if s > 0:
                x = jnp.concatenate(
                    [jnp.concatenate(res, axis=1), jnp.concatenate(ims, axis=1)], axis=0
                )
                far[pair * 2 * n : (pair + 1) * 2 * n, :] = two_sided(tab, (BAND_ADJ, BAND), x)
            else:
                for k, mode in enumerate((2 * pair, 2 * pair + 1)):
                    for c, part in enumerate((res[k], ims[k])):
                        gprobe[:, :, c * modes + mode] += part.reshape(gprobe.shape[:2] + (SUBLANES, n))
        for c in range(2):
            tall = jnp.concatenate([gpatch[c], jnp.zeros((SUBLANES, n), F32)], axis=0)
            tall = pltpu.roll(tall, drop, 0)
            wide = jnp.concatenate([tall, jnp.zeros(tall.shape, F32)], axis=1)
            wide = pltpu.roll(wide, shift, 1)
            gext[s, c, pl.ds(row_tile, n + SUBLANES), pl.ds(lane_tile, 2 * n)] += wide

    @pl.when(rec == pl.num_programs(0) - 1)
    def _():
        gown[...] = gext[:, :, :, n : n + tile_cols]

        @pl.when(side[0] == 0)
        def _():
            gside[...] = gext[:, :, :, n + tile_cols :]
            gkeep[...] = gprobe[:, 0]
            gsend[...] = gprobe[:, 1]

        @pl.when(side[0] != 0)
        def _():
            gside[...] = gext[:, :, :, :n]
            gkeep[...] = gprobe[:, 1]
            gsend[...] = gprobe[:, 0]


def fields(places, side, own, above, below, beside, probe, tab, measured):
    slices, _, tile_rows, tile_cols = own.shape
    modes, _, n, _ = probe.shape
    rows = tile_rows + 2 * above.shape[2]
    records = measured.shape[0]

    def whole(shape):
        return pl.BlockSpec(shape, lambda r, *_: (0,) * len(shape))

    inputs = (own, above, below, beside, probe, tab)
    outs = [(slices, 2, rows, tile_cols), (slices, 2, rows, n)]
    halves = (n // SUBLANES // 2, 2 * modes, SUBLANES, n)
    outs.extend([halves, halves])
    return pl.pallas_call(
        field_kernel,
        out_shape=[jax.ShapeDtypeStruct(s, F32) for s in outs],
        grid_spec=pltpu.PrefetchScalarGridSpec(
            num_scalar_prefetch=2,
            grid=(records,),
            in_specs=[whole(x.shape) for x in inputs]
            + [pl.BlockSpec((1, n, n), lambda r, *_: (r, 0, 0))],
            out_specs=[whole(s) for s in outs],
            scratch_shapes=[
                pltpu.VMEM((slices, 2, rows, tile_cols + 2 * n), F32),
                pltpu.VMEM((slices, 2, rows, tile_cols + 2 * n), F32),
                pltpu.VMEM((n // SUBLANES // 2, 2, 2 * modes, SUBLANES, n), F32),
                pltpu.VMEM((slices, 2, n, n), F32),
                pltpu.VMEM((slices - 1, modes * n, 2 * n), F32),
                pltpu.VMEM((modes * n, 2 * n), F32),
                pltpu.VMEM((n, n), F32),
                pltpu.VMEM((2, n, n), F32),
            ],
        ),
        compiler_params=pltpu.CompilerParams(vmem_limit_bytes=56 << 20),
        name="fields",
    )(places, side, *inputs, measured)


def gram_kernel(*refs):
    probe, *parts, out, own = refs
    grad = parts[0][...]
    for part in parts[1:]:
        grad = grad + part[...]
    own[...] = grad
    total = None
    for i in range(probe.shape[1]):
        rows = jnp.concatenate([probe[:, i, :], own[:, i, :]], axis=0)
        one = lax.dot_general(
            rows, rows, (((1,), (1,)), ((), ())), precision=lax.Precision.HIGHEST,
            preferred_element_type=F32,
        )
        total = one if total is None else total + one
    out[...] = total


def gram(probe, parts):
    rows = 2 * probe.shape[0]
    return pl.pallas_call(
        gram_kernel,
        out_shape=[
            jax.ShapeDtypeStruct((rows, rows), F32),
            jax.ShapeDtypeStruct(probe.shape, F32),
        ],
        name="gram",
    )(probe, *parts)


def ortho_kernel(*refs, modes, scale):
    *grams, probe, grad, out = refs
    m = modes
    s = grams[0][...]
    for other in grams[1:]:
        s = s + other[...]

    def part(a, b):
        return s[a * m : (a + 1) * m, b * m : (b + 1) * m]

    def complex_part(a, b):
        re = part(2 * a, 2 * b) + part(2 * a + 1, 2 * b + 1)
        im = part(2 * a, 2 * b + 1) - part(2 * a + 1, 2 * b)
        return re, im

    pp, pg, gp, gg = (complex_part(a, b) for a, b in ((0, 0), (0, 1), (1, 0), (1, 1)))
    eye = (
        lax.broadcasted_iota(jnp.int32, (m, m), 0) == lax.broadcasted_iota(jnp.int32, (m, m), 1)
    ).astype(F32)

    def trace(x):
        return jnp.sum(jnp.sum(x * eye, axis=1, keepdims=True), axis=0, keepdims=True)

    factor = 0.5 * jnp.sqrt(trace(pp[0]) / (trace(gg[0]) + 1e-06))
    new_re = pp[0] - factor * (pg[0] + gp[0]) + factor * factor * gg[0]
    new_im = pp[1] - factor * (pg[1] + gp[1]) + factor * factor * gg[1]
    a_re = jnp.concatenate([new_re, eye], axis=1)
    a_im = jnp.concatenate([new_im, jnp.zeros((m, m), F32)], axis=1)
    row_idx = lax.broadcasted_iota(jnp.int32, (m, 1), 0)
    for j in range(m):
        inv = 1.0 / jnp.sqrt(a_re[j : j + 1, j : j + 1])
        r_re = a_re[j : j + 1, :] * inv
        r_im = a_im[j : j + 1, :] * inv
        c_re = jnp.where(row_idx > j, a_re[:, j : j + 1] * inv, 0.0)
        c_im = jnp.where(row_idx > j, a_im[:, j : j + 1] * inv, 0.0)
        at = row_idx == j
        a_re, a_im = (
            jnp.where(at, r_re, a_re - (c_re * r_re - c_im * r_im)),
            jnp.where(at, r_im, a_im - (c_re * r_im + c_im * r_re)),
        )
    inv_re = a_re[:, m:] * scale
    inv_im = a_im[:, m:] * scale
    mix = jnp.concatenate(
        [
            jnp.concatenate([inv_re, inv_im], axis=1),
            jnp.concatenate([-inv_im, inv_re], axis=1),
        ],
        axis=0,
    )
    n = probe.shape[2]
    for i in range(probe.shape[1]):
        moved = probe[:, i, :] - factor * grad[:, i, :]
        new = lax.dot_general(
            mix, moved, (((1,), (0,)), ((), ())), precision=lax.Precision.HIGHEST,
            preferred_element_type=F32,
        )
        out[:, 0, i * n : (i + 1) * n] = new[:m]
        out[:, 1, i * n : (i + 1) * n] = new[m:]


def ortho(grams, probe, grad, modes, scale):
    def body(*refs):
        ortho_kernel(*refs, modes=modes, scale=scale)

    pixels = probe.shape[1] * probe.shape[2]
    return pl.pallas_call(
        body, out_shape=jax.ShapeDtypeStruct((modes, 2, pixels), F32), name="ortho"
    )(*grams, probe, grad)


def take(array, which, dim):
    return lax.dynamic_index_in_dim(array, which, dim, keepdims=False)


def updates(probe, keep, send, bottom, top, middle):
    modes, _, width, _ = probe.shape
    row_devices = lax.axis_size("row")
    col_devices = lax.axis_size("col")
    devices = row_devices * col_devices
    share = width // devices
    row_idx, col_idx = lax.axis_index("row"), lax.axis_index("col")
    index = row_idx * col_devices + col_idx
    row_bits = [1 << b for b in range(row_devices.bit_length() - 1)]

    if share == SUBLANES and row_devices <= 8:
        received = swapped(send, "col", 1)
        parts = []
        for k in range(row_devices):
            block = take(keep, row_idx ^ k, 0) + take(received, row_idx ^ k, 0)
            parts.append(swapped(block, "row", k) if k else block)
    else:
        even, odd = jnp.where(col_idx == 0, keep, send), jnp.where(col_idx == 0, send, keep)
        grad = jnp.stack([even, odd], axis=1).transpose(0, 1, 3, 2, 4)
        grad = grad.reshape(row_devices, col_devices, share, 2 * modes, width)
        grad = grad.transpose(1, 0, 3, 2, 4)
        grad = take(grad, col_idx, 0) + swapped(take(grad, 1 - col_idx, 0), "col", 1)
        for bit in reversed(row_bits):
            grad = grad.reshape((2, bit) + grad.shape[-3:])
            mine = (row_idx // bit) % 2
            grad = take(grad, mine, 0) + swapped(take(grad, 1 - mine, 0), "row", bit)
        parts = [grad.reshape(2 * modes, share, width)]

    parts, bottom, top = lax.optimization_barrier((parts, bottom, top))
    from_above = shifted(bottom, "row", 1)
    from_below = shifted(top, "row", -1)
    own_probe = lax.dynamic_slice_in_dim(probe, index * share, share, 2)
    own_probe = own_probe.transpose(1, 0, 2, 3).reshape(2 * modes, share, width)
    total, own_grad = gram(own_probe, parts)
    total = total + swapped(total, "col", 1)
    if len(row_bits) % 2:
        total = total + swapped(total, "row", row_bits.pop(0))
    while row_bits:
        a, b, *row_bits = row_bits
        grams = [total] + [swapped(total, "row", k) for k in (a, b, a ^ b)]
        total = (grams[0] + grams[1]) + (grams[2] + grams[3])
    new_probe = ortho(grams, own_probe, own_grad, modes, float(width))
    object_grad = middle() + jnp.concatenate([from_above, from_below], axis=2)
    return new_probe, object_grad


def per_device(object_slices, probe, taps, measured, positions):
    width = probe.shape[-1]
    half = width // 2
    slices, _, tile_rows, tile_cols = object_slices.shape
    row_idx = lax.axis_index("row")
    col_idx = lax.axis_index("col")

    above = shifted(object_slices[:, :, tile_rows - half :], "row", 1)
    below = shifted(object_slices[:, :, :half], "row", -1)
    tab = block_tables(taps, width)
    above, below, tab = lax.optimization_barrier((above, below, tab))
    near = (1 - col_idx) * (tile_cols - LANES)
    strip = jnp.concatenate([
        lax.dynamic_slice_in_dim(x, near, LANES, 3) for x in (above, object_slices, below)
    ], axis=2)
    beside = swapped(strip, "col", 1)

    anchor = jnp.stack([row_idx * tile_rows - half, col_idx * tile_cols - LANES])
    places = (positions - anchor[None, :]).astype(jnp.int32)
    side = col_idx.astype(jnp.int32).reshape(1)
    gown, gside, gkeep, gsend = fields(
        places, side, object_slices, above, below, beside, probe, tab, measured
    )

    got = swapped(gside, "col", 1)

    def folded(first, last):
        part = got[:, :, first:last]
        low = jnp.where(col_idx == 0, 0.0, part)
        high = jnp.where(col_idx == 0, part, 0.0)
        inner = jnp.zeros(part.shape[:3] + (tile_cols - 2 * LANES,), F32)
        return gown[:, :, first:last] + jnp.concatenate([low, inner, high], axis=3)

    bottom, top = folded(half + tile_rows, tile_rows + 2 * half), folded(0, half)
    new_probe, object_grad = updates(
        probe, gkeep, gsend, bottom, top, lambda: folded(half, half + tile_rows)
    )
    return (object_grad, new_probe)


def solution(mesh):
    placed = (
        P(None, None, ("groups", "row"), "col"),
        P("groups", None, None, None),
        P(),
        P(("groups", "row", "col"), None, None),
        P(("groups", "row", "col"), None),
    )
    return jax.shard_map(
        per_device,
        mesh=mesh,
        in_specs=placed,
        out_specs=(P(None, None, ("groups", "row"), "col"), P("groups", None, ("row", "col"))),
        check_vma=False,
    )
```

```python
import math

import jax
import jax.numpy as jnp
import numpy as np
from jax import lax
from jax.experimental import pallas as pl
from jax.experimental.pallas import tpu as pltpu
from jax.sharding import PartitionSpec as P

F32 = jnp.float32
BF16 = jnp.bfloat16
LANES = 128
SUBLANES = 8


def shifted(value, axis, step):
    count = lax.axis_size(axis)
    pairs = [(i, i + step) for i in range(count) if 0 <= i + step < count]
    return lax.ppermute(value, axis, pairs)


def swapped(value, axis, bit):
    count = lax.axis_size(axis)
    return lax.ppermute(value, axis, [(i, i ^ bit) for i in range(count)])


def hi_lo(value):
    high = lax.reduce_precision(value, 8, 7)
    return high.astype(BF16), (value - high).astype(BF16)


def block_tables(taps, width):
    reach = taps.shape[1] // 2
    padded = jnp.pad(taps, ((0, 0), (width, width)))
    idx = lax.iota(jnp.int32, width)
    offset = idx[None, :] - idx[:, None] + reach
    tap_idx = lax.iota(jnp.int32, taps.shape[1])
    hot = (offset[None, :, :] == tap_idx[:, None, None]).astype(F32)
    band_re = jnp.sum(hot * taps[0][:, None, None], axis=0)
    band_im = jnp.sum(hot * taps[1][:, None, None], axis=0)
    phase = np.arange(width)[:, None] * np.arange(width)[None, :] % width
    angle = 2.0 * math.pi / width * phase
    norm = 1.0 / math.sqrt(width)
    dft_re = jnp.asarray(np.cos(angle) * norm, F32)
    dft_im = jnp.asarray(-np.sin(angle) * norm, F32)

    def block(re, im):
        return jnp.concatenate(
            [jnp.concatenate([re, -im], axis=1), jnp.concatenate([im, re], axis=1)], axis=0
        )

    band, dft = block(band_re, band_im), block(dft_re, dft_im)
    parts = []
    for matrix in (band, band.T, dft, dft.T):
        parts.extend(hi_lo(matrix))
    return jnp.stack(parts)


def split(value):
    high = value.astype(BF16)
    return high, (value - high.astype(F32)).astype(BF16)


def mxu(a, b):
    return lax.dot_general(a, b, (((1,), (0,)), ((), ())), preferred_element_type=F32)


def left_product(tab, which, x):
    high, low = split(x)
    w_high, w_low = tab[2 * which], tab[2 * which + 1]
    return mxu(w_high, high) + (mxu(w_high, low) + mxu(w_low, high))


def right_product(tab, which, x):
    high, low = split(x)
    w_high, w_low = tab[2 * which], tab[2 * which + 1]
    return mxu(high, w_high) + (mxu(low, w_high) + mxu(high, w_low))


def to_rows(y):
    n = LANES
    return jnp.concatenate(
        [
            jnp.concatenate([y[:n, :n], y[n:, :n]], axis=1),
            jnp.concatenate([y[:n, n:], y[n:, n:]], axis=1),
        ],
        axis=0,
    )


def two_sided(tab, forward, x):
    base, adjoint = forward
    return right_product(tab, adjoint, to_rows(left_product(tab, base, x)))


BAND, BAND_ADJ, DFT, DFT_ADJ = range(4)


def field_kernel(
    places, side, own, above, below, beside, probe, tab, measured,
    gown, gside, gkeep, gsend, ext, gext, gprobe, patch, waves, far, intensity, gpatch,
):
    rec = pl.program_id(0)
    slices = own.shape[0]
    modes = probe.shape[0]
    n = LANES
    tile_cols = own.shape[3]
    half = above.shape[2]
    tile_rows = own.shape[2]
    weight = 1.0 / (8.0 * modes)

    @pl.when(rec == 0)
    def _():
        gext[...] = jnp.zeros(gext.shape, F32)
        gprobe[...] = jnp.zeros(gprobe.shape, F32)
        ext[:, :, :half, n : n + tile_cols] = above[...]
        ext[:, :, half : half + tile_rows, n : n + tile_cols] = own[...]
        ext[:, :, half + tile_rows :, n : n + tile_cols] = below[...]
        nothing = jnp.zeros(beside.shape, F32)

        @pl.when(side[0] == 0)
        def _():
            ext[:, :, :, :n] = nothing
            ext[:, :, :, n + tile_cols :] = beside[...]

        @pl.when(side[0] != 0)
        def _():
            ext[:, :, :, :n] = beside[...]
            ext[:, :, :, n + tile_cols :] = nothing

    row = places[rec, 0]
    col = places[rec, 1]
    lane_tile = pl.multiple_of(col // n * n, n)
    shift = col % n
    row_tile = pl.multiple_of(row // SUBLANES * SUBLANES, SUBLANES)
    drop = row % SUBLANES
    for s in range(slices):
        for c in range(2):
            window = ext[s, c, pl.ds(row_tile, n + SUBLANES), pl.ds(lane_tile, 2 * n)]
            window = pltpu.roll(window, (2 * n - shift) % (2 * n), 1)[:, :n]
            patch[s, c] = pltpu.roll(window, (n + SUBLANES - drop) % (n + SUBLANES), 0)[:n]

    def wave_in(s, mode):
        if s == 0:
            return probe[mode, 0], probe[mode, 1]
        block = waves[s - 1, mode * n : (mode + 1) * n, :]
        return block[:, :n], block[:, n:]

    intensity[...] = jnp.zeros(intensity.shape, F32)
    for s in range(slices):
        last = s + 1 == slices
        obj_re, obj_im = patch[s, 0], patch[s, 1]
        for pair in range(modes // 2):
            res, ims = [], []
            for mode in (2 * pair, 2 * pair + 1):
                re, im = wave_in(s, mode)
                res.append(re * obj_re - im * obj_im)
                ims.append(re * obj_im + im * obj_re)
            x = jnp.concatenate(
                [jnp.concatenate(res, axis=1), jnp.concatenate(ims, axis=1)], axis=0
            )
            z = two_sided(tab, (DFT, DFT_ADJ) if last else (BAND, BAND_ADJ), x)
            if last:
                far[pair * 2 * n : (pair + 1) * 2 * n, :] = z
                squares = z * z
                both = squares[:n] + squares[n:]
                intensity[...] += both[:, :n] + both[:, n:]
            else:
                waves[s, pair * 2 * n : (pair + 1) * 2 * n, :] = z

    factor = 2.0 * weight * (intensity[...] - measured[0])
    for pair in range(modes // 2):
        block = far[pair * 2 * n : (pair + 1) * 2 * n, :]
        scale = jnp.concatenate([jnp.concatenate([factor, factor], axis=1)] * 2, axis=0)
        far[pair * 2 * n : (pair + 1) * 2 * n, :] = two_sided(
            tab, (DFT_ADJ, DFT), to_rows(block * scale)
        )
    for s in reversed(range(slices)):
        obj_re, obj_im = patch[s, 0], patch[s, 1]
        for pair in range(modes // 2):
            res, ims = [], []
            sum_re = sum_im = None
            for mode in (2 * pair, 2 * pair + 1):
                block = far[mode * n : (mode + 1) * n, :]
                g_re, g_im = block[:, :n], block[:, n:]
                re, im = wave_in(s, mode)
                add_re = g_re * re + g_im * im
                add_im = g_im * re - g_re * im
                sum_re = add_re if sum_re is None else sum_re + add_re
                sum_im = add_im if sum_im is None else sum_im + add_im
                res.append(g_re * obj_re + g_im * obj_im)
                ims.append(g_im * obj_re - g_re * obj_im)
            if pair == 0:
                gpatch[0] = sum_re
                gpatch[1] = sum_im
            else:
                gpatch[0] += sum_re
                gpatch[1] += sum_im
            if s > 0:
                x = jnp.concatenate(
                    [jnp.concatenate(res, axis=1), jnp.concatenate(ims, axis=1)], axis=0
                )
                far[pair * 2 * n : (pair + 1) * 2 * n, :] = two_sided(tab, (BAND_ADJ, BAND), x)
            else:
                for k, mode in enumerate((2 * pair, 2 * pair + 1)):
                    for c, part in enumerate((res[k], ims[k])):
                        gprobe[:, :, c * modes + mode] += part.reshape(gprobe.shape[:2] + (SUBLANES, n))
        for c in range(2):
            tall = jnp.concatenate([gpatch[c], jnp.zeros((SUBLANES, n), F32)], axis=0)
            tall = pltpu.roll(tall, drop, 0)
            wide = jnp.concatenate([tall, jnp.zeros(tall.shape, F32)], axis=1)
            wide = pltpu.roll(wide, shift, 1)
            gext[s, c, pl.ds(row_tile, n + SUBLANES), pl.ds(lane_tile, 2 * n)] += wide

    @pl.when(rec == pl.num_programs(0) - 1)
    def _():
        gown[...] = gext[:, :, :, n : n + tile_cols]

        @pl.when(side[0] == 0)
        def _():
            gside[...] = gext[:, :, :, n + tile_cols :]
            gkeep[...] = gprobe[:, 0]
            gsend[...] = gprobe[:, 1]

        @pl.when(side[0] != 0)
        def _():
            gside[...] = gext[:, :, :, :n]
            gkeep[...] = gprobe[:, 1]
            gsend[...] = gprobe[:, 0]


def fields(places, side, own, above, below, beside, probe, tab, measured):
    slices, _, tile_rows, tile_cols = own.shape
    modes, _, n, _ = probe.shape
    rows = tile_rows + 2 * above.shape[2]
    records = measured.shape[0]

    def whole(shape):
        return pl.BlockSpec(shape, lambda r, *_: (0,) * len(shape))

    inputs = (own, above, below, beside, probe, tab)
    outs = [(slices, 2, rows, tile_cols), (slices, 2, rows, n)]
    halves = (n // SUBLANES // 2, 2 * modes, SUBLANES, n)
    outs.extend([halves, halves])
    return pl.pallas_call(
        field_kernel,
        out_shape=[jax.ShapeDtypeStruct(s, F32) for s in outs],
        grid_spec=pltpu.PrefetchScalarGridSpec(
            num_scalar_prefetch=2,
            grid=(records,),
            in_specs=[whole(x.shape) for x in inputs]
            + [pl.BlockSpec((1, n, n), lambda r, *_: (r, 0, 0))],
            out_specs=[whole(s) for s in outs],
            scratch_shapes=[
                pltpu.VMEM((slices, 2, rows, tile_cols + 2 * n), F32),
                pltpu.VMEM((slices, 2, rows, tile_cols + 2 * n), F32),
                pltpu.VMEM((n // SUBLANES // 2, 2, 2 * modes, SUBLANES, n), F32),
                pltpu.VMEM((slices, 2, n, n), F32),
                pltpu.VMEM((slices - 1, modes * n, 2 * n), F32),
                pltpu.VMEM((modes * n, 2 * n), F32),
                pltpu.VMEM((n, n), F32),
                pltpu.VMEM((2, n, n), F32),
            ],
        ),
        compiler_params=pltpu.CompilerParams(vmem_limit_bytes=56 << 20),
        name="fields",
    )(places, side, *inputs, measured)


def gram_kernel(*refs):
    probe, *parts, out, own = refs
    grad = parts[0][...]
    for part in parts[1:]:
        grad = grad + part[...]
    own[...] = grad
    total = None
    for i in range(probe.shape[1]):
        rows = jnp.concatenate([probe[:, i, :], own[:, i, :]], axis=0)
        one = lax.dot_general(
            rows, rows, (((1,), (1,)), ((), ())), precision=lax.Precision.HIGHEST,
            preferred_element_type=F32,
        )
        total = one if total is None else total + one
    out[...] = total


def gram(probe, parts):
    rows = 2 * probe.shape[0]
    return pl.pallas_call(
        gram_kernel,
        out_shape=[
            jax.ShapeDtypeStruct((rows, rows), F32),
            jax.ShapeDtypeStruct(probe.shape, F32),
        ],
        name="gram",
    )(probe, *parts)


def ortho_kernel(*refs, modes, scale):
    *grams, probe, grad, out = refs
    m = modes
    s = grams[0][...]
    for other in grams[1:]:
        s = s + other[...]

    def part(a, b):
        return s[a * m : (a + 1) * m, b * m : (b + 1) * m]

    def complex_part(a, b):
        re = part(2 * a, 2 * b) + part(2 * a + 1, 2 * b + 1)
        im = part(2 * a, 2 * b + 1) - part(2 * a + 1, 2 * b)
        return re, im

    pp, pg, gp, gg = (complex_part(a, b) for a, b in ((0, 0), (0, 1), (1, 0), (1, 1)))
    eye = (
        lax.broadcasted_iota(jnp.int32, (m, m), 0) == lax.broadcasted_iota(jnp.int32, (m, m), 1)
    ).astype(F32)

    def trace(x):
        return jnp.sum(jnp.sum(x * eye, axis=1, keepdims=True), axis=0, keepdims=True)

    factor = 0.5 * jnp.sqrt(trace(pp[0]) / (trace(gg[0]) + 1e-06))
    new_re = pp[0] - factor * (pg[0] + gp[0]) + factor * factor * gg[0]
    new_im = pp[1] - factor * (pg[1] + gp[1]) + factor * factor * gg[1]
    a_re = jnp.concatenate([new_re, eye], axis=1)
    a_im = jnp.concatenate([new_im, jnp.zeros((m, m), F32)], axis=1)
    row_idx = lax.broadcasted_iota(jnp.int32, (m, 1), 0)
    for j in range(m):
        inv = 1.0 / jnp.sqrt(a_re[j : j + 1, j : j + 1])
        r_re = a_re[j : j + 1, :] * inv
        r_im = a_im[j : j + 1, :] * inv
        c_re = jnp.where(row_idx > j, a_re[:, j : j + 1] * inv, 0.0)
        c_im = jnp.where(row_idx > j, a_im[:, j : j + 1] * inv, 0.0)
        at = row_idx == j
        a_re, a_im = (
            jnp.where(at, r_re, a_re - (c_re * r_re - c_im * r_im)),
            jnp.where(at, r_im, a_im - (c_re * r_im + c_im * r_re)),
        )
    inv_re = a_re[:, m:] * scale
    inv_im = a_im[:, m:] * scale
    mix = jnp.concatenate(
        [
            jnp.concatenate([inv_re, inv_im], axis=1),
            jnp.concatenate([-inv_im, inv_re], axis=1),
        ],
        axis=0,
    )
    n = probe.shape[2]
    for i in range(probe.shape[1]):
        moved = probe[:, i, :] - factor * grad[:, i, :]
        new = lax.dot_general(
            mix, moved, (((1,), (0,)), ((), ())), precision=lax.Precision.HIGHEST,
            preferred_element_type=F32,
        )
        out[:, 0, i * n : (i + 1) * n] = new[:m]
        out[:, 1, i * n : (i + 1) * n] = new[m:]


def ortho(grams, probe, grad, modes, scale):
    def body(*refs):
        ortho_kernel(*refs, modes=modes, scale=scale)

    pixels = probe.shape[1] * probe.shape[2]
    return pl.pallas_call(
        body, out_shape=jax.ShapeDtypeStruct((modes, 2, pixels), F32), name="ortho"
    )(*grams, probe, grad)


def take(array, which, dim):
    return lax.dynamic_index_in_dim(array, which, dim, keepdims=False)


def updates(probe, keep, send, bottom, top, middle):
    modes, _, width, _ = probe.shape
    row_devices = lax.axis_size("row")
    col_devices = lax.axis_size("col")
    devices = row_devices * col_devices
    share = width // devices
    row_idx, col_idx = lax.axis_index("row"), lax.axis_index("col")
    index = row_idx * col_devices + col_idx
    row_bits = [1 << b for b in range(row_devices.bit_length() - 1)]

    if share == SUBLANES and row_devices <= 8:
        received = swapped(send, "col", 1)
        parts = []
        for k in range(row_devices):
            block = take(keep, row_idx ^ k, 0) + take(received, row_idx ^ k, 0)
            parts.append(swapped(block, "row", k) if k else block)
    else:
        even, odd = jnp.where(col_idx == 0, keep, send), jnp.where(col_idx == 0, send, keep)
        grad = jnp.stack([even, odd], axis=1).transpose(0, 1, 3, 2, 4)
        grad = grad.reshape(row_devices, col_devices, share, 2 * modes, width)
        grad = grad.transpose(1, 0, 3, 2, 4)
        grad = take(grad, col_idx, 0) + swapped(take(grad, 1 - col_idx, 0), "col", 1)
        for bit in reversed(row_bits):
            grad = grad.reshape((2, bit) + grad.shape[-3:])
            mine = (row_idx // bit) % 2
            grad = take(grad, mine, 0) + swapped(take(grad, 1 - mine, 0), "row", bit)
        parts = [grad.reshape(2 * modes, share, width)]

    parts, bottom, top = lax.optimization_barrier((parts, bottom, top))
    from_above = shifted(bottom, "row", 1)
    from_below = shifted(top, "row", -1)
    own_probe = lax.dynamic_slice_in_dim(probe, index * share, share, 2)
    own_probe = own_probe.transpose(1, 0, 2, 3).reshape(2 * modes, share, width)
    total, own_grad = gram(own_probe, parts)
    total = total + swapped(total, "col", 1)
    high_bits = row_bits[1:]
    if len(high_bits) % 2:
        total = total + swapped(total, "row", high_bits.pop())
    while high_bits:
        a, b, *high_bits = high_bits
        near, far, both = (swapped(total, "row", k) for k in (a, b, a ^ b))
        total = (total + near) + (far + both)
    grams = [total, swapped(total, "row", row_bits[0])]
    new_probe = ortho(grams, own_probe, own_grad, modes, float(width))
    object_grad = middle() + jnp.concatenate([from_above, from_below], axis=2)
    return new_probe, object_grad


def per_device(object_slices, probe, taps, measured, positions):
    width = probe.shape[-1]
    half = width // 2
    slices, _, tile_rows, tile_cols = object_slices.shape
    row_idx = lax.axis_index("row")
    col_idx = lax.axis_index("col")

    above = shifted(object_slices[:, :, tile_rows - half :], "row", 1)
    below = shifted(object_slices[:, :, :half], "row", -1)
    tab = block_tables(taps, width)
    above, below, tab = lax.optimization_barrier((above, below, tab))
    near = (1 - col_idx) * (tile_cols - LANES)
    strip = jnp.concatenate([
        lax.dynamic_slice_in_dim(x, near, LANES, 3) for x in (above, object_slices, below)
    ], axis=2)
    beside = swapped(strip, "col", 1)

    anchor = jnp.stack([row_idx * tile_rows - half, col_idx * tile_cols - LANES])
    places = (positions - anchor[None, :]).astype(jnp.int32)
    side = col_idx.astype(jnp.int32).reshape(1)
    gown, gside, gkeep, gsend = fields(
        places, side, object_slices, above, below, beside, probe, tab, measured
    )

    got = swapped(gside, "col", 1)

    def folded(first, last):
        part = got[:, :, first:last]
        low = jnp.where(col_idx == 0, 0.0, part)
        high = jnp.where(col_idx == 0, part, 0.0)
        inner = jnp.zeros(part.shape[:3] + (tile_cols - 2 * LANES,), F32)
        return gown[:, :, first:last] + jnp.concatenate([low, inner, high], axis=3)

    bottom, top = folded(half + tile_rows, tile_rows + 2 * half), folded(0, half)
    new_probe, object_grad = updates(
        probe, gkeep, gsend, bottom, top, lambda: folded(half, half + tile_rows)
    )
    return (object_grad, new_probe)


def solution(mesh):
    placed = (
        P(None, None, ("groups", "row"), "col"),
        P("groups", None, None, None),
        P(),
        P(("groups", "row", "col"), None, None),
        P(("groups", "row", "col"), None),
    )
    return jax.shard_map(
        per_device,
        mesh=mesh,
        in_specs=placed,
        out_specs=(P(None, None, ("groups", "row"), "col"), P("groups", None, ("row", "col"))),
        check_vma=False,
    )
```

```python
import math

import jax
import jax.numpy as jnp
import numpy as np
from jax import lax
from jax.experimental import pallas as pl
from jax.experimental.pallas import tpu as pltpu
from jax.sharding import PartitionSpec as P

F32 = jnp.float32
BF16 = jnp.bfloat16
LANES = 128
SUBLANES = 8


def shifted(value, axis, step):
    count = lax.axis_size(axis)
    pairs = [(i, i + step) for i in range(count) if 0 <= i + step < count]
    return lax.ppermute(value, axis, pairs)


def swapped(value, axis, bit):
    count = lax.axis_size(axis)
    return lax.ppermute(value, axis, [(i, i ^ bit) for i in range(count)])


def hi_lo(value):
    high = lax.reduce_precision(value, 8, 7)
    return high.astype(BF16), (value - high).astype(BF16)


def block_tables(taps, width):
    reach = taps.shape[1] // 2
    padded = jnp.pad(taps, ((0, 0), (width, width)))
    idx = lax.iota(jnp.int32, width)
    offset = idx[None, :] - idx[:, None] + reach
    tap_idx = lax.iota(jnp.int32, taps.shape[1])
    hot = (offset[None, :, :] == tap_idx[:, None, None]).astype(F32)
    band_re = jnp.sum(hot * taps[0][:, None, None], axis=0)
    band_im = jnp.sum(hot * taps[1][:, None, None], axis=0)
    phase = np.arange(width)[:, None] * np.arange(width)[None, :] % width
    angle = 2.0 * math.pi / width * phase
    norm = 1.0 / math.sqrt(width)
    dft_re = jnp.asarray(np.cos(angle) * norm, F32)
    dft_im = jnp.asarray(-np.sin(angle) * norm, F32)

    def block(re, im):
        return jnp.concatenate(
            [jnp.concatenate([re, -im], axis=1), jnp.concatenate([im, re], axis=1)], axis=0
        )

    band, dft = block(band_re, band_im), block(dft_re, dft_im)
    parts = []
    for matrix in (band, band.T, dft, dft.T):
        parts.extend(hi_lo(matrix))
    return jnp.stack(parts)


def split(value):
    high = value.astype(BF16)
    return high, (value - high.astype(F32)).astype(BF16)


def mxu(a, b):
    return lax.dot_general(a, b, (((1,), (0,)), ((), ())), preferred_element_type=F32)


def left_product(tab, which, x):
    high, low = split(x)
    w_high, w_low = tab[2 * which], tab[2 * which + 1]
    return mxu(w_high, high) + (mxu(w_high, low) + mxu(w_low, high))


def right_product(tab, which, x):
    high, low = split(x)
    w_high, w_low = tab[2 * which], tab[2 * which + 1]
    return mxu(high, w_high) + (mxu(low, w_high) + mxu(high, w_low))


def to_rows(y):
    n = LANES
    return jnp.concatenate(
        [
            jnp.concatenate([y[:n, :n], y[n:, :n]], axis=1),
            jnp.concatenate([y[:n, n:], y[n:, n:]], axis=1),
        ],
        axis=0,
    )


def two_sided(tab, forward, x):
    base, adjoint = forward
    return right_product(tab, adjoint, to_rows(left_product(tab, base, x)))


BAND, BAND_ADJ, DFT, DFT_ADJ = range(4)


def field_kernel(
    places, side, own, above, below, beside, probe, tab, measured,
    gown, gside, gkeep, gsend, ext, gext, gprobe, patch, waves, far, intensity, gpatch,
):
    rec = pl.program_id(0)
    slices = own.shape[0]
    modes = probe.shape[0]
    n = LANES
    tile_cols = own.shape[3]
    half = above.shape[2]
    tile_rows = own.shape[2]
    weight = 1.0 / (8.0 * modes)

    @pl.when(rec == 0)
    def _():
        gext[...] = jnp.zeros(gext.shape, F32)
        gprobe[...] = jnp.zeros(gprobe.shape, F32)
        ext[:, :, :half, n : n + tile_cols] = above[...]
        ext[:, :, half : half + tile_rows, n : n + tile_cols] = own[...]
        ext[:, :, half + tile_rows :, n : n + tile_cols] = below[...]
        nothing = jnp.zeros(beside.shape, F32)

        @pl.when(side[0] == 0)
        def _():
            ext[:, :, :, :n] = nothing
            ext[:, :, :, n + tile_cols :] = beside[...]

        @pl.when(side[0] != 0)
        def _():
            ext[:, :, :, :n] = beside[...]
            ext[:, :, :, n + tile_cols :] = nothing

    row = places[rec, 0]
    col = places[rec, 1]
    lane_tile = pl.multiple_of(col // n * n, n)
    shift = col % n
    row_tile = pl.multiple_of(row // SUBLANES * SUBLANES, SUBLANES)
    drop = row % SUBLANES
    for s in range(slices):
        for c in range(2):
            window = ext[s, c, pl.ds(row_tile, n + SUBLANES), pl.ds(lane_tile, 2 * n)]
            window = pltpu.roll(window, (2 * n - shift) % (2 * n), 1)[:, :n]
            patch[s, c] = pltpu.roll(window, (n + SUBLANES - drop) % (n + SUBLANES), 0)[:n]

    def wave_in(s, mode):
        if s == 0:
            return probe[mode, 0], probe[mode, 1]
        block = waves[s - 1, mode * n : (mode + 1) * n, :]
        return block[:, :n], block[:, n:]

    intensity[...] = jnp.zeros(intensity.shape, F32)
    for s in range(slices):
        last = s + 1 == slices
        obj_re, obj_im = patch[s, 0], patch[s, 1]
        for pair in range(modes // 2):
            res, ims = [], []
            for mode in (2 * pair, 2 * pair + 1):
                re, im = wave_in(s, mode)
                res.append(re * obj_re - im * obj_im)
                ims.append(re * obj_im + im * obj_re)
            x = jnp.concatenate(
                [jnp.concatenate(res, axis=1), jnp.concatenate(ims, axis=1)], axis=0
            )
            z = two_sided(tab, (DFT, DFT_ADJ) if last else (BAND, BAND_ADJ), x)
            if last:
                far[pair * 2 * n : (pair + 1) * 2 * n, :] = z
                squares = z * z
                both = squares[:n] + squares[n:]
                intensity[...] += both[:, :n] + both[:, n:]
            else:
                waves[s, pair * 2 * n : (pair + 1) * 2 * n, :] = z

    factor = 2.0 * weight * (intensity[...] - measured[0])
    for pair in range(modes // 2):
        block = far[pair * 2 * n : (pair + 1) * 2 * n, :]
        scale = jnp.concatenate([jnp.concatenate([factor, factor], axis=1)] * 2, axis=0)
        far[pair * 2 * n : (pair + 1) * 2 * n, :] = two_sided(
            tab, (DFT_ADJ, DFT), to_rows(block * scale)
        )
    for s in reversed(range(slices)):
        obj_re, obj_im = patch[s, 0], patch[s, 1]
        for pair in range(modes // 2):
            res, ims = [], []
            sum_re = sum_im = None
            for mode in (2 * pair, 2 * pair + 1):
                block = far[mode * n : (mode + 1) * n, :]
                g_re, g_im = block[:, :n], block[:, n:]
                re, im = wave_in(s, mode)
                add_re = g_re * re + g_im * im
                add_im = g_im * re - g_re * im
                sum_re = add_re if sum_re is None else sum_re + add_re
                sum_im = add_im if sum_im is None else sum_im + add_im
                res.append(g_re * obj_re + g_im * obj_im)
                ims.append(g_im * obj_re - g_re * obj_im)
            if pair == 0:
                gpatch[0] = sum_re
                gpatch[1] = sum_im
            else:
                gpatch[0] += sum_re
                gpatch[1] += sum_im
            if s > 0:
                x = jnp.concatenate(
                    [jnp.concatenate(res, axis=1), jnp.concatenate(ims, axis=1)], axis=0
                )
                far[pair * 2 * n : (pair + 1) * 2 * n, :] = two_sided(tab, (BAND_ADJ, BAND), x)
            else:
                for k, mode in enumerate((2 * pair, 2 * pair + 1)):
                    for c, part in enumerate((res[k], ims[k])):
                        gprobe[:, :, c * modes + mode] += part.reshape(gprobe.shape[:2] + (SUBLANES, n))
        for c in range(2):
            tall = jnp.concatenate([gpatch[c], jnp.zeros((SUBLANES, n), F32)], axis=0)
            tall = pltpu.roll(tall, drop, 0)
            wide = jnp.concatenate([tall, jnp.zeros(tall.shape, F32)], axis=1)
            wide = pltpu.roll(wide, shift, 1)
            gext[s, c, pl.ds(row_tile, n + SUBLANES), pl.ds(lane_tile, 2 * n)] += wide

    @pl.when(rec == pl.num_programs(0) - 1)
    def _():
        gown[...] = gext[:, :, :, n : n + tile_cols]

        @pl.when(side[0] == 0)
        def _():
            gside[...] = gext[:, :, :, n + tile_cols :]
            gkeep[...] = gprobe[:, 0]
            gsend[...] = gprobe[:, 1]

        @pl.when(side[0] != 0)
        def _():
            gside[...] = gext[:, :, :, :n]
            gkeep[...] = gprobe[:, 1]
            gsend[...] = gprobe[:, 0]


def fields(places, side, own, above, below, beside, probe, tab, measured):
    slices, _, tile_rows, tile_cols = own.shape
    modes, _, n, _ = probe.shape
    rows = tile_rows + 2 * above.shape[2]
    records = measured.shape[0]

    def whole(shape):
        return pl.BlockSpec(shape, lambda r, *_: (0,) * len(shape))

    inputs = (own, above, below, beside, probe, tab)
    outs = [(slices, 2, rows, tile_cols), (slices, 2, rows, n)]
    halves = (n // SUBLANES // 2, 2 * modes, SUBLANES, n)
    outs.extend([halves, halves])
    return pl.pallas_call(
        field_kernel,
        out_shape=[jax.ShapeDtypeStruct(s, F32) for s in outs],
        grid_spec=pltpu.PrefetchScalarGridSpec(
            num_scalar_prefetch=2,
            grid=(records,),
            in_specs=[whole(x.shape) for x in inputs]
            + [pl.BlockSpec((1, n, n), lambda r, *_: (r, 0, 0))],
            out_specs=[whole(s) for s in outs],
            scratch_shapes=[
                pltpu.VMEM((slices, 2, rows, tile_cols + 2 * n), F32),
                pltpu.VMEM((slices, 2, rows, tile_cols + 2 * n), F32),
                pltpu.VMEM((n // SUBLANES // 2, 2, 2 * modes, SUBLANES, n), F32),
                pltpu.VMEM((slices, 2, n, n), F32),
                pltpu.VMEM((slices - 1, modes * n, 2 * n), F32),
                pltpu.VMEM((modes * n, 2 * n), F32),
                pltpu.VMEM((n, n), F32),
                pltpu.VMEM((2, n, n), F32),
            ],
        ),
        compiler_params=pltpu.CompilerParams(vmem_limit_bytes=56 << 20),
        name="fields",
    )(places, side, *inputs, measured)


def gram_kernel(*refs):
    probe, *parts, out, own = refs
    grad = parts[0][...]
    for part in parts[1:]:
        grad = grad + part[...]
    own[...] = grad
    total = None
    for i in range(probe.shape[1]):
        rows = jnp.concatenate([probe[:, i, :], own[:, i, :]], axis=0)
        one = lax.dot_general(
            rows, rows, (((1,), (1,)), ((), ())), precision=lax.Precision.HIGHEST,
            preferred_element_type=F32,
        )
        total = one if total is None else total + one
    out[...] = total


def gram(probe, parts):
    rows = 2 * probe.shape[0]
    return pl.pallas_call(
        gram_kernel,
        out_shape=[
            jax.ShapeDtypeStruct((rows, rows), F32),
            jax.ShapeDtypeStruct(probe.shape, F32),
        ],
        name="gram",
    )(probe, *parts)


def ortho_kernel(*refs, modes, scale):
    *grams, probe, grad, out = refs
    m = modes
    s = grams[0][...]
    for other in grams[1:]:
        s = s + other[...]

    def part(a, b):
        return s[a * m : (a + 1) * m, b * m : (b + 1) * m]

    def complex_part(a, b):
        re = part(2 * a, 2 * b) + part(2 * a + 1, 2 * b + 1)
        im = part(2 * a, 2 * b + 1) - part(2 * a + 1, 2 * b)
        return re, im

    pp, pg, gp, gg = (complex_part(a, b) for a, b in ((0, 0), (0, 1), (1, 0), (1, 1)))
    eye = (
        lax.broadcasted_iota(jnp.int32, (m, m), 0) == lax.broadcasted_iota(jnp.int32, (m, m), 1)
    ).astype(F32)

    def trace(x):
        return jnp.sum(jnp.sum(x * eye, axis=1, keepdims=True), axis=0, keepdims=True)

    factor = 0.5 * jnp.sqrt(trace(pp[0]) / (trace(gg[0]) + 1e-06))
    new_re = pp[0] - factor * (pg[0] + gp[0]) + factor * factor * gg[0]
    new_im = pp[1] - factor * (pg[1] + gp[1]) + factor * factor * gg[1]
    a_re = jnp.concatenate([new_re, eye], axis=1)
    a_im = jnp.concatenate([new_im, jnp.zeros((m, m), F32)], axis=1)
    row_idx = lax.broadcasted_iota(jnp.int32, (m, 1), 0)
    for j in range(m):
        inv = 1.0 / jnp.sqrt(a_re[j : j + 1, j : j + 1])
        r_re = a_re[j : j + 1, :] * inv
        r_im = a_im[j : j + 1, :] * inv
        c_re = jnp.where(row_idx > j, a_re[:, j : j + 1] * inv, 0.0)
        c_im = jnp.where(row_idx > j, a_im[:, j : j + 1] * inv, 0.0)
        at = row_idx == j
        a_re, a_im = (
            jnp.where(at, r_re, a_re - (c_re * r_re - c_im * r_im)),
            jnp.where(at, r_im, a_im - (c_re * r_im + c_im * r_re)),
        )
    inv_re = a_re[:, m:] * scale
    inv_im = a_im[:, m:] * scale
    mix = jnp.concatenate(
        [
            jnp.concatenate([inv_re, inv_im], axis=1),
            jnp.concatenate([-inv_im, inv_re], axis=1),
        ],
        axis=0,
    )
    n = probe.shape[2]
    for i in range(probe.shape[1]):
        moved = probe[:, i, :] - factor * grad[:, i, :]
        new = lax.dot_general(
            mix, moved, (((1,), (0,)), ((), ())), precision=lax.Precision.HIGHEST,
            preferred_element_type=F32,
        )
        out[:, 0, i * n : (i + 1) * n] = new[:m]
        out[:, 1, i * n : (i + 1) * n] = new[m:]


def ortho(grams, probe, grad, modes, scale):
    def body(*refs):
        ortho_kernel(*refs, modes=modes, scale=scale)

    pixels = probe.shape[1] * probe.shape[2]
    return pl.pallas_call(
        body, out_shape=jax.ShapeDtypeStruct((modes, 2, pixels), F32), name="ortho"
    )(*grams, probe, grad)


def take(array, which, dim):
    return lax.dynamic_index_in_dim(array, which, dim, keepdims=False)


def own_block(probe):
    modes, _, width, _ = probe.shape
    devices = lax.axis_size("row") * lax.axis_size("col")
    share = width // devices
    index = lax.axis_index(("row", "col"))
    block = lax.dynamic_slice_in_dim(probe, index * share, share, 2)
    return block.transpose(1, 0, 2, 3).reshape(2 * modes, share, width)


def updates(own_probe, keep, send, bottom, top, middle):
    rows, share, width = own_probe.shape
    modes = rows // 2
    row_devices = lax.axis_size("row")
    col_devices = lax.axis_size("col")
    row_idx, col_idx = lax.axis_index("row"), lax.axis_index("col")
    row_bits = [1 << b for b in range(row_devices.bit_length() - 1)]

    if share == SUBLANES and row_devices <= 8:
        received = swapped(send, "col", 1)
        pairs = (row_devices // 2, 2) + keep.shape[1:]
        keep, received = keep.reshape(pairs), received.reshape(pairs)
        low, high = row_idx % 2, row_idx // 2
        send = take(keep, 1 - low, 1) + take(received, 1 - low, 1)
        keep, received = take(keep, low, 1) + take(received, low, 1), swapped(send, "row", 1)
        parts = []
        for k in range(row_devices // 2):
            block = take(keep, high ^ k, 0) + take(received, high ^ k, 0)
            parts.append(swapped(block, "row", 2 * k) if k else block)
    else:
        even, odd = jnp.where(col_idx == 0, keep, send), jnp.where(col_idx == 0, send, keep)
        grad = jnp.stack([even, odd], axis=1).transpose(0, 1, 3, 2, 4)
        grad = grad.reshape(row_devices, col_devices, share, 2 * modes, width)
        grad = grad.transpose(1, 0, 3, 2, 4)
        grad = take(grad, col_idx, 0) + swapped(take(grad, 1 - col_idx, 0), "col", 1)
        for bit in reversed(row_bits):
            grad = grad.reshape((2, bit) + grad.shape[-3:])
            mine = (row_idx // bit) % 2
            grad = take(grad, mine, 0) + swapped(take(grad, 1 - mine, 0), "row", bit)
        parts = [grad.reshape(2 * modes, share, width)]

    parts, bottom, top = lax.optimization_barrier((parts, bottom, top))
    from_above = shifted(bottom, "row", 1)
    from_below = shifted(top, "row", -1)
    total, own_grad = gram(own_probe, parts)
    total = total + swapped(total, "col", 1)
    high_bits = row_bits[1:]
    if len(high_bits) % 2:
        total = total + swapped(total, "row", high_bits.pop())
    while high_bits:
        a, b, *high_bits = high_bits
        near, far, both = (swapped(total, "row", k) for k in (a, b, a ^ b))
        total = (total + near) + (far + both)
    grams = [total, swapped(total, "row", row_bits[0])]
    new_probe = ortho(grams, own_probe, own_grad, modes, float(width))
    object_grad = middle() + jnp.concatenate([from_above, from_below], axis=2)
    return new_probe, object_grad


def per_device(object_slices, probe, taps, measured, positions):
    width = probe.shape[-1]
    half = width // 2
    slices, _, tile_rows, tile_cols = object_slices.shape
    row_idx = lax.axis_index("row")
    col_idx = lax.axis_index("col")

    bottom_rows, later = lax.optimization_barrier(
        (object_slices[:, :, tile_rows - half :], object_slices)
    )
    above = shifted(bottom_rows, "row", 1)
    below = shifted(later[:, :, :half], "row", -1)
    tab = block_tables(taps, width)
    own_probe = own_block(probe)
    above, below, tab, own_probe = lax.optimization_barrier((above, below, tab, own_probe))
    near = (1 - col_idx) * (tile_cols - LANES)
    strip = jnp.concatenate([
        lax.dynamic_slice_in_dim(x, near, LANES, 3) for x in (above, object_slices, below)
    ], axis=2)
    beside = swapped(strip, "col", 1)

    anchor = jnp.stack([row_idx * tile_rows - half, col_idx * tile_cols - LANES])
    places = (positions - anchor[None, :]).astype(jnp.int32)
    side = col_idx.astype(jnp.int32).reshape(1)
    gown, gside, gkeep, gsend = fields(
        places, side, object_slices, above, below, beside, probe, tab, measured
    )

    got = swapped(gside, "col", 1)

    def folded(first, last):
        part = got[:, :, first:last]
        low = jnp.where(col_idx == 0, 0.0, part)
        high = jnp.where(col_idx == 0, part, 0.0)
        inner = jnp.zeros(part.shape[:3] + (tile_cols - 2 * LANES,), F32)
        return gown[:, :, first:last] + jnp.concatenate([low, inner, high], axis=3)

    bottom, top = folded(half + tile_rows, tile_rows + 2 * half), folded(0, half)
    new_probe, object_grad = updates(
        own_probe, gkeep, gsend, bottom, top, lambda: folded(half, half + tile_rows)
    )
    return (object_grad, new_probe)


def solution(mesh):
    placed = (
        P(None, None, ("groups", "row"), "col"),
        P("groups", None, None, None),
        P(),
        P(("groups", "row", "col"), None, None),
        P(("groups", "row", "col"), None),
    )
    return jax.shard_map(
        per_device,
        mesh=mesh,
        in_specs=placed,
        out_specs=(P(None, None, ("groups", "row"), "col"), P("groups", None, ("row", "col"))),
        check_vma=False,
    )
```

```python
import math

import jax
import jax.numpy as jnp
import numpy as np
from jax import lax
from jax.experimental import pallas as pl
from jax.experimental.pallas import tpu as pltpu
from jax.sharding import PartitionSpec as P

F32 = jnp.float32
BF16 = jnp.bfloat16
LANES = 128
SUBLANES = 8


def shifted(value, axis, step):
    count = lax.axis_size(axis)
    pairs = [(i, i + step) for i in range(count) if 0 <= i + step < count]
    return lax.ppermute(value, axis, pairs)


def swapped(value, axis, bit):
    count = lax.axis_size(axis)
    return lax.ppermute(value, axis, [(i, i ^ bit) for i in range(count)])


def hi_lo(value):
    high = lax.reduce_precision(value, 8, 7)
    return high.astype(BF16), (value - high).astype(BF16)


def block_tables(taps, width):
    reach = taps.shape[1] // 2
    padded = jnp.pad(taps, ((0, 0), (width, width)))
    idx = lax.iota(jnp.int32, width)
    offset = idx[None, :] - idx[:, None] + reach
    tap_idx = lax.iota(jnp.int32, taps.shape[1])
    hot = (offset[None, :, :] == tap_idx[:, None, None]).astype(F32)
    band_re = jnp.sum(hot * taps[0][:, None, None], axis=0)
    band_im = jnp.sum(hot * taps[1][:, None, None], axis=0)
    phase = np.arange(width)[:, None] * np.arange(width)[None, :] % width
    angle = 2.0 * math.pi / width * phase
    norm = 1.0 / math.sqrt(width)
    dft_re = jnp.asarray(np.cos(angle) * norm, F32)
    dft_im = jnp.asarray(-np.sin(angle) * norm, F32)

    def block(re, im):
        return jnp.concatenate(
            [jnp.concatenate([re, -im], axis=1), jnp.concatenate([im, re], axis=1)], axis=0
        )

    band, dft = block(band_re, band_im), block(dft_re, dft_im)
    parts = []
    for matrix in (band, band.T, dft, dft.T):
        parts.extend(hi_lo(matrix))
    return jnp.stack(parts)


def split(value):
    high = value.astype(BF16)
    return high, (value - high.astype(F32)).astype(BF16)


def mxu(a, b):
    return lax.dot_general(a, b, (((1,), (0,)), ((), ())), preferred_element_type=F32)


def left_product(tab, which, x):
    high, low = split(x)
    w_high, w_low = tab[2 * which], tab[2 * which + 1]
    return mxu(w_high, high) + (mxu(w_high, low) + mxu(w_low, high))


def right_product(tab, which, x):
    high, low = split(x)
    w_high, w_low = tab[2 * which], tab[2 * which + 1]
    return mxu(high, w_high) + (mxu(low, w_high) + mxu(high, w_low))


def to_rows(y):
    n = LANES
    return jnp.concatenate(
        [
            jnp.concatenate([y[:n, :n], y[n:, :n]], axis=1),
            jnp.concatenate([y[:n, n:], y[n:, n:]], axis=1),
        ],
        axis=0,
    )


def two_sided(tab, forward, x):
    base, adjoint = forward
    return right_product(tab, adjoint, to_rows(left_product(tab, base, x)))


BAND, BAND_ADJ, DFT, DFT_ADJ = range(4)


def field_kernel(
    places, side, own, above, below, beside, probe, tab, measured,
    gown, gside, gkeep, gsend, ext, gext, gprobe, patch, waves, far, intensity, gpatch,
):
    rec = pl.program_id(0)
    slices = own.shape[0]
    modes = probe.shape[0]
    n = LANES
    tile_cols = own.shape[3]
    half = above.shape[2]
    tile_rows = own.shape[2]
    weight = 1.0 / (8.0 * modes)

    @pl.when(rec == 0)
    def _():
        gext[...] = jnp.zeros(gext.shape, F32)
        gprobe[...] = jnp.zeros(gprobe.shape, F32)
        ext[:, :, :half, n : n + tile_cols] = above[...]
        ext[:, :, half : half + tile_rows, n : n + tile_cols] = own[...]
        ext[:, :, half + tile_rows :, n : n + tile_cols] = below[...]
        nothing = jnp.zeros(beside.shape, F32)

        @pl.when(side[0] == 0)
        def _():
            ext[:, :, :, :n] = nothing
            ext[:, :, :, n + tile_cols :] = beside[...]

        @pl.when(side[0] != 0)
        def _():
            ext[:, :, :, :n] = beside[...]
            ext[:, :, :, n + tile_cols :] = nothing

    row = places[rec, 0]
    col = places[rec, 1]
    lane_tile = pl.multiple_of(col // n * n, n)
    shift = col % n
    row_tile = pl.multiple_of(row // SUBLANES * SUBLANES, SUBLANES)
    drop = row % SUBLANES
    for s in range(slices):
        for c in range(2):
            window = ext[s, c, pl.ds(row_tile, n + SUBLANES), pl.ds(lane_tile, 2 * n)]
            window = pltpu.roll(window, (2 * n - shift) % (2 * n), 1)[:, :n]
            patch[s, c] = pltpu.roll(window, (n + SUBLANES - drop) % (n + SUBLANES), 0)[:n]

    def wave_in(s, mode):
        if s == 0:
            return probe[mode, 0], probe[mode, 1]
        block = waves[s - 1, mode * n : (mode + 1) * n, :]
        return block[:, :n], block[:, n:]

    intensity[...] = jnp.zeros(intensity.shape, F32)
    for s in range(slices):
        last = s + 1 == slices
        obj_re, obj_im = patch[s, 0], patch[s, 1]
        for pair in range(modes // 2):
            res, ims = [], []
            for mode in (2 * pair, 2 * pair + 1):
                re, im = wave_in(s, mode)
                res.append(re * obj_re - im * obj_im)
                ims.append(re * obj_im + im * obj_re)
            x = jnp.concatenate(
                [jnp.concatenate(res, axis=1), jnp.concatenate(ims, axis=1)], axis=0
            )
            z = two_sided(tab, (DFT, DFT_ADJ) if last else (BAND, BAND_ADJ), x)
            if last:
                far[pair * 2 * n : (pair + 1) * 2 * n, :] = z
                squares = z * z
                both = squares[:n] + squares[n:]
                intensity[...] += both[:, :n] + both[:, n:]
            else:
                waves[s, pair * 2 * n : (pair + 1) * 2 * n, :] = z

    factor = 2.0 * weight * (intensity[...] - measured[0])
    for pair in range(modes // 2):
        block = far[pair * 2 * n : (pair + 1) * 2 * n, :]
        scale = jnp.concatenate([jnp.concatenate([factor, factor], axis=1)] * 2, axis=0)
        far[pair * 2 * n : (pair + 1) * 2 * n, :] = two_sided(
            tab, (DFT_ADJ, DFT), to_rows(block * scale)
        )
    for s in reversed(range(slices)):
        obj_re, obj_im = patch[s, 0], patch[s, 1]
        for pair in range(modes // 2):
            res, ims = [], []
            sum_re = sum_im = None
            for mode in (2 * pair, 2 * pair + 1):
                block = far[mode * n : (mode + 1) * n, :]
                g_re, g_im = block[:, :n], block[:, n:]
                re, im = wave_in(s, mode)
                add_re = g_re * re + g_im * im
                add_im = g_im * re - g_re * im
                sum_re = add_re if sum_re is None else sum_re + add_re
                sum_im = add_im if sum_im is None else sum_im + add_im
                res.append(g_re * obj_re + g_im * obj_im)
                ims.append(g_im * obj_re - g_re * obj_im)
            if pair == 0:
                gpatch[0] = sum_re
                gpatch[1] = sum_im
            else:
                gpatch[0] += sum_re
                gpatch[1] += sum_im
            if s > 0:
                x = jnp.concatenate(
                    [jnp.concatenate(res, axis=1), jnp.concatenate(ims, axis=1)], axis=0
                )
                far[pair * 2 * n : (pair + 1) * 2 * n, :] = two_sided(tab, (BAND_ADJ, BAND), x)
            else:
                for k, mode in enumerate((2 * pair, 2 * pair + 1)):
                    for c, part in enumerate((res[k], ims[k])):
                        gprobe[:, :, c * modes + mode] += part.reshape(gprobe.shape[:2] + (SUBLANES, n))
        for c in range(2):
            tall = jnp.concatenate([gpatch[c], jnp.zeros((SUBLANES, n), F32)], axis=0)
            tall = pltpu.roll(tall, drop, 0)
            wide = jnp.concatenate([tall, jnp.zeros(tall.shape, F32)], axis=1)
            wide = pltpu.roll(wide, shift, 1)
            gext[s, c, pl.ds(row_tile, n + SUBLANES), pl.ds(lane_tile, 2 * n)] += wide

    @pl.when(rec == pl.num_programs(0) - 1)
    def _():
        gown[...] = gext[:, :, :, n : n + tile_cols]

        @pl.when(side[0] == 0)
        def _():
            gside[...] = gext[:, :, :, n + tile_cols :]
            gkeep[...] = gprobe[:, 0]
            gsend[...] = gprobe[:, 1]

        @pl.when(side[0] != 0)
        def _():
            gside[...] = gext[:, :, :, :n]
            gkeep[...] = gprobe[:, 1]
            gsend[...] = gprobe[:, 0]


def fields(places, side, own, above, below, beside, probe, tab, measured):
    slices, _, tile_rows, tile_cols = own.shape
    modes, _, n, _ = probe.shape
    rows = tile_rows + 2 * above.shape[2]
    records = measured.shape[0]

    def whole(shape):
        return pl.BlockSpec(shape, lambda r, *_: (0,) * len(shape))

    inputs = (own, above, below, beside, probe, tab)
    outs = [(slices, 2, rows, tile_cols), (slices, 2, rows, n)]
    halves = (n // SUBLANES // 2, 2 * modes, SUBLANES, n)
    outs.extend([halves, halves])
    return pl.pallas_call(
        field_kernel,
        out_shape=[jax.ShapeDtypeStruct(s, F32) for s in outs],
        grid_spec=pltpu.PrefetchScalarGridSpec(
            num_scalar_prefetch=2,
            grid=(records,),
            in_specs=[whole(x.shape) for x in inputs]
            + [pl.BlockSpec((1, n, n), lambda r, *_: (r, 0, 0))],
            out_specs=[whole(s) for s in outs],
            scratch_shapes=[
                pltpu.VMEM((slices, 2, rows, tile_cols + 2 * n), F32),
                pltpu.VMEM((slices, 2, rows, tile_cols + 2 * n), F32),
                pltpu.VMEM((n // SUBLANES // 2, 2, 2 * modes, SUBLANES, n), F32),
                pltpu.VMEM((slices, 2, n, n), F32),
                pltpu.VMEM((slices - 1, modes * n, 2 * n), F32),
                pltpu.VMEM((modes * n, 2 * n), F32),
                pltpu.VMEM((n, n), F32),
                pltpu.VMEM((2, n, n), F32),
            ],
        ),
        compiler_params=pltpu.CompilerParams(vmem_limit_bytes=56 << 20),
        name="fields",
    )(places, side, *inputs, measured)


def gram_kernel(*refs):
    probe, *parts, out, own = refs
    grad = parts[0][...]
    for part in parts[1:]:
        grad = grad + part[...]
    own[...] = grad
    total = None
    for i in range(probe.shape[1]):
        rows = jnp.concatenate([probe[:, i, :], own[:, i, :]], axis=0)
        one = lax.dot_general(
            rows, rows, (((1,), (1,)), ((), ())), precision=lax.Precision.HIGHEST,
            preferred_element_type=F32,
        )
        total = one if total is None else total + one
    out[...] = total


def gram(probe, parts):
    rows = 2 * probe.shape[0]
    return pl.pallas_call(
        gram_kernel,
        out_shape=[
            jax.ShapeDtypeStruct((rows, rows), F32),
            jax.ShapeDtypeStruct(probe.shape, F32),
        ],
        name="gram",
    )(probe, *parts)


def ortho_kernel(*refs, modes, scale):
    *grams, probe, grad, out = refs
    m = modes
    s = grams[0][...]
    for other in grams[1:]:
        s = s + other[...]

    def part(a, b):
        return s[a * m : (a + 1) * m, b * m : (b + 1) * m]

    def complex_part(a, b):
        re = part(2 * a, 2 * b) + part(2 * a + 1, 2 * b + 1)
        im = part(2 * a, 2 * b + 1) - part(2 * a + 1, 2 * b)
        return re, im

    pp, pg, gp, gg = (complex_part(a, b) for a, b in ((0, 0), (0, 1), (1, 0), (1, 1)))
    eye = (
        lax.broadcasted_iota(jnp.int32, (m, m), 0) == lax.broadcasted_iota(jnp.int32, (m, m), 1)
    ).astype(F32)

    def trace(x):
        return jnp.sum(jnp.sum(x * eye, axis=1, keepdims=True), axis=0, keepdims=True)

    factor = 0.5 * jnp.sqrt(trace(pp[0]) / (trace(gg[0]) + 1e-06))
    new_re = pp[0] - factor * (pg[0] + gp[0]) + factor * factor * gg[0]
    new_im = pp[1] - factor * (pg[1] + gp[1]) + factor * factor * gg[1]
    a_re = jnp.concatenate([new_re, eye], axis=1)
    a_im = jnp.concatenate([new_im, jnp.zeros((m, m), F32)], axis=1)
    row_idx = lax.broadcasted_iota(jnp.int32, (m, 1), 0)
    for j in range(m):
        inv = 1.0 / jnp.sqrt(a_re[j : j + 1, j : j + 1])
        r_re = a_re[j : j + 1, :] * inv
        r_im = a_im[j : j + 1, :] * inv
        c_re = jnp.where(row_idx > j, a_re[:, j : j + 1] * inv, 0.0)
        c_im = jnp.where(row_idx > j, a_im[:, j : j + 1] * inv, 0.0)
        at = row_idx == j
        a_re, a_im = (
            jnp.where(at, r_re, a_re - (c_re * r_re - c_im * r_im)),
            jnp.where(at, r_im, a_im - (c_re * r_im + c_im * r_re)),
        )
    inv_re = a_re[:, m:] * scale
    inv_im = a_im[:, m:] * scale
    mix = jnp.concatenate(
        [
            jnp.concatenate([inv_re, inv_im], axis=1),
            jnp.concatenate([-inv_im, inv_re], axis=1),
        ],
        axis=0,
    )
    n = probe.shape[2]
    for i in range(probe.shape[1]):
        moved = probe[:, i, :] - factor * grad[:, i, :]
        new = lax.dot_general(
            mix, moved, (((1,), (0,)), ((), ())), precision=lax.Precision.HIGHEST,
            preferred_element_type=F32,
        )
        out[:, 0, i * n : (i + 1) * n] = new[:m]
        out[:, 1, i * n : (i + 1) * n] = new[m:]


def ortho(grams, probe, grad, modes, scale):
    def body(*refs):
        ortho_kernel(*refs, modes=modes, scale=scale)

    pixels = probe.shape[1] * probe.shape[2]
    return pl.pallas_call(
        body, out_shape=jax.ShapeDtypeStruct((modes, 2, pixels), F32), name="ortho"
    )(*grams, probe, grad)


def take(array, which, dim):
    return lax.dynamic_index_in_dim(array, which, dim, keepdims=False)


def own_block(probe):
    modes, _, width, _ = probe.shape
    devices = lax.axis_size("row") * lax.axis_size("col")
    share = width // devices
    index = lax.axis_index(("row", "col"))
    block = lax.dynamic_slice_in_dim(probe, index * share, share, 2)
    return block.transpose(1, 0, 2, 3).reshape(2 * modes, share, width)


def updates(own_probe, keep, send, bottom, top, middle):
    rows, share, width = own_probe.shape
    modes = rows // 2
    row_devices = lax.axis_size("row")
    col_devices = lax.axis_size("col")
    row_idx, col_idx = lax.axis_index("row"), lax.axis_index("col")
    row_bits = [1 << b for b in range(row_devices.bit_length() - 1)]

    from_above = shifted(bottom, "row", 1)
    if share == SUBLANES and row_devices <= 8:
        received = swapped(send, "col", 1)
        parts = []
        for k in range(row_devices):
            block = take(keep, row_idx ^ k, 0) + take(received, row_idx ^ k, 0)
            parts.append(swapped(block, "row", k) if k else block)
    else:
        even, odd = jnp.where(col_idx == 0, keep, send), jnp.where(col_idx == 0, send, keep)
        grad = jnp.stack([even, odd], axis=1).transpose(0, 1, 3, 2, 4)
        grad = grad.reshape(row_devices, col_devices, share, 2 * modes, width)
        grad = grad.transpose(1, 0, 3, 2, 4)
        grad = take(grad, col_idx, 0) + swapped(take(grad, 1 - col_idx, 0), "col", 1)
        for bit in reversed(row_bits):
            grad = grad.reshape((2, bit) + grad.shape[-3:])
            mine = (row_idx // bit) % 2
            grad = take(grad, mine, 0) + swapped(take(grad, 1 - mine, 0), "row", bit)
        parts = [grad.reshape(2 * modes, share, width)]

    parts, top, from_above = lax.optimization_barrier((parts, top, from_above))
    from_below = shifted(top, "row", -1)
    total, own_grad = gram(own_probe, parts)
    total = total + swapped(total, "col", 1)
    high_bits = row_bits[1:]
    if len(high_bits) % 2:
        total = total + swapped(total, "row", high_bits.pop())
    while high_bits:
        a, b, *high_bits = high_bits
        near, far, both = (swapped(total, "row", k) for k in (a, b, a ^ b))
        total = (total + near) + (far + both)
    grams = [total, swapped(total, "row", row_bits[0])]
    object_grad = middle() + jnp.concatenate([from_above, from_below], axis=2)
    grams, object_grad = lax.optimization_barrier((grams, object_grad))
    new_probe = ortho(grams, own_probe, own_grad, modes, float(width))
    return new_probe, object_grad


def per_device(object_slices, probe, taps, measured, positions):
    width = probe.shape[-1]
    half = width // 2
    slices, _, tile_rows, tile_cols = object_slices.shape
    row_idx = lax.axis_index("row")
    col_idx = lax.axis_index("col")

    above = shifted(object_slices[:, :, tile_rows - half :], "row", 1)
    below = shifted(object_slices[:, :, :half], "row", -1)
    tab = block_tables(taps, width)
    own_probe = own_block(probe)
    above, below, tab, own_probe = lax.optimization_barrier((above, below, tab, own_probe))
    near = (1 - col_idx) * (tile_cols - LANES)
    strip = jnp.concatenate([
        lax.dynamic_slice_in_dim(x, near, LANES, 3) for x in (above, object_slices, below)
    ], axis=2)
    beside = swapped(strip, "col", 1)

    anchor = jnp.stack([row_idx * tile_rows - half, col_idx * tile_cols - LANES])
    places = (positions - anchor[None, :]).astype(jnp.int32)
    side = col_idx.astype(jnp.int32).reshape(1)
    gown, gside, gkeep, gsend = fields(
        places, side, object_slices, above, below, beside, probe, tab, measured
    )

    got = swapped(gside, "col", 1)

    def folded(first, last):
        part = got[:, :, first:last]
        low = jnp.where(col_idx == 0, 0.0, part)
        high = jnp.where(col_idx == 0, part, 0.0)
        inner = jnp.zeros(part.shape[:3] + (tile_cols - 2 * LANES,), F32)
        return gown[:, :, first:last] + jnp.concatenate([low, inner, high], axis=3)

    bottom, top = folded(half + tile_rows, tile_rows + 2 * half), folded(0, half)
    new_probe, object_grad = updates(
        own_probe, gkeep, gsend, bottom, top, lambda: folded(half, half + tile_rows)
    )
    return (object_grad, new_probe)


def solution(mesh):
    placed = (
        P(None, None, ("groups", "row"), "col"),
        P("groups", None, None, None),
        P(),
        P(("groups", "row", "col"), None, None),
        P(("groups", "row", "col"), None),
    )
    return jax.shard_map(
        per_device,
        mesh=mesh,
        in_specs=placed,
        out_specs=(P(None, None, ("groups", "row"), "col"), P("groups", None, ("row", "col"))),
        check_vma=False,
    )
```

```python
import math

import jax
import jax.numpy as jnp
import numpy as np
from jax import lax
from jax.experimental import pallas as pl
from jax.experimental.pallas import tpu as pltpu
from jax.sharding import PartitionSpec as P

F32 = jnp.float32
BF16 = jnp.bfloat16
LANES = 128
SUBLANES = 8


def shifted(value, axis, step):
    count = lax.axis_size(axis)
    pairs = [(i, i + step) for i in range(count) if 0 <= i + step < count]
    return lax.ppermute(value, axis, pairs)


def swapped(value, axis, bit):
    count = lax.axis_size(axis)
    return lax.ppermute(value, axis, [(i, i ^ bit) for i in range(count)])


def hi_lo(value):
    high = lax.reduce_precision(value, 8, 7)
    return high.astype(BF16), (value - high).astype(BF16)


def block_tables(taps, width):
    reach = taps.shape[1] // 2
    padded = jnp.pad(taps, ((0, 0), (width, width)))
    idx = lax.iota(jnp.int32, width)
    offset = idx[None, :] - idx[:, None] + reach
    tap_idx = lax.iota(jnp.int32, taps.shape[1])
    hot = (offset[None, :, :] == tap_idx[:, None, None]).astype(F32)
    band_re = jnp.sum(hot * taps[0][:, None, None], axis=0)
    band_im = jnp.sum(hot * taps[1][:, None, None], axis=0)
    phase = np.arange(width)[:, None] * np.arange(width)[None, :] % width
    angle = 2.0 * math.pi / width * phase
    norm = 1.0 / math.sqrt(width)
    dft_re = jnp.asarray(np.cos(angle) * norm, F32)
    dft_im = jnp.asarray(-np.sin(angle) * norm, F32)

    def block(re, im):
        return jnp.concatenate(
            [jnp.concatenate([re, -im], axis=1), jnp.concatenate([im, re], axis=1)], axis=0
        )

    band, dft = block(band_re, band_im), block(dft_re, dft_im)
    parts = []
    for matrix in (band, band.T, dft, dft.T):
        parts.extend(hi_lo(matrix))
    return jnp.stack(parts)


def split(value):
    high = value.astype(BF16)
    return high, (value - high.astype(F32)).astype(BF16)


def mxu(a, b):
    return lax.dot_general(a, b, (((1,), (0,)), ((), ())), preferred_element_type=F32)


def left_product(tab, which, x):
    high, low = split(x)
    w_high, w_low = tab[2 * which], tab[2 * which + 1]
    return mxu(w_high, high) + (mxu(w_high, low) + mxu(w_low, high))


def right_product(tab, which, x):
    high, low = split(x)
    w_high, w_low = tab[2 * which], tab[2 * which + 1]
    return mxu(high, w_high) + (mxu(low, w_high) + mxu(high, w_low))


def to_rows(y):
    n = LANES
    return jnp.concatenate(
        [
            jnp.concatenate([y[:n, :n], y[n:, :n]], axis=1),
            jnp.concatenate([y[:n, n:], y[n:, n:]], axis=1),
        ],
        axis=0,
    )


def two_sided(tab, forward, x):
    base, adjoint = forward
    return right_product(tab, adjoint, to_rows(left_product(tab, base, x)))


BAND, BAND_ADJ, DFT, DFT_ADJ = range(4)


def field_kernel(
    places, side, own, above, below, beside, probe, tab, measured,
    gown, gside, gkeep, gsend, ext, gext, gprobe, patch, waves, far, intensity, gpatch,
):
    rec = pl.program_id(0)
    slices = own.shape[0]
    modes = probe.shape[0]
    n = LANES
    tile_cols = own.shape[3]
    half = above.shape[2]
    tile_rows = own.shape[2]
    weight = 1.0 / (8.0 * modes)

    @pl.when(rec == 0)
    def _():
        gext[...] = jnp.zeros(gext.shape, F32)
        gprobe[...] = jnp.zeros(gprobe.shape, F32)
        ext[:, :, :half, n : n + tile_cols] = above[...]
        ext[:, :, half : half + tile_rows, n : n + tile_cols] = own[...]
        ext[:, :, half + tile_rows :, n : n + tile_cols] = below[...]
        nothing = jnp.zeros(beside.shape, F32)

        @pl.when(side[0] == 0)
        def _():
            ext[:, :, :, :n] = nothing
            ext[:, :, :, n + tile_cols :] = beside[...]

        @pl.when(side[0] != 0)
        def _():
            ext[:, :, :, :n] = beside[...]
            ext[:, :, :, n + tile_cols :] = nothing

    row = places[rec, 0]
    col = places[rec, 1]
    lane_tile = pl.multiple_of(col // n * n, n)
    shift = col % n
    row_tile = pl.multiple_of(row // SUBLANES * SUBLANES, SUBLANES)
    drop = row % SUBLANES
    for s in range(slices):
        for c in range(2):
            window = ext[s, c, pl.ds(row_tile, n + SUBLANES), pl.ds(lane_tile, 2 * n)]
            window = pltpu.roll(window, (2 * n - shift) % (2 * n), 1)[:, :n]
            patch[s, c] = pltpu.roll(window, (n + SUBLANES - drop) % (n + SUBLANES), 0)[:n]

    def wave_in(s, mode):
        if s == 0:
            return probe[mode, 0], probe[mode, 1]
        block = waves[s - 1, mode * n : (mode + 1) * n, :]
        return block[:, :n], block[:, n:]

    intensity[...] = jnp.zeros(intensity.shape, F32)
    for s in range(slices):
        last = s + 1 == slices
        obj_re, obj_im = patch[s, 0], patch[s, 1]
        for pair in range(modes // 2):
            res, ims = [], []
            for mode in (2 * pair, 2 * pair + 1):
                re, im = wave_in(s, mode)
                res.append(re * obj_re - im * obj_im)
                ims.append(re * obj_im + im * obj_re)
            x = jnp.concatenate(
                [jnp.concatenate(res, axis=1), jnp.concatenate(ims, axis=1)], axis=0
            )
            z = two_sided(tab, (DFT, DFT_ADJ) if last else (BAND, BAND_ADJ), x)
            if last:
                far[pair * 2 * n : (pair + 1) * 2 * n, :] = z
                squares = z * z
                both = squares[:n] + squares[n:]
                intensity[...] += both[:, :n] + both[:, n:]
            else:
                waves[s, pair * 2 * n : (pair + 1) * 2 * n, :] = z

    factor = 2.0 * weight * (intensity[...] - measured[0])
    for pair in range(modes // 2):
        block = far[pair * 2 * n : (pair + 1) * 2 * n, :]
        scale = jnp.concatenate([jnp.concatenate([factor, factor], axis=1)] * 2, axis=0)
        far[pair * 2 * n : (pair + 1) * 2 * n, :] = two_sided(
            tab, (DFT_ADJ, DFT), to_rows(block * scale)
        )
    for s in reversed(range(slices)):
        obj_re, obj_im = patch[s, 0], patch[s, 1]
        for pair in range(modes // 2):
            res, ims = [], []
            sum_re = sum_im = None
            for mode in (2 * pair, 2 * pair + 1):
                block = far[mode * n : (mode + 1) * n, :]
                g_re, g_im = block[:, :n], block[:, n:]
                re, im = wave_in(s, mode)
                add_re = g_re * re + g_im * im
                add_im = g_im * re - g_re * im
                sum_re = add_re if sum_re is None else sum_re + add_re
                sum_im = add_im if sum_im is None else sum_im + add_im
                res.append(g_re * obj_re + g_im * obj_im)
                ims.append(g_im * obj_re - g_re * obj_im)
            if pair == 0:
                gpatch[0] = sum_re
                gpatch[1] = sum_im
            else:
                gpatch[0] += sum_re
                gpatch[1] += sum_im
            if s > 0:
                x = jnp.concatenate(
                    [jnp.concatenate(res, axis=1), jnp.concatenate(ims, axis=1)], axis=0
                )
                far[pair * 2 * n : (pair + 1) * 2 * n, :] = two_sided(tab, (BAND_ADJ, BAND), x)
            else:
                for k, mode in enumerate((2 * pair, 2 * pair + 1)):
                    for c, part in enumerate((res[k], ims[k])):
                        gprobe[:, :, c * modes + mode] += part.reshape(gprobe.shape[:2] + (SUBLANES, n))
        for c in range(2):
            tall = jnp.concatenate([gpatch[c], jnp.zeros((SUBLANES, n), F32)], axis=0)
            tall = pltpu.roll(tall, drop, 0)
            wide = jnp.concatenate([tall, jnp.zeros(tall.shape, F32)], axis=1)
            wide = pltpu.roll(wide, shift, 1)
            gext[s, c, pl.ds(row_tile, n + SUBLANES), pl.ds(lane_tile, 2 * n)] += wide

    @pl.when(rec == pl.num_programs(0) - 1)
    def _():
        gown[...] = gext[:, :, :, n : n + tile_cols]

        @pl.when(side[0] == 0)
        def _():
            gside[...] = gext[:, :, :, n + tile_cols :]
            gkeep[...] = gprobe[:, 0]
            gsend[...] = gprobe[:, 1]

        @pl.when(side[0] != 0)
        def _():
            gside[...] = gext[:, :, :, :n]
            gkeep[...] = gprobe[:, 1]
            gsend[...] = gprobe[:, 0]


def fields(places, side, own, above, below, beside, probe, tab, measured):
    slices, _, tile_rows, tile_cols = own.shape
    modes, _, n, _ = probe.shape
    rows = tile_rows + 2 * above.shape[2]
    records = measured.shape[0]

    def whole(shape):
        return pl.BlockSpec(shape, lambda r, *_: (0,) * len(shape))

    inputs = (own, above, below, beside, probe, tab)
    outs = [(slices, 2, rows, tile_cols), (slices, 2, rows, n)]
    halves = (n // SUBLANES // 2, 2 * modes, SUBLANES, n)
    outs.extend([halves, halves])
    return pl.pallas_call(
        field_kernel,
        out_shape=[jax.ShapeDtypeStruct(s, F32) for s in outs],
        grid_spec=pltpu.PrefetchScalarGridSpec(
            num_scalar_prefetch=2,
            grid=(records,),
            in_specs=[whole(x.shape) for x in inputs]
            + [pl.BlockSpec((1, n, n), lambda r, *_: (r, 0, 0))],
            out_specs=[whole(s) for s in outs],
            scratch_shapes=[
                pltpu.VMEM((slices, 2, rows, tile_cols + 2 * n), F32),
                pltpu.VMEM((slices, 2, rows, tile_cols + 2 * n), F32),
                pltpu.VMEM((n // SUBLANES // 2, 2, 2 * modes, SUBLANES, n), F32),
                pltpu.VMEM((slices, 2, n, n), F32),
                pltpu.VMEM((slices - 1, modes * n, 2 * n), F32),
                pltpu.VMEM((modes * n, 2 * n), F32),
                pltpu.VMEM((n, n), F32),
                pltpu.VMEM((2, n, n), F32),
            ],
        ),
        compiler_params=pltpu.CompilerParams(vmem_limit_bytes=56 << 20),
        name="fields",
    )(places, side, *inputs, measured)


def gram_kernel(*refs):
    probe, *parts, out, own = refs
    grad = parts[0][...]
    for part in parts[1:]:
        grad = grad + part[...]
    own[...] = grad
    total = None
    for i in range(probe.shape[1]):
        rows = jnp.concatenate([probe[:, i, :], own[:, i, :]], axis=0)
        one = lax.dot_general(
            rows, rows, (((1,), (1,)), ((), ())), precision=lax.Precision.HIGHEST,
            preferred_element_type=F32,
        )
        total = one if total is None else total + one
    out[...] = total


def gram(probe, parts):
    rows = 2 * probe.shape[0]
    return pl.pallas_call(
        gram_kernel,
        out_shape=[
            jax.ShapeDtypeStruct((rows, rows), F32),
            jax.ShapeDtypeStruct(probe.shape, F32),
        ],
        name="gram",
    )(probe, *parts)


def ortho_update(grams, probe, grad, out, modes, scale):
    m = modes
    s = grams[0][...]
    for other in grams[1:]:
        s = s + other[...]

    def part(a, b):
        return s[a * m : (a + 1) * m, b * m : (b + 1) * m]

    def complex_part(a, b):
        re = part(2 * a, 2 * b) + part(2 * a + 1, 2 * b + 1)
        im = part(2 * a, 2 * b + 1) - part(2 * a + 1, 2 * b)
        return re, im

    pp, pg, gp, gg = (complex_part(a, b) for a, b in ((0, 0), (0, 1), (1, 0), (1, 1)))
    eye = (
        lax.broadcasted_iota(jnp.int32, (m, m), 0) == lax.broadcasted_iota(jnp.int32, (m, m), 1)
    ).astype(F32)

    def trace(x):
        return jnp.sum(jnp.sum(x * eye, axis=1, keepdims=True), axis=0, keepdims=True)

    factor = 0.5 * jnp.sqrt(trace(pp[0]) / (trace(gg[0]) + 1e-06))
    new_re = pp[0] - factor * (pg[0] + gp[0]) + factor * factor * gg[0]
    new_im = pp[1] - factor * (pg[1] + gp[1]) + factor * factor * gg[1]
    a_re = jnp.concatenate([new_re, eye], axis=1)
    a_im = jnp.concatenate([new_im, jnp.zeros((m, m), F32)], axis=1)
    row_idx = lax.broadcasted_iota(jnp.int32, (m, 1), 0)
    for j in range(m):
        inv = 1.0 / jnp.sqrt(a_re[j : j + 1, j : j + 1])
        r_re = a_re[j : j + 1, :] * inv
        r_im = a_im[j : j + 1, :] * inv
        c_re = jnp.where(row_idx > j, a_re[:, j : j + 1] * inv, 0.0)
        c_im = jnp.where(row_idx > j, a_im[:, j : j + 1] * inv, 0.0)
        at = row_idx == j
        a_re, a_im = (
            jnp.where(at, r_re, a_re - (c_re * r_re - c_im * r_im)),
            jnp.where(at, r_im, a_im - (c_re * r_im + c_im * r_re)),
        )
    inv_re = a_re[:, m:] * scale
    inv_im = a_im[:, m:] * scale
    mix = jnp.concatenate(
        [
            jnp.concatenate([inv_re, inv_im], axis=1),
            jnp.concatenate([-inv_im, inv_re], axis=1),
        ],
        axis=0,
    )
    n = probe.shape[2]
    for i in range(probe.shape[1]):
        moved = probe[:, i, :] - factor * grad[:, i, :]
        new = lax.dot_general(
            mix, moved, (((1,), (0,)), ((), ())), precision=lax.Precision.HIGHEST,
            preferred_element_type=F32,
        )
        out[:, 0, i * n : (i + 1) * n] = new[:m]
        out[:, 1, i * n : (i + 1) * n] = new[m:]


def finish(side, grams, probe, grad, gown, beside, above, below, modes, scale):
    slices, _, rows, tile_cols = gown.shape
    half = above.shape[2]
    tile_rows = rows - 2 * half
    n = beside.shape[3]
    pixels = probe.shape[1] * probe.shape[2]
    count = len(grams)

    def body(side_ref, *refs):
        gram_refs, rest = refs[:count], refs[count:]
        probe_ref, grad_ref, own_ref, beside_ref, above_ref, below_ref, new_ref, out = rest
        near = pl.multiple_of(jnp.where(side_ref[0] == 0, tile_cols - n, 0), n)
        out[...] = own_ref[:, :, half : half + tile_rows]
        out[:, :, :, pl.ds(near, n)] += beside_ref[:, :, half : half + tile_rows]
        out[:, :, :half] += above_ref[...]
        out[:, :, tile_rows - half :] += below_ref[...]

        @pl.when(pl.program_id(0) == 0)
        def _():
            ortho_update(gram_refs, probe_ref, grad_ref, new_ref, modes, scale)

    def whole(shape):
        return pl.BlockSpec(shape, lambda s, *_: (0,) * len(shape))

    def one_slice(shape):
        return pl.BlockSpec((1,) + shape[1:], lambda s, *_: (s,) + (0,) * (len(shape) - 1))

    outs = [(modes, 2, pixels), (slices, 2, tile_rows, tile_cols)]
    small, large = (*grams, probe, grad), (gown, beside, above, below)
    return pl.pallas_call(
        body,
        out_shape=[jax.ShapeDtypeStruct(s, F32) for s in outs],
        grid_spec=pltpu.PrefetchScalarGridSpec(
            num_scalar_prefetch=1,
            grid=(slices,),
            in_specs=[whole(x.shape) for x in small] + [one_slice(x.shape) for x in large],
            out_specs=[whole(outs[0]), one_slice(outs[1])],
        ),
        name="finish",
    )(side, *small, *large)


def take(array, which, dim):
    return lax.dynamic_index_in_dim(array, which, dim, keepdims=False)


def own_block(probe):
    modes, _, width, _ = probe.shape
    devices = lax.axis_size("row") * lax.axis_size("col")
    share = width // devices
    index = lax.axis_index(("row", "col"))
    block = lax.dynamic_slice_in_dim(probe, index * share, share, 2)
    return block.transpose(1, 0, 2, 3).reshape(2 * modes, share, width)


def updates(own_probe, keep, send, bottom, top, side, gown, beside):
    rows, share, width = own_probe.shape
    modes = rows // 2
    row_devices = lax.axis_size("row")
    col_devices = lax.axis_size("col")
    row_idx, col_idx = lax.axis_index("row"), lax.axis_index("col")
    row_bits = [1 << b for b in range(row_devices.bit_length() - 1)]

    if share == SUBLANES and row_devices <= 8:
        received = swapped(send, "col", 1)
        parts = []
        for k in range(row_devices):
            block = take(keep, row_idx ^ k, 0) + take(received, row_idx ^ k, 0)
            parts.append(swapped(block, "row", k) if k else block)
    else:
        even, odd = jnp.where(col_idx == 0, keep, send), jnp.where(col_idx == 0, send, keep)
        grad = jnp.stack([even, odd], axis=1).transpose(0, 1, 3, 2, 4)
        grad = grad.reshape(row_devices, col_devices, share, 2 * modes, width)
        grad = grad.transpose(1, 0, 3, 2, 4)
        grad = take(grad, col_idx, 0) + swapped(take(grad, 1 - col_idx, 0), "col", 1)
        for bit in reversed(row_bits):
            grad = grad.reshape((2, bit) + grad.shape[-3:])
            mine = (row_idx // bit) % 2
            grad = take(grad, mine, 0) + swapped(take(grad, 1 - mine, 0), "row", bit)
        parts = [grad.reshape(2 * modes, share, width)]

    parts, bottom, top = lax.optimization_barrier((parts, bottom, top))
    from_above = shifted(bottom, "row", 1)
    from_below = shifted(top, "row", -1)
    total, own_grad = gram(own_probe, parts)
    total = total + swapped(total, "col", 1)
    high_bits = row_bits[1:]
    if len(high_bits) % 2:
        total = total + swapped(total, "row", high_bits.pop())
    while high_bits:
        a, b, *high_bits = high_bits
        near, far, both = (swapped(total, "row", k) for k in (a, b, a ^ b))
        total = (total + near) + (far + both)
    grams = [total, swapped(total, "row", row_bits[0])]
    return finish(
        side, grams, own_probe, own_grad, gown, beside, from_above, from_below, modes, float(width)
    )


def per_device(object_slices, probe, taps, measured, positions):
    width = probe.shape[-1]
    half = width // 2
    slices, _, tile_rows, tile_cols = object_slices.shape
    row_idx = lax.axis_index("row")
    col_idx = lax.axis_index("col")

    above = shifted(object_slices[:, :, tile_rows - half :], "row", 1)
    below = shifted(object_slices[:, :, :half], "row", -1)
    tab = block_tables(taps, width)
    own_probe = own_block(probe)
    above, below, tab, own_probe = lax.optimization_barrier((above, below, tab, own_probe))
    near = (1 - col_idx) * (tile_cols - LANES)
    strip = jnp.concatenate([
        lax.dynamic_slice_in_dim(x, near, LANES, 3) for x in (above, object_slices, below)
    ], axis=2)
    beside = swapped(strip, "col", 1)

    anchor = jnp.stack([row_idx * tile_rows - half, col_idx * tile_cols - LANES])
    places = (positions - anchor[None, :]).astype(jnp.int32)
    side = col_idx.astype(jnp.int32).reshape(1)
    gown, gside, gkeep, gsend = fields(
        places, side, object_slices, above, below, beside, probe, tab, measured
    )

    got = swapped(gside, "col", 1)

    def folded(first, last):
        part = got[:, :, first:last]
        low = jnp.where(col_idx == 0, 0.0, part)
        high = jnp.where(col_idx == 0, part, 0.0)
        inner = jnp.zeros(part.shape[:3] + (tile_cols - 2 * LANES,), F32)
        return gown[:, :, first:last] + jnp.concatenate([low, inner, high], axis=3)

    bottom, top = folded(half + tile_rows, tile_rows + 2 * half), folded(0, half)
    new_probe, object_grad = updates(
        own_probe, gkeep, gsend, bottom, top, side, gown, got
    )
    return (object_grad, new_probe)


def solution(mesh):
    placed = (
        P(None, None, ("groups", "row"), "col"),
        P("groups", None, None, None),
        P(),
        P(("groups", "row", "col"), None, None),
        P(("groups", "row", "col"), None),
    )
    return jax.shard_map(
        per_device,
        mesh=mesh,
        in_specs=placed,
        out_specs=(P(None, None, ("groups", "row"), "col"), P("groups", None, ("row", "col"))),
        check_vma=False,
    )
```

```python
import math

import jax
import jax.numpy as jnp
import numpy as np
from jax import lax
from jax.experimental import pallas as pl
from jax.experimental.pallas import tpu as pltpu
from jax.sharding import PartitionSpec as P

F32 = jnp.float32
BF16 = jnp.bfloat16
LANES = 128
SUBLANES = 8


def shifted(value, axis, step):
    count = lax.axis_size(axis)
    pairs = [(i, i + step) for i in range(count) if 0 <= i + step < count]
    return lax.ppermute(value, axis, pairs)


def swapped(value, axis, bit):
    count = lax.axis_size(axis)
    return lax.ppermute(value, axis, [(i, i ^ bit) for i in range(count)])


def hi_lo(value):
    high = lax.reduce_precision(value, 8, 7)
    return high.astype(BF16), (value - high).astype(BF16)


def block_tables(taps, width):
    reach = taps.shape[1] // 2
    padded = jnp.pad(taps, ((0, 0), (width, width)))
    idx = lax.iota(jnp.int32, width)
    offset = idx[None, :] - idx[:, None] + reach
    tap_idx = lax.iota(jnp.int32, taps.shape[1])
    hot = (offset[None, :, :] == tap_idx[:, None, None]).astype(F32)
    band_re = jnp.sum(hot * taps[0][:, None, None], axis=0)
    band_im = jnp.sum(hot * taps[1][:, None, None], axis=0)
    phase = np.arange(width)[:, None] * np.arange(width)[None, :] % width
    angle = 2.0 * math.pi / width * phase
    norm = 1.0 / math.sqrt(width)
    dft_re = jnp.asarray(np.cos(angle) * norm, F32)
    dft_im = jnp.asarray(-np.sin(angle) * norm, F32)

    def block(re, im):
        return jnp.concatenate(
            [jnp.concatenate([re, -im], axis=1), jnp.concatenate([im, re], axis=1)], axis=0
        )

    band, dft = block(band_re, band_im), block(dft_re, dft_im)
    parts = []
    for matrix in (band, band.T, dft, dft.T):
        parts.extend(hi_lo(matrix))
    return jnp.stack(parts)


def split(value):
    high = value.astype(BF16)
    return high, (value - high.astype(F32)).astype(BF16)


def mxu(a, b):
    return lax.dot_general(a, b, (((1,), (0,)), ((), ())), preferred_element_type=F32)


def left_product(tab, which, x):
    high, low = split(x)
    w_high, w_low = tab[2 * which], tab[2 * which + 1]
    return mxu(w_high, high) + (mxu(w_high, low) + mxu(w_low, high))


def right_product(tab, which, x):
    high, low = split(x)
    w_high, w_low = tab[2 * which], tab[2 * which + 1]
    return mxu(high, w_high) + (mxu(low, w_high) + mxu(high, w_low))


def to_rows(y):
    n = LANES
    return jnp.concatenate(
        [
            jnp.concatenate([y[:n, :n], y[n:, :n]], axis=1),
            jnp.concatenate([y[:n, n:], y[n:, n:]], axis=1),
        ],
        axis=0,
    )


def two_sided(tab, forward, x):
    base, adjoint = forward
    return right_product(tab, adjoint, to_rows(left_product(tab, base, x)))


BAND, BAND_ADJ, DFT, DFT_ADJ = range(4)


def field_kernel(
    places, side, own, above, below, beside, probe, tab, measured,
    gown, gside, gkeep, gsend, ext, gext, gprobe, patch, waves, far, intensity, gpatch,
):
    rec = pl.program_id(0)
    slices = own.shape[0]
    modes = probe.shape[0]
    n = LANES
    tile_cols = own.shape[3]
    half = above.shape[2]
    tile_rows = own.shape[2]
    weight = 1.0 / (8.0 * modes)

    @pl.when(rec == 0)
    def _():
        gext[...] = jnp.zeros(gext.shape, F32)
        gprobe[...] = jnp.zeros(gprobe.shape, F32)
        ext[:, :, :half, n : n + tile_cols] = above[...]
        ext[:, :, half : half + tile_rows, n : n + tile_cols] = own[...]
        ext[:, :, half + tile_rows :, n : n + tile_cols] = below[...]
        nothing = jnp.zeros(beside.shape, F32)

        @pl.when(side[0] == 0)
        def _():
            ext[:, :, :, :n] = nothing
            ext[:, :, :, n + tile_cols :] = beside[...]

        @pl.when(side[0] != 0)
        def _():
            ext[:, :, :, :n] = beside[...]
            ext[:, :, :, n + tile_cols :] = nothing

    row = places[rec, 0]
    col = places[rec, 1]
    lane_tile = pl.multiple_of(col // n * n, n)
    shift = col % n
    row_tile = pl.multiple_of(row // SUBLANES * SUBLANES, SUBLANES)
    drop = row % SUBLANES
    for s in range(slices):
        for c in range(2):
            window = ext[s, c, pl.ds(row_tile, n + SUBLANES), pl.ds(lane_tile, 2 * n)]
            window = pltpu.roll(window, (2 * n - shift) % (2 * n), 1)[:, :n]
            patch[s, c] = pltpu.roll(window, (n + SUBLANES - drop) % (n + SUBLANES), 0)[:n]

    def wave_in(s, mode):
        if s == 0:
            return probe[mode, 0], probe[mode, 1]
        block = waves[s - 1, mode * n : (mode + 1) * n, :]
        return block[:, :n], block[:, n:]

    intensity[...] = jnp.zeros(intensity.shape, F32)
    for s in range(slices):
        last = s + 1 == slices
        obj_re, obj_im = patch[s, 0], patch[s, 1]
        for pair in range(modes // 2):
            res, ims = [], []
            for mode in (2 * pair, 2 * pair + 1):
                re, im = wave_in(s, mode)
                res.append(re * obj_re - im * obj_im)
                ims.append(re * obj_im + im * obj_re)
            x = jnp.concatenate(
                [jnp.concatenate(res, axis=1), jnp.concatenate(ims, axis=1)], axis=0
            )
            z = two_sided(tab, (DFT, DFT_ADJ) if last else (BAND, BAND_ADJ), x)
            if last:
                far[pair * 2 * n : (pair + 1) * 2 * n, :] = z
                squares = z * z
                both = squares[:n] + squares[n:]
                intensity[...] += both[:, :n] + both[:, n:]
            else:
                waves[s, pair * 2 * n : (pair + 1) * 2 * n, :] = z

    factor = 2.0 * weight * (intensity[...] - measured[0])
    for pair in range(modes // 2):
        block = far[pair * 2 * n : (pair + 1) * 2 * n, :]
        scale = jnp.concatenate([jnp.concatenate([factor, factor], axis=1)] * 2, axis=0)
        far[pair * 2 * n : (pair + 1) * 2 * n, :] = two_sided(
            tab, (DFT_ADJ, DFT), to_rows(block * scale)
        )
    for s in reversed(range(slices)):
        obj_re, obj_im = patch[s, 0], patch[s, 1]
        for pair in range(modes // 2):
            res, ims = [], []
            sum_re = sum_im = None
            for mode in (2 * pair, 2 * pair + 1):
                block = far[mode * n : (mode + 1) * n, :]
                g_re, g_im = block[:, :n], block[:, n:]
                re, im = wave_in(s, mode)
                add_re = g_re * re + g_im * im
                add_im = g_im * re - g_re * im
                sum_re = add_re if sum_re is None else sum_re + add_re
                sum_im = add_im if sum_im is None else sum_im + add_im
                res.append(g_re * obj_re + g_im * obj_im)
                ims.append(g_im * obj_re - g_re * obj_im)
            if pair == 0:
                gpatch[0] = sum_re
                gpatch[1] = sum_im
            else:
                gpatch[0] += sum_re
                gpatch[1] += sum_im
            if s > 0:
                x = jnp.concatenate(
                    [jnp.concatenate(res, axis=1), jnp.concatenate(ims, axis=1)], axis=0
                )
                far[pair * 2 * n : (pair + 1) * 2 * n, :] = two_sided(tab, (BAND_ADJ, BAND), x)
            else:
                for k, mode in enumerate((2 * pair, 2 * pair + 1)):
                    for c, part in enumerate((res[k], ims[k])):
                        gprobe[:, :, c * modes + mode] += part.reshape(gprobe.shape[:2] + (SUBLANES, n))
        for c in range(2):
            tall = jnp.concatenate([gpatch[c], jnp.zeros((SUBLANES, n), F32)], axis=0)
            tall = pltpu.roll(tall, drop, 0)
            wide = jnp.concatenate([tall, jnp.zeros(tall.shape, F32)], axis=1)
            wide = pltpu.roll(wide, shift, 1)
            gext[s, c, pl.ds(row_tile, n + SUBLANES), pl.ds(lane_tile, 2 * n)] += wide

    @pl.when(rec == pl.num_programs(0) - 1)
    def _():
        gown[...] = gext[:, :, :, n : n + tile_cols]

        @pl.when(side[0] == 0)
        def _():
            gside[...] = gext[:, :, :, n + tile_cols :]
            gkeep[...] = gprobe[:, 0]
            gsend[...] = gprobe[:, 1]

        @pl.when(side[0] != 0)
        def _():
            gside[...] = gext[:, :, :, :n]
            gkeep[...] = gprobe[:, 1]
            gsend[...] = gprobe[:, 0]


def fields(places, side, own, above, below, beside, probe, tab, measured):
    slices, _, tile_rows, tile_cols = own.shape
    modes, _, n, _ = probe.shape
    rows = tile_rows + 2 * above.shape[2]
    records = measured.shape[0]

    def whole(shape):
        return pl.BlockSpec(shape, lambda r, *_: (0,) * len(shape))

    inputs = (own, above, below, beside, probe, tab)
    outs = [(slices, 2, rows, tile_cols), (slices, 2, rows, n)]
    halves = (n // SUBLANES // 2, 2 * modes, SUBLANES, n)
    outs.extend([halves, halves])
    return pl.pallas_call(
        field_kernel,
        out_shape=[jax.ShapeDtypeStruct(s, F32) for s in outs],
        grid_spec=pltpu.PrefetchScalarGridSpec(
            num_scalar_prefetch=2,
            grid=(records,),
            in_specs=[whole(x.shape) for x in inputs]
            + [pl.BlockSpec((1, n, n), lambda r, *_: (r, 0, 0))],
            out_specs=[whole(s) for s in outs],
            scratch_shapes=[
                pltpu.VMEM((slices, 2, rows, tile_cols + 2 * n), F32),
                pltpu.VMEM((slices, 2, rows, tile_cols + 2 * n), F32),
                pltpu.VMEM((n // SUBLANES // 2, 2, 2 * modes, SUBLANES, n), F32),
                pltpu.VMEM((slices, 2, n, n), F32),
                pltpu.VMEM((slices - 1, modes * n, 2 * n), F32),
                pltpu.VMEM((modes * n, 2 * n), F32),
                pltpu.VMEM((n, n), F32),
                pltpu.VMEM((2, n, n), F32),
            ],
        ),
        compiler_params=pltpu.CompilerParams(vmem_limit_bytes=56 << 20),
        name="fields",
    )(places, side, *inputs, measured)


def gram_kernel(*refs):
    probe, *parts, out, own = refs
    grad = parts[0][...]
    for part in parts[1:]:
        grad = grad + part[...]
    own[...] = grad
    total = None
    for i in range(probe.shape[1]):
        rows = jnp.concatenate([probe[:, i, :], own[:, i, :]], axis=0)
        one = lax.dot_general(
            rows, rows, (((1,), (1,)), ((), ())), precision=lax.Precision.HIGHEST,
            preferred_element_type=F32,
        )
        total = one if total is None else total + one
    out[...] = total


def gram(probe, parts):
    rows = 2 * probe.shape[0]
    return pl.pallas_call(
        gram_kernel,
        out_shape=[
            jax.ShapeDtypeStruct((rows, rows), F32),
            jax.ShapeDtypeStruct(probe.shape, F32),
        ],
        name="gram",
    )(probe, *parts)


def ortho_kernel(*refs, modes, scale):
    *grams, probe, grad, out = refs
    m = modes
    s = grams[0][...]
    for other in grams[1:]:
        s = s + other[...]

    def part(a, b):
        return s[a * m : (a + 1) * m, b * m : (b + 1) * m]

    def complex_part(a, b):
        re = part(2 * a, 2 * b) + part(2 * a + 1, 2 * b + 1)
        im = part(2 * a, 2 * b + 1) - part(2 * a + 1, 2 * b)
        return re, im

    pp, pg, gp, gg = (complex_part(a, b) for a, b in ((0, 0), (0, 1), (1, 0), (1, 1)))
    eye = (
        lax.broadcasted_iota(jnp.int32, (m, m), 0) == lax.broadcasted_iota(jnp.int32, (m, m), 1)
    ).astype(F32)

    def trace(x):
        return jnp.sum(jnp.sum(x * eye, axis=1, keepdims=True), axis=0, keepdims=True)

    factor = 0.5 * jnp.sqrt(trace(pp[0]) / (trace(gg[0]) + 1e-06))
    new_re = pp[0] - factor * (pg[0] + gp[0]) + factor * factor * gg[0]
    new_im = pp[1] - factor * (pg[1] + gp[1]) + factor * factor * gg[1]
    a_re = jnp.concatenate([new_re, eye], axis=1)
    a_im = jnp.concatenate([new_im, jnp.zeros((m, m), F32)], axis=1)
    row_idx = lax.broadcasted_iota(jnp.int32, (m, 1), 0)
    for j in range(m):
        inv = 1.0 / jnp.sqrt(a_re[j : j + 1, j : j + 1])
        r_re = a_re[j : j + 1, :] * inv
        r_im = a_im[j : j + 1, :] * inv
        c_re = jnp.where(row_idx > j, a_re[:, j : j + 1] * inv, 0.0)
        c_im = jnp.where(row_idx > j, a_im[:, j : j + 1] * inv, 0.0)
        at = row_idx == j
        a_re, a_im = (
            jnp.where(at, r_re, a_re - (c_re * r_re - c_im * r_im)),
            jnp.where(at, r_im, a_im - (c_re * r_im + c_im * r_re)),
        )
    inv_re = a_re[:, m:] * scale
    inv_im = a_im[:, m:] * scale
    mix = jnp.concatenate(
        [
            jnp.concatenate([inv_re, inv_im], axis=1),
            jnp.concatenate([-inv_im, inv_re], axis=1),
        ],
        axis=0,
    )
    n = probe.shape[2]
    for i in range(probe.shape[1]):
        moved = probe[:, i, :] - factor * grad[:, i, :]
        new = lax.dot_general(
            mix, moved, (((1,), (0,)), ((), ())), precision=lax.Precision.HIGHEST,
            preferred_element_type=F32,
        )
        out[:, 0, i * n : (i + 1) * n] = new[:m]
        out[:, 1, i * n : (i + 1) * n] = new[m:]


def ortho(grams, probe, grad, modes, scale):
    def body(*refs):
        ortho_kernel(*refs, modes=modes, scale=scale)

    pixels = probe.shape[1] * probe.shape[2]
    return pl.pallas_call(
        body, out_shape=jax.ShapeDtypeStruct((modes, 2, pixels), F32), name="ortho"
    )(*grams, probe, grad)


def take(array, which, dim):
    return lax.dynamic_index_in_dim(array, which, dim, keepdims=False)


def own_block(probe):
    modes, _, width, _ = probe.shape
    devices = lax.axis_size("row") * lax.axis_size("col")
    share = width // devices
    index = lax.axis_index(("row", "col"))
    block = lax.dynamic_slice_in_dim(probe, index * share, share, 2)
    return block.transpose(1, 0, 2, 3).reshape(2 * modes, share, width)


def updates(own_probe, keep, send, bottom, top, middle):
    rows, share, width = own_probe.shape
    modes = rows // 2
    row_devices = lax.axis_size("row")
    col_devices = lax.axis_size("col")
    row_idx, col_idx = lax.axis_index("row"), lax.axis_index("col")
    row_bits = [1 << b for b in range(row_devices.bit_length() - 1)]

    if share == SUBLANES and row_devices <= 8:
        received = swapped(send, "col", 1)
        parts = []
        for k in range(row_devices):
            block = take(keep, row_idx ^ k, 0) + take(received, row_idx ^ k, 0)
            parts.append(swapped(block, "row", k) if k else block)
    else:
        even, odd = jnp.where(col_idx == 0, keep, send), jnp.where(col_idx == 0, send, keep)
        grad = jnp.stack([even, odd], axis=1).transpose(0, 1, 3, 2, 4)
        grad = grad.reshape(row_devices, col_devices, share, 2 * modes, width)
        grad = grad.transpose(1, 0, 3, 2, 4)
        grad = take(grad, col_idx, 0) + swapped(take(grad, 1 - col_idx, 0), "col", 1)
        for bit in reversed(row_bits):
            grad = grad.reshape((2, bit) + grad.shape[-3:])
            mine = (row_idx // bit) % 2
            grad = take(grad, mine, 0) + swapped(take(grad, 1 - mine, 0), "row", bit)
        parts = [grad.reshape(2 * modes, share, width)]

    parts, bottom, top = lax.optimization_barrier((parts, bottom, top))
    from_above = shifted(bottom, "row", 1)
    from_below = shifted(top, "row", -1)
    total, own_grad = gram(own_probe, parts)
    total = total + swapped(total, "col", 1)
    high_bits = row_bits[1:]
    if len(high_bits) % 2:
        total = total + swapped(total, "row", high_bits.pop())
    while high_bits:
        a, b, *high_bits = high_bits
        near, far, both = (swapped(total, "row", k) for k in (a, b, a ^ b))
        total = (total + near) + (far + both)
    grams = [total, swapped(total, "row", row_bits[0])]
    new_probe = ortho(grams, own_probe, own_grad, modes, float(width))
    object_grad = middle() + jnp.concatenate([from_above, from_below], axis=2)
    return new_probe, object_grad


def per_device(object_slices, probe, taps, measured, positions):
    width = probe.shape[-1]
    half = width // 2
    slices, _, tile_rows, tile_cols = object_slices.shape
    row_idx = lax.axis_index("row")
    col_idx = lax.axis_index("col")

    above = shifted(object_slices[:, :, tile_rows - half :], "row", 1)
    below = shifted(object_slices[:, :, :half], "row", -1)
    tab = block_tables(taps, width)
    own_probe = own_block(probe)
    above, below, tab, own_probe = lax.optimization_barrier((above, below, tab, own_probe))
    near = (1 - col_idx) * (tile_cols - LANES)
    strip = jnp.concatenate([
        lax.dynamic_slice_in_dim(x, near, LANES, 3) for x in (above, object_slices, below)
    ], axis=2)
    beside = swapped(strip, "col", 1)

    anchor = jnp.stack([row_idx * tile_rows - half, col_idx * tile_cols - LANES])
    places = (positions - anchor[None, :]).astype(jnp.int32)
    side = col_idx.astype(jnp.int32).reshape(1)
    gown, gside, gkeep, gsend = fields(
        places, side, object_slices, above, below, beside, probe, tab, measured
    )

    got = swapped(gside, "col", 1)

    def folded(first, last):
        part = got[:, :, first:last]
        low = jnp.where(col_idx == 0, 0.0, part)
        high = jnp.where(col_idx == 0, part, 0.0)
        inner = jnp.zeros(part.shape[:3] + (tile_cols - 2 * LANES,), F32)
        return gown[:, :, first:last] + jnp.concatenate([low, inner, high], axis=3)

    bottom, top = folded(half + tile_rows, tile_rows + 2 * half), folded(0, half)
    new_probe, object_grad = updates(
        own_probe, gkeep, gsend, bottom, top, lambda: folded(half, half + tile_rows)
    )
    return (object_grad, new_probe)


def solution(mesh):
    placed = (
        P(None, None, ("groups", "row"), "col"),
        P("groups", None, None, None),
        P(),
        P(("groups", "row", "col"), None, None),
        P(("groups", "row", "col"), None),
    )
    return jax.shard_map(
        per_device,
        mesh=mesh,
        in_specs=placed,
        out_specs=(P(None, None, ("groups", "row"), "col"), P("groups", None, ("row", "col"))),
        check_vma=False,
    )
```

```python
import math

import jax
import jax.numpy as jnp
import numpy as np
from jax import lax
from jax.experimental import pallas as pl
from jax.experimental.pallas import tpu as pltpu
from jax.sharding import PartitionSpec as P

F32 = jnp.float32
BF16 = jnp.bfloat16
LANES = 128
SUBLANES = 8


def shifted(value, axis, step):
    count = lax.axis_size(axis)
    pairs = [(i, i + step) for i in range(count) if 0 <= i + step < count]
    return lax.ppermute(value, axis, pairs)


def swapped(value, axis, bit):
    count = lax.axis_size(axis)
    return lax.ppermute(value, axis, [(i, i ^ bit) for i in range(count)])


def hi_lo(value):
    high = lax.reduce_precision(value, 8, 7)
    return high.astype(BF16), (value - high).astype(BF16)


def block_tables(taps, width):
    reach = taps.shape[1] // 2
    padded = jnp.pad(taps, ((0, 0), (width, width)))
    idx = lax.iota(jnp.int32, width)
    offset = idx[None, :] - idx[:, None] + reach
    tap_idx = lax.iota(jnp.int32, taps.shape[1])
    hot = (offset[None, :, :] == tap_idx[:, None, None]).astype(F32)
    band_re = jnp.sum(hot * taps[0][:, None, None], axis=0)
    band_im = jnp.sum(hot * taps[1][:, None, None], axis=0)
    phase = np.arange(width)[:, None] * np.arange(width)[None, :] % width
    angle = 2.0 * math.pi / width * phase
    norm = 1.0 / math.sqrt(width)
    dft_re = jnp.asarray(np.cos(angle) * norm, F32)
    dft_im = jnp.asarray(-np.sin(angle) * norm, F32)

    def block(re, im):
        return jnp.concatenate(
            [jnp.concatenate([re, -im], axis=1), jnp.concatenate([im, re], axis=1)], axis=0
        )

    band, dft = block(band_re, band_im), block(dft_re, dft_im)
    parts = []
    for matrix in (band, band.T, dft, dft.T):
        parts.extend(hi_lo(matrix))
    return jnp.stack(parts)


def split(value):
    high = value.astype(BF16)
    return high, (value - high.astype(F32)).astype(BF16)


def mxu(a, b):
    return lax.dot_general(a, b, (((1,), (0,)), ((), ())), preferred_element_type=F32)


def left_product(tab, which, x):
    high, low = split(x)
    w_high, w_low = tab[2 * which], tab[2 * which + 1]
    return mxu(w_high, high) + (mxu(w_high, low) + mxu(w_low, high))


def right_product(tab, which, x):
    high, low = split(x)
    w_high, w_low = tab[2 * which], tab[2 * which + 1]
    return mxu(high, w_high) + (mxu(low, w_high) + mxu(high, w_low))


def to_rows(y):
    n = LANES
    return jnp.concatenate(
        [
            jnp.concatenate([y[:n, :n], y[n:, :n]], axis=1),
            jnp.concatenate([y[:n, n:], y[n:, n:]], axis=1),
        ],
        axis=0,
    )


def two_sided(tab, forward, x):
    base, adjoint = forward
    return right_product(tab, adjoint, to_rows(left_product(tab, base, x)))


BAND, BAND_ADJ, DFT, DFT_ADJ = range(4)


def field_kernel(
    places, side, own, above, below, beside, probe, tab, measured,
    gown, gside, gkeep, gsend, ext, gext, gprobe, patch, waves, far, intensity, gpatch,
):
    rec = pl.program_id(0)
    slices = own.shape[0]
    modes = probe.shape[0]
    n = LANES
    tile_cols = own.shape[3]
    half = above.shape[2]
    tile_rows = own.shape[2]
    weight = 1.0 / (8.0 * modes)

    @pl.when(rec == 0)
    def _():
        gext[...] = jnp.zeros(gext.shape, F32)
        gprobe[...] = jnp.zeros(gprobe.shape, F32)
        ext[:, :, :half, n : n + tile_cols] = above[...]
        ext[:, :, half : half + tile_rows, n : n + tile_cols] = own[...]
        ext[:, :, half + tile_rows :, n : n + tile_cols] = below[...]
        nothing = jnp.zeros(beside.shape, F32)

        @pl.when(side[0] == 0)
        def _():
            ext[:, :, :, :n] = nothing
            ext[:, :, :, n + tile_cols :] = beside[...]

        @pl.when(side[0] != 0)
        def _():
            ext[:, :, :, :n] = beside[...]
            ext[:, :, :, n + tile_cols :] = nothing

    row = places[rec, 0]
    col = places[rec, 1]
    lane_tile = pl.multiple_of(col // n * n, n)
    shift = col % n
    row_tile = pl.multiple_of(row // SUBLANES * SUBLANES, SUBLANES)
    drop = row % SUBLANES
    for s in range(slices):
        for c in range(2):
            window = ext[s, c, pl.ds(row_tile, n + SUBLANES), pl.ds(lane_tile, 2 * n)]
            window = pltpu.roll(window, (2 * n - shift) % (2 * n), 1)[:, :n]
            patch[s, c] = pltpu.roll(window, (n + SUBLANES - drop) % (n + SUBLANES), 0)[:n]

    def wave_in(s, mode):
        if s == 0:
            return probe[mode, 0], probe[mode, 1]
        block = waves[s - 1, mode * n : (mode + 1) * n, :]
        return block[:, :n], block[:, n:]

    intensity[...] = jnp.zeros(intensity.shape, F32)
    for s in range(slices):
        last = s + 1 == slices
        obj_re, obj_im = patch[s, 0], patch[s, 1]
        for pair in range(modes // 2):
            res, ims = [], []
            for mode in (2 * pair, 2 * pair + 1):
                re, im = wave_in(s, mode)
                res.append(re * obj_re - im * obj_im)
                ims.append(re * obj_im + im * obj_re)
            x = jnp.concatenate(
                [jnp.concatenate(res, axis=1), jnp.concatenate(ims, axis=1)], axis=0
            )
            z = two_sided(tab, (DFT, DFT_ADJ) if last else (BAND, BAND_ADJ), x)
            if last:
                far[pair * 2 * n : (pair + 1) * 2 * n, :] = z
                squares = z * z
                both = squares[:n] + squares[n:]
                intensity[...] += both[:, :n] + both[:, n:]
            else:
                waves[s, pair * 2 * n : (pair + 1) * 2 * n, :] = z

    factor = 2.0 * weight * (intensity[...] - measured[0])
    for pair in range(modes // 2):
        block = far[pair * 2 * n : (pair + 1) * 2 * n, :]
        scale = jnp.concatenate([jnp.concatenate([factor, factor], axis=1)] * 2, axis=0)
        far[pair * 2 * n : (pair + 1) * 2 * n, :] = two_sided(
            tab, (DFT_ADJ, DFT), to_rows(block * scale)
        )
    for s in reversed(range(slices)):
        obj_re, obj_im = patch[s, 0], patch[s, 1]
        for pair in range(modes // 2):
            res, ims = [], []
            sum_re = sum_im = None
            for mode in (2 * pair, 2 * pair + 1):
                block = far[mode * n : (mode + 1) * n, :]
                g_re, g_im = block[:, :n], block[:, n:]
                re, im = wave_in(s, mode)
                add_re = g_re * re + g_im * im
                add_im = g_im * re - g_re * im
                sum_re = add_re if sum_re is None else sum_re + add_re
                sum_im = add_im if sum_im is None else sum_im + add_im
                res.append(g_re * obj_re + g_im * obj_im)
                ims.append(g_im * obj_re - g_re * obj_im)
            if pair == 0:
                gpatch[0] = sum_re
                gpatch[1] = sum_im
            else:
                gpatch[0] += sum_re
                gpatch[1] += sum_im
            if s > 0:
                x = jnp.concatenate(
                    [jnp.concatenate(res, axis=1), jnp.concatenate(ims, axis=1)], axis=0
                )
                far[pair * 2 * n : (pair + 1) * 2 * n, :] = two_sided(tab, (BAND_ADJ, BAND), x)
            else:
                for k, mode in enumerate((2 * pair, 2 * pair + 1)):
                    for c, part in enumerate((res[k], ims[k])):
                        gprobe[:, :, c * modes + mode] += part.reshape(gprobe.shape[:2] + (SUBLANES, n))
        for c in range(2):
            tall = jnp.concatenate([gpatch[c], jnp.zeros((SUBLANES, n), F32)], axis=0)
            tall = pltpu.roll(tall, drop, 0)
            wide = jnp.concatenate([tall, jnp.zeros(tall.shape, F32)], axis=1)
            wide = pltpu.roll(wide, shift, 1)
            gext[s, c, pl.ds(row_tile, n + SUBLANES), pl.ds(lane_tile, 2 * n)] += wide

    @pl.when(rec == pl.num_programs(0) - 1)
    def _():
        gown[...] = gext[:, :, :, n : n + tile_cols]

        @pl.when(side[0] == 0)
        def _():
            gside[...] = gext[:, :, :, n + tile_cols :]
            gkeep[...] = gprobe[:, 0]
            gsend[...] = gprobe[:, 1]

        @pl.when(side[0] != 0)
        def _():
            gside[...] = gext[:, :, :, :n]
            gkeep[...] = gprobe[:, 1]
            gsend[...] = gprobe[:, 0]


def fields(places, side, own, above, below, beside, probe, tab, measured):
    slices, _, tile_rows, tile_cols = own.shape
    modes, _, n, _ = probe.shape
    rows = tile_rows + 2 * above.shape[2]
    records = measured.shape[0]

    def whole(shape):
        return pl.BlockSpec(shape, lambda r, *_: (0,) * len(shape))

    inputs = (own, above, below, beside, probe, tab)
    outs = [(slices, 2, rows, tile_cols), (slices, 2, rows, n)]
    halves = (n // SUBLANES // 2, 2 * modes, SUBLANES, n)
    outs.extend([halves, halves])
    return pl.pallas_call(
        field_kernel,
        out_shape=[jax.ShapeDtypeStruct(s, F32) for s in outs],
        grid_spec=pltpu.PrefetchScalarGridSpec(
            num_scalar_prefetch=2,
            grid=(records,),
            in_specs=[whole(x.shape) for x in inputs]
            + [pl.BlockSpec((1, n, n), lambda r, *_: (r, 0, 0))],
            out_specs=[whole(s) for s in outs],
            scratch_shapes=[
                pltpu.VMEM((slices, 2, rows, tile_cols + 2 * n), F32),
                pltpu.VMEM((slices, 2, rows, tile_cols + 2 * n), F32),
                pltpu.VMEM((n // SUBLANES // 2, 2, 2 * modes, SUBLANES, n), F32),
                pltpu.VMEM((slices, 2, n, n), F32),
                pltpu.VMEM((slices - 1, modes * n, 2 * n), F32),
                pltpu.VMEM((modes * n, 2 * n), F32),
                pltpu.VMEM((n, n), F32),
                pltpu.VMEM((2, n, n), F32),
            ],
        ),
        compiler_params=pltpu.CompilerParams(vmem_limit_bytes=56 << 20),
        name="fields",
    )(places, side, *inputs, measured)


def gram_kernel(*refs):
    probe, *parts, out, own = refs
    grad = parts[0][...]
    for part in parts[1:]:
        grad = grad + part[...]
    own[...] = grad
    total = None
    for i in range(probe.shape[1]):
        rows = jnp.concatenate([probe[:, i, :], own[:, i, :]], axis=0)
        one = lax.dot_general(
            rows, rows, (((1,), (1,)), ((), ())), precision=lax.Precision.HIGHEST,
            preferred_element_type=F32,
        )
        total = one if total is None else total + one
    out[...] = total


def gram(probe, parts):
    rows = 2 * probe.shape[0]
    return pl.pallas_call(
        gram_kernel,
        out_shape=[
            jax.ShapeDtypeStruct((rows, rows), F32),
            jax.ShapeDtypeStruct(probe.shape, F32),
        ],
        name="gram",
    )(probe, *parts)


def ortho_kernel(*refs, modes, scale):
    *grams, probe, grad, out = refs
    m = modes
    s = grams[0][...]
    for other in grams[1:]:
        s = s + other[...]

    def part(a, b):
        return s[a * m : (a + 1) * m, b * m : (b + 1) * m]

    def complex_part(a, b):
        re = part(2 * a, 2 * b) + part(2 * a + 1, 2 * b + 1)
        im = part(2 * a, 2 * b + 1) - part(2 * a + 1, 2 * b)
        return re, im

    pp, pg, gp, gg = (complex_part(a, b) for a, b in ((0, 0), (0, 1), (1, 0), (1, 1)))
    eye = (
        lax.broadcasted_iota(jnp.int32, (m, m), 0) == lax.broadcasted_iota(jnp.int32, (m, m), 1)
    ).astype(F32)

    def trace(x):
        return jnp.sum(jnp.sum(x * eye, axis=1, keepdims=True), axis=0, keepdims=True)

    factor = 0.5 * jnp.sqrt(trace(pp[0]) / (trace(gg[0]) + 1e-06))
    new_re = pp[0] - factor * (pg[0] + gp[0]) + factor * factor * gg[0]
    new_im = pp[1] - factor * (pg[1] + gp[1]) + factor * factor * gg[1]
    a_re = jnp.concatenate([new_re, eye], axis=1)
    a_im = jnp.concatenate([new_im, jnp.zeros((m, m), F32)], axis=1)
    row_idx = lax.broadcasted_iota(jnp.int32, (m, 1), 0)
    for j in range(m):
        inv = 1.0 / jnp.sqrt(a_re[j : j + 1, j : j + 1])
        r_re = a_re[j : j + 1, :] * inv
        r_im = a_im[j : j + 1, :] * inv
        c_re = jnp.where(row_idx > j, a_re[:, j : j + 1] * inv, 0.0)
        c_im = jnp.where(row_idx > j, a_im[:, j : j + 1] * inv, 0.0)
        at = row_idx == j
        a_re, a_im = (
            jnp.where(at, r_re, a_re - (c_re * r_re - c_im * r_im)),
            jnp.where(at, r_im, a_im - (c_re * r_im + c_im * r_re)),
        )
    inv_re = a_re[:, m:] * scale
    inv_im = a_im[:, m:] * scale
    mix = jnp.concatenate(
        [
            jnp.concatenate([inv_re, inv_im], axis=1),
            jnp.concatenate([-inv_im, inv_re], axis=1),
        ],
        axis=0,
    )
    n = probe.shape[2]
    for i in range(probe.shape[1]):
        moved = probe[:, i, :] - factor * grad[:, i, :]
        new = lax.dot_general(
            mix, moved, (((1,), (0,)), ((), ())), precision=lax.Precision.HIGHEST,
            preferred_element_type=F32,
        )
        out[:, 0, i * n : (i + 1) * n] = new[:m]
        out[:, 1, i * n : (i + 1) * n] = new[m:]


def ortho(grams, probe, grad, modes, scale):
    def body(*refs):
        ortho_kernel(*refs, modes=modes, scale=scale)

    pixels = probe.shape[1] * probe.shape[2]
    return pl.pallas_call(
        body, out_shape=jax.ShapeDtypeStruct((modes, 2, pixels), F32), name="ortho"
    )(*grams, probe, grad)


def take(array, which, dim):
    return lax.dynamic_index_in_dim(array, which, dim, keepdims=False)


def own_block(probe):
    modes, _, width, _ = probe.shape
    devices = lax.axis_size("row") * lax.axis_size("col")
    share = width // devices
    index = lax.axis_index(("row", "col"))
    block = lax.dynamic_slice_in_dim(probe, index * share, share, 2)
    return block.transpose(1, 0, 2, 3).reshape(2 * modes, share, width)


def updates(own_probe, keep, send, bottom, top, middle):
    rows, share, width = own_probe.shape
    modes = rows // 2
    row_devices = lax.axis_size("row")
    col_devices = lax.axis_size("col")
    row_idx, col_idx = lax.axis_index("row"), lax.axis_index("col")
    row_bits = [1 << b for b in range(row_devices.bit_length() - 1)]

    if share == SUBLANES and row_devices <= 8:
        received = swapped(send, "col", 1)
        parts = []
        for k in range(row_devices):
            block = take(keep, row_idx ^ k, 0) + take(received, row_idx ^ k, 0)
            parts.append(swapped(block, "row", k) if k else block)
    else:
        even, odd = jnp.where(col_idx == 0, keep, send), jnp.where(col_idx == 0, send, keep)
        grad = jnp.stack([even, odd], axis=1).transpose(0, 1, 3, 2, 4)
        grad = grad.reshape(row_devices, col_devices, share, 2 * modes, width)
        grad = grad.transpose(1, 0, 3, 2, 4)
        grad = take(grad, col_idx, 0) + swapped(take(grad, 1 - col_idx, 0), "col", 1)
        for bit in reversed(row_bits):
            grad = grad.reshape((2, bit) + grad.shape[-3:])
            mine = (row_idx // bit) % 2
            grad = take(grad, mine, 0) + swapped(take(grad, 1 - mine, 0), "row", bit)
        parts = [grad.reshape(2 * modes, share, width)]

    late = parts[4:6]
    early, bottom, top = lax.optimization_barrier((parts[:4] + parts[6:], bottom, top))
    parts = early + late
    from_above = shifted(bottom, "row", 1)
    from_below = shifted(top, "row", -1)
    total, own_grad = gram(own_probe, parts)
    total = total + swapped(total, "col", 1)
    high_bits = row_bits[1:]
    if len(high_bits) % 2:
        total = total + swapped(total, "row", high_bits.pop())
    while high_bits:
        a, b, *high_bits = high_bits
        near, far, both = (swapped(total, "row", k) for k in (a, b, a ^ b))
        total = (total + near) + (far + both)
    grams = [total, swapped(total, "row", row_bits[0])]
    new_probe = ortho(grams, own_probe, own_grad, modes, float(width))
    object_grad = middle() + jnp.concatenate([from_above, from_below], axis=2)
    return new_probe, object_grad


def per_device(object_slices, probe, taps, measured, positions):
    width = probe.shape[-1]
    half = width // 2
    slices, _, tile_rows, tile_cols = object_slices.shape
    row_idx = lax.axis_index("row")
    col_idx = lax.axis_index("col")

    above = shifted(object_slices[:, :, tile_rows - half :], "row", 1)
    below = shifted(object_slices[:, :, :half], "row", -1)
    tab = block_tables(taps, width)
    own_probe = own_block(probe)
    above, below, tab, own_probe = lax.optimization_barrier((above, below, tab, own_probe))
    near = (1 - col_idx) * (tile_cols - LANES)
    strip = jnp.concatenate([
        lax.dynamic_slice_in_dim(x, near, LANES, 3) for x in (above, object_slices, below)
    ], axis=2)
    beside = swapped(strip, "col", 1)

    anchor = jnp.stack([row_idx * tile_rows - half, col_idx * tile_cols - LANES])
    places = (positions - anchor[None, :]).astype(jnp.int32)
    side = col_idx.astype(jnp.int32).reshape(1)
    gown, gside, gkeep, gsend = fields(
        places, side, object_slices, above, below, beside, probe, tab, measured
    )

    got = swapped(gside, "col", 1)

    def folded(first, last):
        part = got[:, :, first:last]
        low = jnp.where(col_idx == 0, 0.0, part)
        high = jnp.where(col_idx == 0, part, 0.0)
        inner = jnp.zeros(part.shape[:3] + (tile_cols - 2 * LANES,), F32)
        return gown[:, :, first:last] + jnp.concatenate([low, inner, high], axis=3)

    bottom, top = folded(half + tile_rows, tile_rows + 2 * half), folded(0, half)
    new_probe, object_grad = updates(
        own_probe, gkeep, gsend, bottom, top, lambda: folded(half, half + tile_rows)
    )
    return (object_grad, new_probe)


def solution(mesh):
    placed = (
        P(None, None, ("groups", "row"), "col"),
        P("groups", None, None, None),
        P(),
        P(("groups", "row", "col"), None, None),
        P(("groups", "row", "col"), None),
    )
    return jax.shard_map(
        per_device,
        mesh=mesh,
        in_specs=placed,
        out_specs=(P(None, None, ("groups", "row"), "col"), P("groups", None, ("row", "col"))),
        check_vma=False,
    )
```

```python
import math

import jax
import jax.numpy as jnp
import numpy as np
from jax import lax
from jax.experimental import pallas as pl
from jax.experimental.pallas import tpu as pltpu
from jax.sharding import PartitionSpec as P

F32 = jnp.float32
BF16 = jnp.bfloat16
LANES = 128
SUBLANES = 8


def shifted(value, axis, step):
    count = lax.axis_size(axis)
    pairs = [(i, i + step) for i in range(count) if 0 <= i + step < count]
    return lax.ppermute(value, axis, pairs)


def swapped(value, axis, bit):
    count = lax.axis_size(axis)
    return lax.ppermute(value, axis, [(i, i ^ bit) for i in range(count)])


def hi_lo(value):
    high = lax.reduce_precision(value, 8, 7)
    return high.astype(BF16), (value - high).astype(BF16)


def block_tables(taps, width):
    reach = taps.shape[1] // 2
    padded = jnp.pad(taps, ((0, 0), (width, width)))
    idx = lax.iota(jnp.int32, width)
    offset = idx[None, :] - idx[:, None] + reach
    tap_idx = lax.iota(jnp.int32, taps.shape[1])
    hot = (offset[None, :, :] == tap_idx[:, None, None]).astype(F32)
    band_re = jnp.sum(hot * taps[0][:, None, None], axis=0)
    band_im = jnp.sum(hot * taps[1][:, None, None], axis=0)
    phase = np.arange(width)[:, None] * np.arange(width)[None, :] % width
    angle = 2.0 * math.pi / width * phase
    norm = 1.0 / math.sqrt(width)
    dft_re = jnp.asarray(np.cos(angle) * norm, F32)
    dft_im = jnp.asarray(-np.sin(angle) * norm, F32)

    def block(re, im):
        return jnp.concatenate(
            [jnp.concatenate([re, -im], axis=1), jnp.concatenate([im, re], axis=1)], axis=0
        )

    band, dft = block(band_re, band_im), block(dft_re, dft_im)
    parts = []
    for matrix in (band, band.T, dft, dft.T):
        parts.extend(hi_lo(matrix))
    return jnp.stack(parts)


def split(value):
    high = value.astype(BF16)
    return high, (value - high.astype(F32)).astype(BF16)


def mxu(a, b):
    return lax.dot_general(a, b, (((1,), (0,)), ((), ())), preferred_element_type=F32)


def left_product(tab, which, x):
    high, low = split(x)
    w_high, w_low = tab[2 * which], tab[2 * which + 1]
    return mxu(w_high, high) + (mxu(w_high, low) + mxu(w_low, high))


def right_product(tab, which, x):
    high, low = split(x)
    w_high, w_low = tab[2 * which], tab[2 * which + 1]
    return mxu(high, w_high) + (mxu(low, w_high) + mxu(high, w_low))


def to_rows(y):
    n = LANES
    return jnp.concatenate(
        [
            jnp.concatenate([y[:n, :n], y[n:, :n]], axis=1),
            jnp.concatenate([y[:n, n:], y[n:, n:]], axis=1),
        ],
        axis=0,
    )


def two_sided(tab, forward, x):
    base, adjoint = forward
    return right_product(tab, adjoint, to_rows(left_product(tab, base, x)))


BAND, BAND_ADJ, DFT, DFT_ADJ = range(4)


def field_kernel(
    places, side, own, above, below, beside, probe, tab, measured,
    gown, gside, gkeep, gsend, ext, gext, gprobe, patch, waves, far, intensity, gpatch,
):
    rec = pl.program_id(0)
    slices = own.shape[0]
    modes = probe.shape[0]
    n = LANES
    tile_cols = own.shape[3]
    half = above.shape[2]
    tile_rows = own.shape[2]
    weight = 1.0 / (8.0 * modes)

    @pl.when(rec == 0)
    def _():
        gext[...] = jnp.zeros(gext.shape, F32)
        gprobe[...] = jnp.zeros(gprobe.shape, F32)
        ext[:, :, :half, n : n + tile_cols] = above[...]
        ext[:, :, half : half + tile_rows, n : n + tile_cols] = own[...]
        ext[:, :, half + tile_rows :, n : n + tile_cols] = below[...]
        nothing = jnp.zeros(beside.shape, F32)

        @pl.when(side[0] == 0)
        def _():
            ext[:, :, :, :n] = nothing
            ext[:, :, :, n + tile_cols :] = beside[...]

        @pl.when(side[0] != 0)
        def _():
            ext[:, :, :, :n] = beside[...]
            ext[:, :, :, n + tile_cols :] = nothing

    row = places[rec, 0]
    col = places[rec, 1]
    lane_tile = pl.multiple_of(col // n * n, n)
    shift = col % n
    row_tile = pl.multiple_of(row // SUBLANES * SUBLANES, SUBLANES)
    drop = row % SUBLANES
    for s in range(slices):
        for c in range(2):
            window = ext[s, c, pl.ds(row_tile, n + SUBLANES), pl.ds(lane_tile, 2 * n)]
            window = pltpu.roll(window, (2 * n - shift) % (2 * n), 1)[:, :n]
            patch[s, c] = pltpu.roll(window, (n + SUBLANES - drop) % (n + SUBLANES), 0)[:n]

    def wave_in(s, mode):
        if s == 0:
            return probe[mode, 0], probe[mode, 1]
        block = waves[s - 1, mode * n : (mode + 1) * n, :]
        return block[:, :n], block[:, n:]

    intensity[...] = jnp.zeros(intensity.shape, F32)
    for s in range(slices):
        last = s + 1 == slices
        obj_re, obj_im = patch[s, 0], patch[s, 1]
        for pair in range(modes // 2):
            res, ims = [], []
            for mode in (2 * pair, 2 * pair + 1):
                re, im = wave_in(s, mode)
                res.append(re * obj_re - im * obj_im)
                ims.append(re * obj_im + im * obj_re)
            x = jnp.concatenate(
                [jnp.concatenate(res, axis=1), jnp.concatenate(ims, axis=1)], axis=0
            )
            z = two_sided(tab, (DFT, DFT_ADJ) if last else (BAND, BAND_ADJ), x)
            if last:
                far[pair * 2 * n : (pair + 1) * 2 * n, :] = z
                squares = z * z
                both = squares[:n] + squares[n:]
                intensity[...] += both[:, :n] + both[:, n:]
            else:
                waves[s, pair * 2 * n : (pair + 1) * 2 * n, :] = z

    factor = 2.0 * weight * (intensity[...] - measured[0])
    for pair in range(modes // 2):
        block = far[pair * 2 * n : (pair + 1) * 2 * n, :]
        scale = jnp.concatenate([jnp.concatenate([factor, factor], axis=1)] * 2, axis=0)
        far[pair * 2 * n : (pair + 1) * 2 * n, :] = two_sided(
            tab, (DFT_ADJ, DFT), to_rows(block * scale)
        )
    for s in reversed(range(slices)):
        obj_re, obj_im = patch[s, 0], patch[s, 1]
        for pair in range(modes // 2):
            res, ims = [], []
            sum_re = sum_im = None
            for mode in (2 * pair, 2 * pair + 1):
                block = far[mode * n : (mode + 1) * n, :]
                g_re, g_im = block[:, :n], block[:, n:]
                re, im = wave_in(s, mode)
                add_re = g_re * re + g_im * im
                add_im = g_im * re - g_re * im
                sum_re = add_re if sum_re is None else sum_re + add_re
                sum_im = add_im if sum_im is None else sum_im + add_im
                res.append(g_re * obj_re + g_im * obj_im)
                ims.append(g_im * obj_re - g_re * obj_im)
            if pair == 0:
                gpatch[0] = sum_re
                gpatch[1] = sum_im
            else:
                gpatch[0] += sum_re
                gpatch[1] += sum_im
            if s > 0:
                x = jnp.concatenate(
                    [jnp.concatenate(res, axis=1), jnp.concatenate(ims, axis=1)], axis=0
                )
                far[pair * 2 * n : (pair + 1) * 2 * n, :] = two_sided(tab, (BAND_ADJ, BAND), x)
            else:
                for k, mode in enumerate((2 * pair, 2 * pair + 1)):
                    for c, part in enumerate((res[k], ims[k])):
                        gprobe[:, :, c * modes + mode] += part.reshape(gprobe.shape[:2] + (SUBLANES, n))
        for c in range(2):
            tall = jnp.concatenate([gpatch[c], jnp.zeros((SUBLANES, n), F32)], axis=0)
            tall = pltpu.roll(tall, drop, 0)
            wide = jnp.concatenate([tall, jnp.zeros(tall.shape, F32)], axis=1)
            wide = pltpu.roll(wide, shift, 1)
            gext[s, c, pl.ds(row_tile, n + SUBLANES), pl.ds(lane_tile, 2 * n)] += wide

    @pl.when(rec == pl.num_programs(0) - 1)
    def _():
        gown[...] = gext[:, :, :, n : n + tile_cols]

        @pl.when(side[0] == 0)
        def _():
            gside[...] = gext[:, :, :, n + tile_cols :]
            gkeep[...] = gprobe[:, 0]
            gsend[...] = gprobe[:, 1]

        @pl.when(side[0] != 0)
        def _():
            gside[...] = gext[:, :, :, :n]
            gkeep[...] = gprobe[:, 1]
            gsend[...] = gprobe[:, 0]


def fields(places, side, own, above, below, beside, probe, tab, measured):
    slices, _, tile_rows, tile_cols = own.shape
    modes, _, n, _ = probe.shape
    rows = tile_rows + 2 * above.shape[2]
    records = measured.shape[0]

    def whole(shape):
        return pl.BlockSpec(shape, lambda r, *_: (0,) * len(shape))

    inputs = (own, above, below, beside, probe, tab)
    outs = [(slices, 2, rows, tile_cols), (slices, 2, rows, n)]
    halves = (n // SUBLANES // 2, 2 * modes, SUBLANES, n)
    outs.extend([halves, halves])
    return pl.pallas_call(
        field_kernel,
        out_shape=[jax.ShapeDtypeStruct(s, F32) for s in outs],
        grid_spec=pltpu.PrefetchScalarGridSpec(
            num_scalar_prefetch=2,
            grid=(records,),
            in_specs=[whole(x.shape) for x in inputs]
            + [pl.BlockSpec((1, n, n), lambda r, *_: (r, 0, 0))],
            out_specs=[whole(s) for s in outs],
            scratch_shapes=[
                pltpu.VMEM((slices, 2, rows, tile_cols + 2 * n), F32),
                pltpu.VMEM((slices, 2, rows, tile_cols + 2 * n), F32),
                pltpu.VMEM((n // SUBLANES // 2, 2, 2 * modes, SUBLANES, n), F32),
                pltpu.VMEM((slices, 2, n, n), F32),
                pltpu.VMEM((slices - 1, modes * n, 2 * n), F32),
                pltpu.VMEM((modes * n, 2 * n), F32),
                pltpu.VMEM((n, n), F32),
                pltpu.VMEM((2, n, n), F32),
            ],
        ),
        compiler_params=pltpu.CompilerParams(vmem_limit_bytes=56 << 20),
        name="fields",
    )(places, side, *inputs, measured)


def gram_kernel(*refs):
    probe, *parts, out, own = refs
    grad = parts[0][...]
    for part in parts[1:]:
        grad = grad + part[...]
    own[...] = grad
    total = None
    for i in range(probe.shape[1]):
        rows = jnp.concatenate([probe[:, i, :], own[:, i, :]], axis=0)
        one = lax.dot_general(
            rows, rows, (((1,), (1,)), ((), ())), precision=lax.Precision.HIGHEST,
            preferred_element_type=F32,
        )
        total = one if total is None else total + one
    out[...] = total


def gram(probe, parts):
    rows = 2 * probe.shape[0]
    return pl.pallas_call(
        gram_kernel,
        out_shape=[
            jax.ShapeDtypeStruct((rows, rows), F32),
            jax.ShapeDtypeStruct(probe.shape, F32),
        ],
        name="gram",
    )(probe, *parts)


def ortho_kernel(*refs, modes, scale):
    *grams, probe, grad, out = refs
    m = modes
    s = grams[0][...]
    for other in grams[1:]:
        s = s + other[...]

    def part(a, b):
        return s[a * m : (a + 1) * m, b * m : (b + 1) * m]

    def complex_part(a, b):
        re = part(2 * a, 2 * b) + part(2 * a + 1, 2 * b + 1)
        im = part(2 * a, 2 * b + 1) - part(2 * a + 1, 2 * b)
        return re, im

    pp, pg, gp, gg = (complex_part(a, b) for a, b in ((0, 0), (0, 1), (1, 0), (1, 1)))
    eye = (
        lax.broadcasted_iota(jnp.int32, (m, m), 0) == lax.broadcasted_iota(jnp.int32, (m, m), 1)
    ).astype(F32)

    def trace(x):
        return jnp.sum(jnp.sum(x * eye, axis=1, keepdims=True), axis=0, keepdims=True)

    factor = 0.5 * jnp.sqrt(trace(pp[0]) / (trace(gg[0]) + 1e-06))
    new_re = pp[0] - factor * (pg[0] + gp[0]) + factor * factor * gg[0]
    new_im = pp[1] - factor * (pg[1] + gp[1]) + factor * factor * gg[1]
    a_re = jnp.concatenate([new_re, eye], axis=1)
    a_im = jnp.concatenate([new_im, jnp.zeros((m, m), F32)], axis=1)
    row_idx = lax.broadcasted_iota(jnp.int32, (m, 1), 0)
    for j in range(m):
        inv = 1.0 / jnp.sqrt(a_re[j : j + 1, j : j + 1])
        r_re = a_re[j : j + 1, :] * inv
        r_im = a_im[j : j + 1, :] * inv
        c_re = jnp.where(row_idx > j, a_re[:, j : j + 1] * inv, 0.0)
        c_im = jnp.where(row_idx > j, a_im[:, j : j + 1] * inv, 0.0)
        at = row_idx == j
        a_re, a_im = (
            jnp.where(at, r_re, a_re - (c_re * r_re - c_im * r_im)),
            jnp.where(at, r_im, a_im - (c_re * r_im + c_im * r_re)),
        )
    inv_re = a_re[:, m:] * scale
    inv_im = a_im[:, m:] * scale
    mix = jnp.concatenate(
        [
            jnp.concatenate([inv_re, inv_im], axis=1),
            jnp.concatenate([-inv_im, inv_re], axis=1),
        ],
        axis=0,
    )
    n = probe.shape[2]
    for i in range(probe.shape[1]):
        moved = probe[:, i, :] - factor * grad[:, i, :]
        new = lax.dot_general(
            mix, moved, (((1,), (0,)), ((), ())), precision=lax.Precision.HIGHEST,
            preferred_element_type=F32,
        )
        out[:, 0, i * n : (i + 1) * n] = new[:m]
        out[:, 1, i * n : (i + 1) * n] = new[m:]


def ortho(grams, probe, grad, modes, scale):
    def body(*refs):
        ortho_kernel(*refs, modes=modes, scale=scale)

    pixels = probe.shape[1] * probe.shape[2]
    return pl.pallas_call(
        body, out_shape=jax.ShapeDtypeStruct((modes, 2, pixels), F32), name="ortho"
    )(*grams, probe, grad)


def take(array, which, dim):
    return lax.dynamic_index_in_dim(array, which, dim, keepdims=False)


def own_block(probe):
    modes, _, width, _ = probe.shape
    devices = lax.axis_size("row") * lax.axis_size("col")
    share = width // devices
    index = lax.axis_index(("row", "col"))
    block = lax.dynamic_slice_in_dim(probe, index * share, share, 2)
    return block.transpose(1, 0, 2, 3).reshape(2 * modes, share, width)


def updates(own_probe, keep, send, bottom, top, middle):
    rows, share, width = own_probe.shape
    modes = rows // 2
    row_devices = lax.axis_size("row")
    col_devices = lax.axis_size("col")
    row_idx, col_idx = lax.axis_index("row"), lax.axis_index("col")
    row_bits = [1 << b for b in range(row_devices.bit_length() - 1)]

    if share == SUBLANES and row_devices <= 8:
        received = swapped(send, "col", 1)
        parts = []
        for k in range(row_devices):
            block = take(keep, row_idx ^ k, 0) + take(received, row_idx ^ k, 0)
            parts.append(swapped(block, "row", k) if k else block)
    else:
        even, odd = jnp.where(col_idx == 0, keep, send), jnp.where(col_idx == 0, send, keep)
        grad = jnp.stack([even, odd], axis=1).transpose(0, 1, 3, 2, 4)
        grad = grad.reshape(row_devices, col_devices, share, 2 * modes, width)
        grad = grad.transpose(1, 0, 3, 2, 4)
        grad = take(grad, col_idx, 0) + swapped(take(grad, 1 - col_idx, 0), "col", 1)
        for bit in reversed(row_bits):
            grad = grad.reshape((2, bit) + grad.shape[-3:])
            mine = (row_idx // bit) % 2
            grad = take(grad, mine, 0) + swapped(take(grad, 1 - mine, 0), "row", bit)
        parts = [grad.reshape(2 * modes, share, width)]

    late = parts[3:6]
    early, bottom, top = lax.optimization_barrier((parts[:3] + parts[6:], bottom, top))
    parts = early + late
    from_above = shifted(bottom, "row", 1)
    from_below = shifted(top, "row", -1)
    total, own_grad = gram(own_probe, parts)
    total = total + swapped(total, "col", 1)
    high_bits = row_bits[1:]
    if len(high_bits) % 2:
        total = total + swapped(total, "row", high_bits.pop())
    while high_bits:
        a, b, *high_bits = high_bits
        near, far, both = (swapped(total, "row", k) for k in (a, b, a ^ b))
        total = (total + near) + (far + both)
    grams = [total, swapped(total, "row", row_bits[0])]
    new_probe = ortho(grams, own_probe, own_grad, modes, float(width))
    object_grad = middle() + jnp.concatenate([from_above, from_below], axis=2)
    return new_probe, object_grad


def per_device(object_slices, probe, taps, measured, positions):
    width = probe.shape[-1]
    half = width // 2
    slices, _, tile_rows, tile_cols = object_slices.shape
    row_idx = lax.axis_index("row")
    col_idx = lax.axis_index("col")

    above = shifted(object_slices[:, :, tile_rows - half :], "row", 1)
    below = shifted(object_slices[:, :, :half], "row", -1)
    tab = block_tables(taps, width)
    own_probe = own_block(probe)
    above, below, tab, own_probe = lax.optimization_barrier((above, below, tab, own_probe))
    near = (1 - col_idx) * (tile_cols - LANES)
    strip = jnp.concatenate([
        lax.dynamic_slice_in_dim(x, near, LANES, 3) for x in (above, object_slices, below)
    ], axis=2)
    beside = swapped(strip, "col", 1)

    anchor = jnp.stack([row_idx * tile_rows - half, col_idx * tile_cols - LANES])
    places = (positions - anchor[None, :]).astype(jnp.int32)
    side = col_idx.astype(jnp.int32).reshape(1)
    gown, gside, gkeep, gsend = fields(
        places, side, object_slices, above, below, beside, probe, tab, measured
    )

    got = swapped(gside, "col", 1)

    def folded(first, last):
        part = got[:, :, first:last]
        low = jnp.where(col_idx == 0, 0.0, part)
        high = jnp.where(col_idx == 0, part, 0.0)
        inner = jnp.zeros(part.shape[:3] + (tile_cols - 2 * LANES,), F32)
        return gown[:, :, first:last] + jnp.concatenate([low, inner, high], axis=3)

    bottom, top = folded(half + tile_rows, tile_rows + 2 * half), folded(0, half)
    new_probe, object_grad = updates(
        own_probe, gkeep, gsend, bottom, top, lambda: folded(half, half + tile_rows)
    )
    return (object_grad, new_probe)


def solution(mesh):
    placed = (
        P(None, None, ("groups", "row"), "col"),
        P("groups", None, None, None),
        P(),
        P(("groups", "row", "col"), None, None),
        P(("groups", "row", "col"), None),
    )
    return jax.shard_map(
        per_device,
        mesh=mesh,
        in_specs=placed,
        out_specs=(P(None, None, ("groups", "row"), "col"), P("groups", None, ("row", "col"))),
        check_vma=False,
    )
```
